32 devices in a mesh: grp: 2 (over x), seq: 16 (over z, y, core).
Axes of the slice: x: 2, y: 2, z: 4, core: 2. Of those that a mesh axis runs over, the one named last changes fastest.
Arguments:
- projected: bfloat16 [3, 4096, 4096], P(None, ('grp', 'seq')), parts along dimension 1, may hold values from -6 to 6
- short_taps: float32 [3, 3, 4096], replicated, may hold values from -3 to 3
- skip_gain: float32 [4096], replicated, may hold values from -3 to 3
- residues: float32 [2, 2, 4096], replicated, may hold values from -0.125 to 0.125
- pole_angles: float32 [2, 4096], replicated, may hold values from -3.140625 to 3.140625
- decay_rates: float32 [2, 4096], replicated, may hold values from 3.0517578e-05 to 0.03125
Outputs:
- gated: bfloat16 [4096, 4096], P(('grp', 'seq')), parts along dimension 0
The draws below stay inside these ranges and needn't reach their ends.
There are 2 independent parts, one for each index of `grp`. The reference program is written for one: setup_inputs(seed, part) draws one part's arguments, and reference() takes and returns one part's arrays. A program takes and returns all parts, laid end to end along the dimension named above; an argument that names none is the same for every part. Nothing has to cross between parts.
All inputs are finite; a program needn't handle non-finite values.
Results may differ from the reference program's by a relative error of at most 0.008.
Values may be sent and summed in bfloat16 or wider, within the bound.
No kernel may reach another device: no remote copies, remote signals or barrier semaphores. Data moves between devices by JAX's collectives and lax.ppermute only.
A program may use at most 128 MiB of HBM per device.

```python
import math
import jax
import jax.numpy as jnp
from jax import lax

D = 4096
STATE = 2
SHORT = 3
LENGTH = 2048


def draw_decay_rates(key, part):
    pick_key, slow_key, fast_key = jax.random.split(key, 3)
    chooser = jax.random.uniform(pick_key, (STATE, D), jnp.float32)
    slow_rate = jnp.exp(jax.random.uniform(slow_key, (STATE, D), jnp.float32, math.log(0.3 / LENGTH), math.log(2.0 / LENGTH)))
    fast_rate = jnp.exp(jax.random.uniform(fast_key, (STATE, D), jnp.float32, math.log(1.0 / 400.0), math.log(0.99 / 32.0)))
    share = 0.5
    return jnp.where(chooser < share, slow_rate, fast_rate)


def level_of(own_key, extent, cuts, smallest, high):
    gain = 1.0
    for axis_at, shards_of in cuts:
        heights = jax.random.uniform(jax.random.fold_in(jax.random.fold_in(own_key, 6), axis_at), (shards_of,), jnp.float32, smallest / len(cuts), high / len(cuts))
        gain = gain * jnp.repeat(jnp.exp(heights), extent[axis_at] // shards_of).reshape((-1,) + (1,) * (len(extent) - 1 - axis_at))
    return gain


def normal_values(key, extent, deviation, reach, pieces=(), held_as=jnp.bfloat16):
    array = deviation * jax.random.normal(key, extent, jnp.float32)
    if pieces:
        array = array * level_of(key, extent, pieces, -0.22, 0.18)
    return jnp.clip(array, -reach, reach).astype(held_as)


def setup_inputs(seed: int = 0, part: int = 0) -> dict:
    key_of = jax.random.split(jax.random.key(seed), 7)
    own_keys = jax.random.split(jax.random.fold_in(key_of[6], part), 7)
    projected = normal_values(own_keys[0], (3, LENGTH, D), 1.0, 6.0, ((1, 16),))
    short_taps = normal_values(key_of[1], (SHORT, 3, D), 0.6, 3.0, (), jnp.float32)
    skip_gain = normal_values(key_of[2], (D,), 1.0, 3.0, (), jnp.float32)
    residues = normal_values(key_of[3], (2, STATE, D), LENGTH ** -0.5, 0.125, (), jnp.float32)
    pole_angles = jnp.clip(jax.random.uniform(key_of[4], (STATE, D), jnp.float32, -3.140625, 3.140625), -3.140625, 3.140625)
    decay_rates = draw_decay_rates(jax.random.fold_in(key_of[6], 71), part)
    return {"projected": projected, "short_taps": short_taps, "skip_gain": skip_gain, "residues": residues, "pole_angles": pole_angles, "decay_rates": decay_rates}


def filter_values(positions, residues, pole_angles, decay_rates):
    total = jnp.zeros((positions.shape[0], residues.shape[2]), jnp.float32)
    for state in range(residues.shape[1]):
        phase = pole_angles[state][None, :] * positions[:, None]
        damping = jnp.exp(-decay_rates[state][None, :] * positions[:, None])
        total = total + damping * (residues[0, state][None, :] * jnp.cos(phase) - residues[1, state][None, :] * jnp.sin(phase))
    return total.astype(jnp.bfloat16)


def reference(projected, short_taps, skip_gain, residues, pole_angles, decay_rates):
    positions = jnp.arange(LENGTH).astype(jnp.float32)
    kernel = filter_values(positions, residues, pole_angles, decay_rates)
    padded = jnp.pad(projected.astype(jnp.float32), ((0, 0), (2, 0), (0, 0)))
    conv = (short_taps[0][:, None, :] * padded[:, 0:LENGTH]
            + short_taps[1][:, None, :] * padded[:, 1:LENGTH + 1]
            + short_taps[2][:, None, :] * padded[:, 2:LENGTH + 2])
    products = (conv[1] * conv[2]).astype(jnp.bfloat16)
    doubled = 2 * LENGTH
    spectrum = jnp.fft.rfft(products.astype(jnp.float32), n=doubled, axis=0) * jnp.fft.rfft(kernel.astype(jnp.float32), n=doubled, axis=0)
    long_sum = jnp.fft.irfft(spectrum, n=doubled, axis=0)[:LENGTH]
    long_rounded = lax.optimization_barrier(long_sum.astype(jnp.bfloat16))
    gated = conv[0] * (long_rounded.astype(jnp.float32) + skip_gain[None, :] * products.astype(jnp.float32))
    return gated.astype(jnp.bfloat16)
```

```python
import functools

import jax
import jax.numpy as jnp
from jax import lax
from jax.experimental import pallas as pl
from jax.experimental.pallas import tpu as pltpu
from jax.sharding import PartitionSpec as P

SEGMENTS = 8
WIDTH = 256
BLOCK = 1024
WIRE = jnp.float32
f32 = jnp.float32
bf16 = jnp.bfloat16


def order_matrix(row_count, inverse):
    length = row_count // SEGMENTS
    ordered = lax.broadcasted_iota(jnp.int32, (row_count, row_count), 1 if inverse else 0)
    natural = lax.broadcasted_iota(jnp.int32, (row_count, row_count), 0 if inverse else 1)
    wanted = length * (ordered % SEGMENTS) + ordered // SEGMENTS
    return (wanted == natural).astype(f32).astype(bf16)


def row(ref, index, cols):
    return jnp.broadcast_to(ref[index : index + 1, cols], (SEGMENTS, WIDTH))


def steps_of(ref, cols):
    return [ref[SEGMENTS * j : SEGMENTS * (j + 1), cols] for j in range(ref.shape[0] // SEGMENTS)]


def delayed(value, first):
    sublane = lax.broadcasted_iota(jnp.int32, value.shape, 0)
    return jnp.where(sublane == 0, first, pltpu.roll(value, 1, 0))


def short_filter(steps, rim_ref, rim_row, taps_ref, which, cols):
    taps = [row(taps_ref, 3 * tap + which, cols) for tap in range(3)]
    before = [
        delayed(steps[-2], row(rim_ref, rim_row, cols)),
        delayed(steps[-1], row(rim_ref, rim_row + 1, cols)),
    ]
    padded = before + steps
    return [
        taps[0] * padded[j] + taps[1] * padded[j + 1] + taps[2] * padded[j + 2]
        for j in range(len(steps))
    ]


def times(a, b):
    return (a[0] * b[0] - a[1] * b[1], a[0] * b[1] + a[1] * b[0])


def power(pr_ref, pi_ref, exponent, pole, cols):
    return (row(pr_ref, 2 * exponent + pole, cols), row(pi_ref, 2 * exponent + pole, cols))


def states_kernel(order_ref, k_ref, v_ref, rim_ref, taps_ref, pr_ref, pi_ref,
                  prod_ref, scan_ref, total_ref, ks_ref, vs_ref):
    ks_ref[...] = jnp.dot(order_ref[...], k_ref[0], preferred_element_type=f32)
    vs_ref[...] = jnp.dot(order_ref[...], v_ref[0], preferred_element_type=f32)
    for start in range(0, ks_ref.shape[1], WIDTH):
        cols = slice(start, start + WIDTH)
        keys = short_filter(steps_of(ks_ref, cols), rim_ref, 2, taps_ref, 1, cols)
        values = short_filter(steps_of(vs_ref, cols), rim_ref, 4, taps_ref, 2, cols)
        products = [a * b for a, b in zip(keys, values)]
        for j in range(0, len(products), 2):
            pair = jnp.concatenate(products[j : j + 2], axis=0)
            prod_ref[SEGMENTS * j : SEGMENTS * (j + 2), cols] = pair.astype(bf16)
        sublane = lax.broadcasted_iota(jnp.int32, (SEGMENTS, WIDTH), 0)
        for pole in range(2):
            lam = power(pr_ref, pi_ref, 0, pole, cols)
            a1 = 2.0 * lam[0]
            a2 = lam[0] * lam[0] + lam[1] * lam[1]
            late = products[0]
            now = a1 * late + products[1]
            for value in products[2:]:
                late, now = now, a1 * now - a2 * late + value
            state = (now - lam[0] * late, lam[1] * late)
            for level in range(3):
                by = 1 << level
                factor = power(pr_ref, pi_ref, 2 + level, pole, cols)
                kept = sublane >= by
                moved = tuple(jnp.where(kept, pltpu.roll(part, by, 0), 0.0) for part in state)
                add = times(factor, moved)
                state = (state[0] + add[0], state[1] + add[1])
            for part in range(2):
                scan_ref[2 * part + pole, :, cols] = state[part]
                total_ref[2 * part + pole : 2 * part + pole + 1, cols] = state[part][SEGMENTS - 1 :]


def local_kernel(order_ref, q_ref, rim_ref, taps_ref, pr_ref, pi_ref, res_ref, skip_ref, prod_ref, scan_ref,
                 query_ref, local_ref, enter_ref, qs_ref):
    qs_ref[...] = jnp.dot(order_ref[...], q_ref[0], preferred_element_type=f32)
    for start in range(0, qs_ref.shape[1], WIDTH):
        cols = slice(start, start + WIDTH)
        queries = short_filter(steps_of(qs_ref, cols), rim_ref, 0, taps_ref, 0, cols)
        for j, value in enumerate(queries):
            query_ref[SEGMENTS * j : SEGMENTS * (j + 1), cols] = value
        products = []
        for j in range(0, len(queries), 2):
            pair = prod_ref[SEGMENTS * j : SEGMENTS * (j + 2), cols].astype(f32)
            products += [pair[:SEGMENTS], pair[SEGMENTS:]]
        before = delayed(products[-1], 0.0)
        skip = row(skip_ref, 0, cols)
        sublane = lax.broadcasted_iota(jnp.int32, (SEGMENTS, WIDTH), 0)
        zero = jnp.zeros((SEGMENTS, WIDTH), f32)
        coefs = []
        for pole in range(2):
            lam = power(pr_ref, pi_ref, 0, pole, cols)
            back = power(pr_ref, pi_ref, 1, pole, cols)
            gain = (row(res_ref, pole, cols), row(res_ref, 2 + pole, cols))
            a1 = 2.0 * lam[0]
            a2 = lam[0] * lam[0] + lam[1] * lam[1]
            b1 = gain[0] * lam[0] + gain[1] * lam[1]
            carry = tuple(delayed(scan_ref[2 * part + pole, :, cols], 0.0) for part in range(2))
            gain_back = times(gain, back)
            y1 = gain[0] * carry[0] - gain[1] * carry[1]
            y2 = gain_back[0] * (carry[0] - before) - gain_back[1] * carry[1]
            coefs.append([a1, a2, gain[0], b1, y1, y2])
            reach = gain
            for level in range(3):
                factor = power(pr_ref, pi_ref, 2 + level, pole, cols)
                bit = (sublane // (1 << level)) % 2 == 1
                reach = times(reach, (jnp.where(bit, factor[0], 1.0), jnp.where(bit, factor[1], 0.0)))
            reach_back = times(reach, back)
            for part in range(2):
                enter_ref[2 * part + pole, :, cols] = reach[part]
                enter_ref[4 + 2 * part + pole, :, cols] = reach_back[part]
        previous = before
        for j, value in enumerate(products):
            total = skip * value
            for pole in range(2):
                a1, a2, b0, b1, y1, y2 = coefs[pole]
                y = a1 * y1 - a2 * y2 + (b0 * value - b1 * previous)
                coefs[pole][4:] = [y, y1]
                total = total + y
            previous = value
            local_ref[SEGMENTS * j : SEGMENTS * (j + 1), cols] = total


def gate_kernel(order_ref, pr_ref, pi_ref, enter_ref, state_ref, query_ref, local_ref, out_ref, gated_ref):
    for start in range(0, out_ref.shape[1], WIDTH):
        cols = slice(start, start + WIDTH)
        queries = steps_of(query_ref, cols)
        local = steps_of(local_ref, cols)
        coefs = []
        for pole in range(2):
            lam = power(pr_ref, pi_ref, 0, pole, cols)
            a1 = 2.0 * lam[0]
            a2 = lam[0] * lam[0] + lam[1] * lam[1]
            state = (row(state_ref, pole, cols), row(state_ref, 2 + pole, cols))
            y1 = enter_ref[pole, :, cols] * state[0] - enter_ref[2 + pole, :, cols] * state[1]
            y2 = enter_ref[4 + pole, :, cols] * state[0] - enter_ref[6 + pole, :, cols] * state[1]
            coefs.append([a1, a2, y1, y2])
        gated = []
        for j in range(len(queries)):
            total = local[j]
            for pole in range(2):
                a1, a2, y1, y2 = coefs[pole]
                y = a1 * y1 - a2 * y2
                coefs[pole][2:] = [y, y1]
                total = total + y
            gated.append(queries[j] * total)
            if j % 2:
                pair = jnp.concatenate(gated[-2:], axis=0)
                gated_ref[SEGMENTS * (j - 1) : SEGMENTS * (j + 1), cols] = pair.astype(bf16)
    out_ref[...] = jnp.dot(order_ref[...], gated_ref[...], preferred_element_type=f32).astype(bf16)


def rows_spec(count, block):
    return pl.BlockSpec((count, block), lambda i: (0, i))


def planes_spec(count, rows, block):
    return pl.BlockSpec((count, rows, block), lambda i: (0, 0, i))


def plane_spec(which, rows, block):
    return pl.BlockSpec((1, rows, block), lambda i: (which, 0, i))


def on_device(projected, short_taps, skip_gain, residues, pole_angles, decay_rates):
    _, rows, channels = projected.shape
    block = min(BLOCK, channels)
    grid = (channels // block,)
    device = lax.axis_index("seq")
    devices = lax.axis_size("seq")
    length = rows // SEGMENTS
    levels = devices.bit_length() - 1

    rims = lax.ppermute(projected[:, rows - 2 :, :], "seq", [(i, i + 1) for i in range(devices - 1)])
    rims = rims.reshape(6, channels).astype(f32)

    def powers(exponents):
        at = jnp.stack([jnp.asarray(e, f32) for e in exponents])[:, None, None]
        damping = jnp.exp(-decay_rates[None] * at)
        phase = pole_angles[None] * at
        return damping * jnp.cos(phase), damping * jnp.sin(phase)

    pr, pi = powers([1, -1, length, 2 * length, 4 * length])
    pr = pr.reshape(10, channels)
    pi = pi.reshape(10, channels)
    spans = [rows << level for level in range(levels)]
    leads = [rows * (device % (1 << level)) for level in range(levels)]
    wide_r, wide_i = powers(spans + leads)

    order = order_matrix(rows, False)
    restore = order_matrix(rows, True)
    whole = pl.BlockSpec((rows, rows), lambda i: (0, 0))
    params = pltpu.CompilerParams(dimension_semantics=("arbitrary",), vmem_limit_bytes=24 << 20)
    shape = jax.ShapeDtypeStruct
    taps = short_taps.reshape(9, channels)
    gains = residues.reshape(4, channels)

    products, scan, total = pl.pallas_call(
        states_kernel,
        grid=grid,
        in_specs=[whole, plane_spec(1, rows, block), plane_spec(2, rows, block), rows_spec(6, block),
                  rows_spec(9, block), rows_spec(10, block), rows_spec(10, block)],
        out_specs=[rows_spec(rows, block), planes_spec(4, SEGMENTS, block), rows_spec(4, block)],
        out_shape=[shape((rows, channels), bf16), shape((4, SEGMENTS, channels), f32), shape((4, channels), f32)],
        scratch_shapes=[pltpu.VMEM((rows, block), f32)] * 2,
        compiler_params=params,
        name="states",
    )(order, projected, projected, rims, taps, pr, pi)

    query, local, enter = pl.pallas_call(
        local_kernel,
        grid=grid,
        in_specs=[whole, plane_spec(0, rows, block), rows_spec(6, block), rows_spec(9, block),
                  rows_spec(10, block), rows_spec(10, block), rows_spec(4, block), rows_spec(1, block),
                  rows_spec(rows, block), planes_spec(4, SEGMENTS, block)],
        out_specs=[rows_spec(rows, block), rows_spec(rows, block), planes_spec(8, SEGMENTS, block)],
        out_shape=[shape((rows, channels), f32), shape((rows, channels), f32), shape((8, SEGMENTS, channels), f32)],
        scratch_shapes=[pltpu.VMEM((rows, block), f32)],
        compiler_params=params,
        name="local",
    )(order, projected, rims, taps, pr, pi, gains, skip_gain[None], products, scan)

    entering = (jnp.zeros((2, channels), f32), jnp.zeros((2, channels), f32))
    ending = (total[:2], total[2:])
    for level in range(levels):
        sent = jnp.concatenate(ending, axis=0).astype(WIRE)
        got = lax.ppermute(sent, "seq", [(i, i ^ (1 << level)) for i in range(devices)]).astype(f32)
        got = (got[:2], got[2:])
        upper = (device >> level) % 2 == 1
        lead = (wide_r[levels + level], wide_i[levels + level])
        span = (wide_r[level], wide_i[level])
        add = times(lead, got)
        entering = tuple(e + jnp.where(upper, a, 0.0) for e, a in zip(entering, add))
        early = tuple(jnp.where(upper, g, e) for g, e in zip(got, ending))
        late = tuple(jnp.where(upper, e, g) for g, e in zip(got, ending))
        grown = times(span, early)
        ending = tuple(a + b for a, b in zip(grown, late))
    state = jnp.concatenate(entering, axis=0)

    return pl.pallas_call(
        gate_kernel,
        grid=grid,
        in_specs=[whole, rows_spec(10, block), rows_spec(10, block), planes_spec(8, SEGMENTS, block),
                  rows_spec(4, block), rows_spec(rows, block), rows_spec(rows, block)],
        out_specs=rows_spec(rows, block),
        out_shape=shape((rows, channels), bf16),
        scratch_shapes=[pltpu.VMEM((rows, block), bf16)],
        compiler_params=params,
        name="gate",
    )(restore, pr, pi, enter, state, query, local)


def solution(mesh):
    return jax.shard_map(
        on_device,
        mesh=mesh,
        in_specs=(P(None, ("grp", "seq"), None), P(), P(), P(), P(), P()),
        out_specs=P(("grp", "seq"), None),
        check_vma=False,
    )
```

```python
import jax
import jax.numpy as jnp
from jax import lax
from jax.experimental import pallas as pl
from jax.experimental.pallas import tpu as pltpu
from jax.sharding import PartitionSpec as P

SEGMENTS = 8
WIDTH = 256
CHUNK = 1024
POLES = 2
WIRE = jnp.float32
f32 = jnp.float32
bf16 = jnp.bfloat16

LAM, BACK, SEGMENT, SPAN = 0, 1, 2, 5


def order_matrix(row_count, inverse):
    length = row_count // SEGMENTS
    ordered = lax.broadcasted_iota(jnp.int32, (row_count, row_count), 1 if inverse else 0)
    natural = lax.broadcasted_iota(jnp.int32, (row_count, row_count), 0 if inverse else 1)
    wanted = length * (ordered % SEGMENTS) + ordered // SEGMENTS
    return (wanted == natural).astype(f32).astype(bf16)


def wide(value):
    return jnp.broadcast_to(value, (SEGMENTS, value.shape[1]))


def times(a, b):
    return (a[0] * b[0] - a[1] * b[1], a[0] * b[1] + a[1] * b[0])


def plus(a, b):
    return (a[0] + b[0], a[1] + b[1])


def pair_at(ref, index, cols):
    return (ref[4 * index : 4 * index + 2, cols], ref[4 * index + 2 : 4 * index + 4, cols])


def put_pair(ref, index, cols, value):
    ref[4 * index : 4 * index + 2, cols] = value[0]
    ref[4 * index + 2 : 4 * index + 4, cols] = value[1]


def pole_at(ref, index, pole, cols):
    return (wide(ref[pl.ds(4 * index + pole, 1), cols]), wide(ref[pl.ds(4 * index + 2 + pole, 1), cols]))


def half_angle(angle):
    x = 0.5 * angle
    u = x * x
    sine = 1.0 / 6227020800.0
    for term in (-1.0 / 39916800.0, 1.0 / 362880.0, -1.0 / 5040.0, 1.0 / 120.0, -1.0 / 6.0, 1.0):
        sine = sine * u + term
    cosine = -1.0 / 87178291200.0
    for term in (1.0 / 479001600.0, -1.0 / 3628800.0, 1.0 / 40320.0, -1.0 / 720.0, 1.0 / 24.0, -0.5, 1.0):
        cosine = cosine * u + term
    return cosine, sine * x


def fill_powers(power_ref, angle_ref, decay_ref, length, levels):
    cols = slice(None)
    cosine, sine = half_angle(angle_ref[...])
    turn = (1.0 - 2.0 * sine * sine, 2.0 * sine * cosine)
    decay = decay_ref[...]
    damping = jnp.exp(-decay)
    growth = jnp.exp(decay)
    value = (damping * turn[0], damping * turn[1])
    put_pair(power_ref, LAM, cols, value)
    put_pair(power_ref, BACK, cols, (growth * turn[0], -growth * turn[1]))
    for _ in range(length.bit_length() - 1):
        value = times(value, value)
    for level in range(3 + levels):
        put_pair(power_ref, SEGMENT + level, cols, value)
        value = times(value, value)


def steps_of(ref, cols):
    return [ref[SEGMENTS * j : SEGMENTS * (j + 1), cols] for j in range(ref.shape[0] // SEGMENTS)]


def first_mask():
    return lax.broadcasted_iota(jnp.int32, (SEGMENTS, WIDTH), 0) == 0


def delayed(value):
    return jnp.where(first_mask(), 0.0, pltpu.roll(value, 1, 0))


def short_filter(steps, taps_ref, which, cols):
    taps = [wide(taps_ref[tap, which : which + 1, cols]) for tap in range(3)]
    padded = [delayed(steps[-2]), delayed(steps[-1])] + steps
    return [
        taps[0] * padded[j] + taps[1] * padded[j + 1] + taps[2] * padded[j + 2]
        for j in range(len(steps))
    ]


def feedback(lam):
    return 2.0 * lam[0], lam[0] * lam[0] + lam[1] * lam[1]


def span(start, size):
    return pl.ds(pl.multiple_of(start, 128), size)


def loop_columns(chunk_index, chunk, body):
    for part in range(chunk // WIDTH):
        body(part * WIDTH, chunk_index * chunk + part * WIDTH)


def states_kernel(order_ref, angle_ref, decay_ref, taps_ref, proj_ref,
                  prod_ref, scan_ref, total_ref, edge_ref, power_ref,
                  k_ref, v_ref, out_ref, ks_ref, vs_ref, in_sem, out_sem, *, levels):
    rows, channels = k_ref.shape
    chunk = ks_ref.shape[1]
    count = channels // chunk

    def fetch(i, which, ref):
        cols = span(i * chunk, chunk)
        return pltpu.make_async_copy(proj_ref.at[which, :, cols], ref.at[:, cols], in_sem.at[which - 1, i])

    def send(i):
        cols = span(i * chunk, chunk)
        return pltpu.make_async_copy(out_ref.at[:, cols], prod_ref.at[:, cols], out_sem.at[i])

    for i in range(count):
        fetch(i, 1, k_ref).start()
        fetch(i, 2, v_ref).start()
    fill_powers(power_ref, angle_ref, decay_ref, rows // SEGMENTS, levels)

    def body(i, _):
        fetch(i, 1, k_ref).wait()
        fetch(i, 2, v_ref).wait()
        at = span(i * chunk, chunk)
        ks_ref[...] = jnp.dot(order_ref[...], k_ref[:, at], preferred_element_type=f32)
        vs_ref[...] = jnp.dot(order_ref[...], v_ref[:, at], preferred_element_type=f32)
        for step in range(2):
            edge_ref[step : step + 1, at] = ks_ref[SEGMENTS * step : SEGMENTS * step + 1, :]
            edge_ref[2 + step : 3 + step, at] = vs_ref[SEGMENTS * step : SEGMENTS * step + 1, :]

        def column(inner, outer):
            cols = slice(inner, inner + WIDTH)
            here = span(outer, WIDTH)
            keys = short_filter(steps_of(ks_ref, cols), taps_ref, 1, here)
            values = short_filter(steps_of(vs_ref, cols), taps_ref, 2, here)
            products = [a * b for a, b in zip(keys, values)]
            for j in range(2):
                products[j] = jnp.where(first_mask(), 0.0, products[j])
            for j in range(0, len(products), 2):
                both = jnp.concatenate(products[j : j + 2], axis=0)
                out_ref[SEGMENTS * j : SEGMENTS * (j + 2), here] = both.astype(bf16)
            sublane = lax.broadcasted_iota(jnp.int32, (SEGMENTS, WIDTH), 0)
            for pole in range(POLES):
                lam = pole_at(power_ref, LAM, pole, here)
                a1, a2 = feedback(lam)
                late = products[0]
                now = a1 * late + products[1]
                for value in products[2:]:
                    late, now = now, a1 * now - a2 * late + value
                state = (now - lam[0] * late, lam[1] * late)
                for level in range(3):
                    by = 1 << level
                    factor = pole_at(power_ref, SEGMENT + level, pole, here)
                    moved = tuple(jnp.where(sublane >= by, pltpu.roll(part, by, 0), 0.0) for part in state)
                    state = plus(state, times(factor, moved))
                for part in range(2):
                    scan_ref[2 * part + pole, :, here] = state[part]
                    total_ref[2 * part + pole : 2 * part + pole + 1, here] = state[part][SEGMENTS - 1 :]

        loop_columns(i, chunk, column)
        send(i).start()
        return 0

    lax.fori_loop(0, count, body, 0)
    for i in range(count):
        send(i).wait()


def first_products(rim_ref, edge_ref, taps_ref, cols):
    before = rim_ref[:, :, cols].astype(f32)

    def filtered(which, edge, at):
        sequence = [before[which, 0:1], before[which, 1:2], edge_ref[edge : edge + 1, cols], edge_ref[edge + 1 : edge + 2, cols]]
        return sum(taps_ref[tap, which : which + 1, cols] * sequence[at + tap] for tap in range(3))

    return [filtered(1, 0, at) * filtered(2, 2, at) for at in range(2)]


def rims_kernel(rim_ref, edge_ref, taps_ref, power_ref, total_ref, ending_ref, extra_ref):
    cols = slice(None)
    first, second = first_products(rim_ref, edge_ref, taps_ref, cols)
    back = pair_at(power_ref, BACK, cols)
    inner = times(back, (second * back[0] + first, second * back[1]))
    put_pair(extra_ref, 0, cols, inner)
    grown = times(pair_at(power_ref, SPAN, cols), inner)
    put_pair(ending_ref, 0, cols, plus(grown, pair_at(total_ref, 0, cols)))


def join_kernel(ending_ref, got_ref, power_ref, joined_ref, *, level):
    upper = (lax.axis_index("seq") >> level) % 2 == 1
    cols = slice(None)
    mine = pair_at(ending_ref, 0, cols)
    other = tuple(part.astype(f32) for part in pair_at(got_ref, 0, cols))
    factor = pair_at(power_ref, SPAN + level, cols)
    early = tuple(jnp.where(upper, o, m) for o, m in zip(other, mine))
    late = tuple(jnp.where(upper, m, o) for o, m in zip(other, mine))
    put_pair(joined_ref, 0, cols, plus(times(factor, early), late))


def local_kernel(order_ref, taps_ref, gain_ref, skip_ref, power_ref, scan_ref, proj_ref, prod_ref,
                 query_ref, local_ref, enter_ref, lead_ref,
                 q_ref, p_ref, query_out, local_out, qs_ref, in_sem, out_sem, *, levels):
    rows, channels = q_ref.shape
    chunk = qs_ref.shape[1]
    count = channels // chunk

    def copies(i):
        cols = span(i * chunk, chunk)
        return (
            pltpu.make_async_copy(proj_ref.at[0, :, cols], q_ref.at[:, cols], in_sem.at[0, i]),
            pltpu.make_async_copy(prod_ref.at[:, cols], p_ref.at[:, cols], in_sem.at[1, i]),
        )

    def sends(i):
        cols = span(i * chunk, chunk)
        return (
            pltpu.make_async_copy(query_out.at[:, cols], query_ref.at[:, cols], out_sem.at[0, i]),
            pltpu.make_async_copy(local_out.at[:, cols], local_ref.at[:, cols], out_sem.at[1, i]),
        )

    for i in range(count):
        for copy in copies(i):
            copy.start()
    device = lax.axis_index("seq")
    lead = (jnp.ones((POLES, channels), f32), jnp.zeros((POLES, channels), f32))
    for level in range(levels):
        upper = (device >> level) % 2 == 1
        put_pair(lead_ref, level, slice(None), tuple(jnp.where(upper, part, 0.0) for part in lead))
        grown = times(lead, pair_at(power_ref, SPAN + level, slice(None)))
        lead = tuple(jnp.where(upper, g, part) for g, part in zip(grown, lead))

    def body(i, _):
        for copy in copies(i):
            copy.wait()
        at = span(i * chunk, chunk)
        qs_ref[...] = jnp.dot(order_ref[...], q_ref[:, at], preferred_element_type=f32)

        def column(inner, outer):
            cols = slice(inner, inner + WIDTH)
            here = span(outer, WIDTH)
            queries = short_filter(steps_of(qs_ref, cols), taps_ref, 0, here)
            for j, value in enumerate(queries):
                query_out[SEGMENTS * j : SEGMENTS * (j + 1), here] = value
            products = []
            for j in range(0, len(queries), 2):
                both = p_ref[SEGMENTS * j : SEGMENTS * (j + 2), here].astype(f32)
                products += [both[:SEGMENTS], both[SEGMENTS:]]
            before = delayed(products[-1])
            skip = wide(skip_ref[0:1, here])
            sublane = lax.broadcasted_iota(jnp.int32, (SEGMENTS, WIDTH), 0)
            coefs = []
            for pole in range(POLES):
                lam = pole_at(power_ref, LAM, pole, here)
                back = pole_at(power_ref, BACK, pole, here)
                gain = tuple(wide(gain_ref[part, pole : pole + 1, here]) for part in range(2))
                a1, a2 = feedback(lam)
                b1 = gain[0] * lam[0] + gain[1] * lam[1]
                carry = tuple(delayed(scan_ref[2 * part + pole, :, here]) for part in range(2))
                gain_back = times(gain, back)
                y1 = gain[0] * carry[0] - gain[1] * carry[1]
                y2 = gain_back[0] * (carry[0] - before) - gain_back[1] * carry[1]
                coefs.append([a1, a2, gain[0], b1, y1, y2])
                reach = gain
                for level in range(3):
                    factor = pole_at(power_ref, SEGMENT + level, pole, here)
                    bit = (sublane // (1 << level)) % 2 == 1
                    reach = times(reach, (jnp.where(bit, factor[0], 1.0), jnp.where(bit, factor[1], 0.0)))
                for part in range(2):
                    enter_ref[2 * part + pole, :, here] = reach[part]
            previous = before
            for j, value in enumerate(products):
                total = skip * value
                for pole in range(POLES):
                    a1, a2, b0, b1, y1, y2 = coefs[pole]
                    y = a1 * y1 - a2 * y2 + (b0 * value - b1 * previous)
                    coefs[pole][4:] = [y, y1]
                    total = total + y
                previous = value
                local_out[SEGMENTS * j : SEGMENTS * (j + 1), here] = total

        loop_columns(i, chunk, column)
        for copy in sends(i):
            copy.start()
        return 0

    lax.fori_loop(0, count, body, 0)
    for i in range(count):
        for copy in sends(i):
            copy.wait()


def gate_kernel(order_ref, taps_ref, gain_ref, skip_ref, power_ref, enter_ref, lead_ref, extra_ref,
                rim_ref, edge_ref, *rest, levels):
    got_refs = rest[:levels]
    query_hbm, local_hbm, out_hbm = rest[levels : levels + 3]
    q_ref, l_ref, out_ref, gated_ref, state_ref, fix_ref, in_sem, out_sem = rest[levels + 3 :]
    rows, channels = q_ref.shape
    chunk = gated_ref.shape[1]
    count = channels // chunk

    def copies(i):
        cols = span(i * chunk, chunk)
        return (
            pltpu.make_async_copy(query_hbm.at[:, cols], q_ref.at[:, cols], in_sem.at[0, i]),
            pltpu.make_async_copy(local_hbm.at[:, cols], l_ref.at[:, cols], in_sem.at[1, i]),
        )

    def send(i):
        cols = span(i * chunk, chunk)
        return pltpu.make_async_copy(out_ref.at[:, cols], out_hbm.at[:, cols], out_sem.at[i])

    for i in range(count):
        for copy in copies(i):
            copy.start()
    cols = slice(None)
    state = pair_at(extra_ref, 0, cols)
    for level in range(levels):
        got = tuple(part.astype(f32) for part in pair_at(got_refs[level], 0, cols))
        state = plus(state, times(pair_at(lead_ref, level, cols), got))
    put_pair(state_ref, 0, cols, state)
    first, second = first_products(rim_ref, edge_ref, taps_ref, cols)
    skip = skip_ref[...]
    back = pair_at(power_ref, BACK, cols)
    jump = sum(gain_ref[0, pole : pole + 1] * back[0][pole : pole + 1] - gain_ref[1, pole : pole + 1] * back[1][pole : pole + 1]
               for pole in range(POLES))
    fix_ref[0:1] = skip * first - jump * second
    fix_ref[1:2] = skip * second
    before = rim_ref[0].astype(f32)
    fix_ref[2:3] = taps_ref[0, 0:1] * before[0:1] + taps_ref[1, 0:1] * before[1:2]
    fix_ref[3:4] = taps_ref[0, 0:1] * before[1:2]

    def body(i, _):
        for copy in copies(i):
            copy.wait()

        def column(inner, outer):
            cols = slice(inner, inner + WIDTH)
            here = span(outer, WIDTH)
            queries = steps_of(q_ref, here)
            local = steps_of(l_ref, here)
            for j in range(2):
                local[j] = local[j] + jnp.where(first_mask(), fix_ref[j : j + 1, here], 0.0)
                queries[j] = queries[j] + jnp.where(first_mask(), fix_ref[2 + j : 3 + j, here], 0.0)
            coefs = []
            for pole in range(POLES):
                lam = pole_at(power_ref, LAM, pole, here)
                back = pole_at(power_ref, BACK, pole, here)
                state = times(pole_at(state_ref, 0, pole, here), (enter_ref[pole, :, here], enter_ref[2 + pole, :, here]))
                y2 = state[0] * back[0] - state[1] * back[1]
                coefs.append([*feedback(lam), state[0], y2])
            gated = []
            for j in range(len(queries)):
                total = local[j]
                for pole in range(POLES):
                    a1, a2, y1, y2 = coefs[pole]
                    y = a1 * y1 - a2 * y2
                    coefs[pole][2:] = [y, y1]
                    total = total + y
                gated.append(queries[j] * total)
                if j % 2:
                    both = jnp.concatenate(gated[-2:], axis=0)
                    gated_ref[SEGMENTS * (j - 1) : SEGMENTS * (j + 1), cols] = both.astype(bf16)

        loop_columns(i, chunk, column)
        out_ref[:, span(i * chunk, chunk)] = jnp.dot(
            order_ref[...], gated_ref[...], preferred_element_type=f32).astype(bf16)
        send(i).start()
        return 0

    lax.fori_loop(0, count, body, 0)
    for i in range(count):
        send(i).wait()


def kernel_call(body, name, outs, scratch, operands, in_hbm, out_hbm, **options):
    def spec(far):
        return pl.BlockSpec(memory_space=pltpu.HBM if far else pltpu.VMEM)

    def bound(*refs):
        return body(*refs, **options)

    return pl.pallas_call(
        bound,
        in_specs=[spec(far) for far in in_hbm],
        out_specs=[spec(far) for far in out_hbm],
        out_shape=[jax.ShapeDtypeStruct(shape, dtype) for shape, dtype in outs],
        scratch_shapes=scratch,
        compiler_params=pltpu.CompilerParams(vmem_limit_bytes=32 << 20),
        name=name,
    )(*operands)


def on_device(projected, short_taps, skip_gain, residues, pole_angles, decay_rates):
    _, rows, channels = projected.shape
    chunk = min(CHUNK, channels)
    count = channels // chunk
    devices = lax.axis_size("seq")
    levels = devices.bit_length() - 1
    skip_row = skip_gain[None]
    state_shape = ((4, channels), f32)
    plane = (rows, channels)

    rims = lax.ppermute(projected[:, rows - 2 :, :], "seq", [(i, i + 1) for i in range(devices - 1)])

    order = jnp.asarray(order_matrix(rows, False))
    restore = jnp.asarray(order_matrix(rows, True))
    dma = pltpu.SemaphoreType.DMA

    products, scan, total, edges, powers = kernel_call(
        states_kernel, "states",
        [(plane, bf16), ((4, SEGMENTS, channels), f32), state_shape, ((4, channels), f32),
         ((4 * (SPAN + levels), channels), f32)],
        [pltpu.VMEM(plane, bf16)] * 3 + [pltpu.VMEM((rows, chunk), f32)] * 2 + [dma((2, count)), dma((count,))],
        [order, pole_angles, decay_rates, short_taps, projected],
        [False] * 4 + [True], [True] + [False] * 4, levels=levels)

    ending, extra = kernel_call(
        rims_kernel, "rims", [state_shape, state_shape], [],
        [rims, edges, short_taps, powers, total], [False] * 5, [False] * 2)

    query, local, enter, leads = kernel_call(
        local_kernel, "local",
        [(plane, f32), (plane, f32), ((4, SEGMENTS, channels), f32), ((4 * levels, channels), f32)],
        [pltpu.VMEM(plane, bf16)] * 2 + [pltpu.VMEM(plane, f32)] * 2 + [pltpu.VMEM((rows, chunk), f32)]
        + [dma((2, count)), dma((2, count))],
        [order, short_taps, residues, skip_row, powers, scan, projected, products],
        [False] * 6 + [True] * 2, [True] * 2 + [False] * 2, levels=levels)

    received = []
    for level in range(levels):
        sent = ending.astype(WIRE)
        received.append(lax.ppermute(sent, "seq", [(i, i ^ (1 << level)) for i in range(devices)]))
        if level + 1 < levels:
            (ending,) = kernel_call(
                join_kernel, "join", [state_shape], [], [ending, received[-1], powers], [False] * 3, [False],
                level=level)

    (out,) = kernel_call(
        gate_kernel, "gate", [(plane, bf16)],
        [pltpu.VMEM(plane, f32)] * 2 + [pltpu.VMEM(plane, bf16), pltpu.VMEM((rows, chunk), bf16),
         pltpu.VMEM((4, channels), f32), pltpu.VMEM((4, channels), f32), dma((2, count)), dma((count,))],
        [restore, short_taps, residues, skip_row, powers, enter, leads, extra, rims, edges, *received, query, local],
        [False] * (10 + levels) + [True] * 2, [True], levels=levels)
    return out


def solution(mesh):
    return jax.shard_map(
        on_device,
        mesh=mesh,
        in_specs=(P(None, ("grp", "seq"), None), P(), P(), P(), P(), P()),
        out_specs=P(("grp", "seq"), None),
        check_vma=False,
    )
```

```python
import jax
import jax.numpy as jnp
from jax import lax
from jax.experimental import pallas as pl
from jax.experimental.pallas import tpu as pltpu
from jax.sharding import PartitionSpec as P

SEGMENTS = 8
WIDTH = 256
CHUNK = 512
POLES = 2
SUBROWS = 16
PARTS = (1, 1, 2)
f32 = jnp.float32
bf16 = jnp.bfloat16

LAM, BACK, SEGMENT, SPAN = 0, 1, 2, 5


def order_matrix(row_count, inverse):
    length = row_count // SEGMENTS
    ordered = lax.broadcasted_iota(jnp.int32, (row_count, row_count), 1 if inverse else 0)
    natural = lax.broadcasted_iota(jnp.int32, (row_count, row_count), 0 if inverse else 1)
    wanted = length * (ordered % SEGMENTS) + ordered // SEGMENTS
    return (wanted == natural).astype(f32).astype(bf16)


def wide(value):
    return jnp.broadcast_to(value, (SEGMENTS, value.shape[1]))


def times(a, b):
    return (a[0] * b[0] - a[1] * b[1], a[0] * b[1] + a[1] * b[0])


def plus(a, b):
    return (a[0] + b[0], a[1] + b[1])


def pair_at(ref, index, cols):
    return (ref[4 * index : 4 * index + 2, cols], ref[4 * index + 2 : 4 * index + 4, cols])


def put_pair(ref, index, cols, value):
    ref[4 * index : 4 * index + 2, cols] = value[0]
    ref[4 * index + 2 : 4 * index + 4, cols] = value[1]


def pole_at(ref, index, pole, cols):
    return (wide(ref[pl.ds(4 * index + pole, 1), cols]), wide(ref[pl.ds(4 * index + 2 + pole, 1), cols]))


def half_angle(angle):
    x = 0.5 * angle
    u = x * x
    sine = 1.0 / 6227020800.0
    for term in (-1.0 / 39916800.0, 1.0 / 362880.0, -1.0 / 5040.0, 1.0 / 120.0, -1.0 / 6.0, 1.0):
        sine = sine * u + term
    cosine = -1.0 / 87178291200.0
    for term in (1.0 / 479001600.0, -1.0 / 3628800.0, 1.0 / 40320.0, -1.0 / 720.0, 1.0 / 24.0, -0.5, 1.0):
        cosine = cosine * u + term
    return cosine, sine * x


def fill_powers(power_ref, angle_ref, decay_ref, length, levels):
    cols = slice(None)
    cosine, sine = half_angle(angle_ref[...])
    turn = (1.0 - 2.0 * sine * sine, 2.0 * sine * cosine)
    decay = decay_ref[...]
    damping = jnp.exp(-decay)
    growth = jnp.exp(decay)
    value = (damping * turn[0], damping * turn[1])
    put_pair(power_ref, LAM, cols, value)
    put_pair(power_ref, BACK, cols, (growth * turn[0], -growth * turn[1]))
    for _ in range(length.bit_length() - 1):
        value = times(value, value)
    for level in range(3 + levels):
        put_pair(power_ref, SEGMENT + level, cols, value)
        value = times(value, value)


def steps_of(ref, cols):
    return [ref[SEGMENTS * j : SEGMENTS * (j + 1), cols] for j in range(ref.shape[0] // SEGMENTS)]


def first_mask():
    return lax.broadcasted_iota(jnp.int32, (SEGMENTS, WIDTH), 0) == 0


def delayed(value):
    return jnp.where(first_mask(), 0.0, pltpu.roll(value, 1, 0))


def short_filter(steps, taps_ref, which, cols):
    taps = [wide(taps_ref[tap, which : which + 1, cols]) for tap in range(3)]
    padded = [delayed(steps[-2]), delayed(steps[-1])] + steps
    return [
        taps[0] * padded[j] + taps[1] * padded[j + 1] + taps[2] * padded[j + 2]
        for j in range(len(steps))
    ]


def feedback(lam):
    return 2.0 * lam[0], lam[0] * lam[0] + lam[1] * lam[1]


def span(start, size):
    return pl.ds(pl.multiple_of(start, 128), size)


def loop_columns(chunk_index, chunk, body):
    for part in range(chunk // WIDTH):
        body(part * WIDTH, chunk_index * chunk + part * WIDTH)


def states_kernel(angle_hbm, decay_hbm, taps_hbm, gain_hbm, skip_hbm, proj_ref,
                  prod_ref, scan_ref, total_ref, edge_ref, tail_ref, power_ref, taps_ref, gain_ref, skip_ref,
                  order_ref, angle_ref, decay_ref, k_ref, v_ref, top_ref, end_ref, ks_ref, vs_ref,
                  small_sem, in_sem, *, levels):
    rows, channels = k_ref.shape
    chunk = ks_ref.shape[1]
    count = channels // chunk
    last = rows - SUBROWS
    smalls = [
        pltpu.make_async_copy(source, target, small_sem.at[i])
        for i, (source, target) in enumerate([
            (angle_hbm, angle_ref), (decay_hbm, decay_ref), (taps_hbm, taps_ref), (gain_hbm, gain_ref),
            (skip_hbm, skip_ref), (proj_ref.at[pl.ds(1, 2), pl.ds(0, SUBROWS)], top_ref),
            (proj_ref.at[:, pl.ds(last, SUBROWS)], end_ref)])
    ]

    def fetch(i, which, ref):
        cols = span(i * chunk, chunk)
        return pltpu.make_async_copy(proj_ref.at[which, :, cols], ref.at[:, cols], in_sem.at[which - 1, i])

    for copy in smalls[:3]:
        copy.start()
    for i in range(count):
        fetch(i, 1, k_ref).start()
        fetch(i, 2, v_ref).start()
    for copy in smalls[3:]:
        copy.start()
    order_ref[...] = order_matrix(rows, False)
    for copy in smalls[:3]:
        copy.wait()
    fill_powers(power_ref, angle_ref, decay_ref, rows // SEGMENTS, levels)

    def body(i, _):
        fetch(i, 1, k_ref).wait()
        fetch(i, 2, v_ref).wait()
        at = span(i * chunk, chunk)
        ks_ref[...] = jnp.dot(order_ref[...], k_ref[:, at], preferred_element_type=f32)
        vs_ref[...] = jnp.dot(order_ref[...], v_ref[:, at], preferred_element_type=f32)

        def column(inner, outer):
            cols = slice(inner, inner + WIDTH)
            here = span(outer, WIDTH)
            keys = short_filter(steps_of(ks_ref, cols), taps_ref, 1, here)
            values = short_filter(steps_of(vs_ref, cols), taps_ref, 2, here)
            products = [a * b for a, b in zip(keys, values)]
            for j in range(2):
                products[j] = jnp.where(first_mask(), 0.0, products[j])
            for j in range(0, len(products), 2):
                both = jnp.concatenate(products[j : j + 2], axis=0)
                prod_ref[SEGMENTS * j : SEGMENTS * (j + 2), here] = both.astype(bf16)
            sublane = lax.broadcasted_iota(jnp.int32, (SEGMENTS, WIDTH), 0)
            for pole in range(POLES):
                lam = pole_at(power_ref, LAM, pole, here)
                a1, a2 = feedback(lam)
                late = products[0]
                now = a1 * late + products[1]
                for value in products[2:]:
                    late, now = now, a1 * now - a2 * late + value
                state = (now - lam[0] * late, lam[1] * late)
                for level in range(3):
                    by = 1 << level
                    factor = pole_at(power_ref, SEGMENT + level, pole, here)
                    moved = tuple(jnp.where(sublane >= by, pltpu.roll(part, by, 0), 0.0) for part in state)
                    state = plus(state, times(factor, moved))
                for part in range(2):
                    scan_ref[2 * part + pole, :, here] = state[part]
                    total_ref[2 * part + pole : 2 * part + pole + 1, here] = state[part][SEGMENTS - 1 :]

        loop_columns(i, chunk, column)
        return 0

    lax.fori_loop(0, count, body, 0)
    for copy in smalls[3:]:
        copy.wait()
    edge_ref[0:2] = top_ref[0, 0:2]
    edge_ref[2:4] = top_ref[1, 0:2]
    for which in range(3):
        tail = end_ref[which, SUBROWS - 2 : SUBROWS]
        edge_ref[4 + 2 * which : 6 + 2 * which] = tail
        tail_ref[2 * which : 2 * which + 2] = tail


def first_products(tail, heads, taps_ref):
    def filtered(which, at):
        sequence = [tail[2 * which : 2 * which + 1], tail[2 * which + 1 : 2 * which + 2],
                    heads[2 * which - 2 : 2 * which - 1], heads[2 * which - 1 : 2 * which]]
        return sum(taps_ref[tap, which : which + 1] * sequence[at + tap] for tap in range(3))

    return [filtered(1, at) * filtered(2, at) for at in range(2)]


def pick(condition, a, b):
    return tuple(jnp.where(condition, x, y) for x, y in zip(a, b))


def put_wire(wire_ref, value):
    for part in range(2):
        total = value[part][0:1] + value[part][1:2]
        difference = value[part][0:1] - value[part][1:2]
        wire_ref[2 * part : 2 * part + 2] = jnp.concatenate([total, difference], axis=0).astype(bf16)


def from_wire(wire_ref):
    value = []
    for part in range(2):
        both = wire_ref[2 * part : 2 * part + 2].astype(f32)
        total, difference = both[0:1], both[1:2]
        value.append(0.5 * jnp.concatenate([total + difference, total - difference], axis=0))
    return tuple(value)


def merge_kernel(total_ref, mate_ref, edge_ref, mate_edge_ref, far_even_ref, far_odd_ref, power_ref, taps_ref,
                 gain_ref, skip_ref, ending_ref, wire_ref, lead_ref, enter_ref, fix_ref):
    cols = slice(None)
    odd = lax.axis_index("seq") % 2 == 1
    far = far_even_ref[...].astype(f32) + far_odd_ref[...].astype(f32)
    mine = edge_ref[...].astype(f32)
    mates = mate_edge_ref[...].astype(f32)
    even_edge, odd_edge = jnp.where(odd, mates, mine), jnp.where(odd, mine, mates)
    power = pair_at(power_ref, SPAN, cols)
    back = pair_at(power_ref, BACK, cols)
    own, mate = pair_at(total_ref, 0, cols), pair_at(mate_ref, 0, cols)
    even_total, odd_total = pick(odd, mate, own), pick(odd, own, mate)
    extras, firsts, endings = [], [], []
    for tail, edge, total in ((far, even_edge, even_total), (even_edge[4:10], odd_edge, odd_total)):
        first, second = first_products(tail, edge[0:4], taps_ref)
        extra = times(back, (second * back[0] + first, second * back[1]))
        extras.append(extra)
        firsts.append((first, second))
        endings.append(plus(total, times(power, extra)))
    joined = plus(times(power, endings[0]), endings[1])
    put_pair(ending_ref, 0, cols, joined)
    put_wire(wire_ref, joined)
    one = (jnp.ones_like(power[0]), jnp.zeros_like(power[0]))
    put_pair(lead_ref, 0, cols, pick(odd, power, one))
    put_pair(enter_ref, 0, cols, pick(odd, plus(endings[0], extras[1]), extras[0]))
    first, second = pick(odd, firsts[1], firsts[0])
    skip = skip_ref[...]
    jump = sum(gain_ref[0, pole : pole + 1] * back[0][pole : pole + 1] - gain_ref[1, pole : pole + 1] * back[1][pole : pole + 1]
               for pole in range(POLES))
    fix_ref[0:1] = skip * first - jump * second
    fix_ref[1:2] = skip * second
    before = jnp.where(odd, even_edge[4:6], far[0:2])
    fix_ref[2:3] = taps_ref[0, 0:1] * before[0:1] + taps_ref[1, 0:1] * before[1:2]
    fix_ref[3:4] = taps_ref[0, 0:1] * before[1:2]


def join_kernel(ending_ref, got_ref, power_ref, lead_ref, enter_ref,
                joined_ref, wire_ref, next_lead_ref, next_enter_ref, *, level):
    upper = (lax.axis_index("seq") >> level) % 2 == 1
    cols = slice(None)
    mine = pair_at(ending_ref, 0, cols)
    other = from_wire(got_ref)
    factor = pair_at(power_ref, SPAN + level, cols)
    early, late = pick(upper, other, mine), pick(upper, mine, other)
    joined = plus(times(factor, early), late)
    put_pair(joined_ref, 0, cols, joined)
    put_wire(wire_ref, joined)
    lead = pair_at(lead_ref, 0, cols)
    enter = pair_at(enter_ref, 0, cols)
    put_pair(next_lead_ref, 0, cols, pick(upper, times(lead, factor), lead))
    put_pair(next_enter_ref, 0, cols, pick(upper, plus(enter, times(lead, other)), enter))


def local_kernel(taps_ref, gain_ref, skip_ref, power_ref, scan_ref, prod_ref, proj_ref, after_ref,
                 query_ref, local_ref, enter_ref, order_ref, q_ref, qs_ref, in_sem, *, base):
    rows, channels = q_ref.shape
    chunk = qs_ref.shape[1]
    count = channels // chunk

    def fetch(i):
        return pltpu.make_async_copy(
            proj_ref.at[0, :, span(base + i * chunk, chunk)], q_ref.at[:, span(i * chunk, chunk)], in_sem.at[i])

    for i in range(count):
        fetch(i).start()
    order_ref[...] = order_matrix(rows, False)

    def body(i, _):
        fetch(i).wait()
        qs_ref[...] = jnp.dot(order_ref[...], q_ref[:, span(i * chunk, chunk)], preferred_element_type=f32)

        def column(inner, outer):
            cols = slice(inner, inner + WIDTH)
            put = span(outer, WIDTH)
            here = span(base + outer, WIDTH)
            queries = short_filter(steps_of(qs_ref, cols), taps_ref, 0, here)
            for j, value in enumerate(queries):
                query_ref[SEGMENTS * j : SEGMENTS * (j + 1), put] = value
            products = []
            for j in range(0, len(queries), 2):
                both = prod_ref[SEGMENTS * j : SEGMENTS * (j + 2), here].astype(f32)
                products += [both[:SEGMENTS], both[SEGMENTS:]]
            before = delayed(products[-1])
            skip = wide(skip_ref[0:1, here])
            sublane = lax.broadcasted_iota(jnp.int32, (SEGMENTS, WIDTH), 0)
            coefs = []
            for pole in range(POLES):
                lam = pole_at(power_ref, LAM, pole, here)
                back = pole_at(power_ref, BACK, pole, here)
                gain = tuple(wide(gain_ref[part, pole : pole + 1, here]) for part in range(2))
                a1, a2 = feedback(lam)
                b1 = gain[0] * lam[0] + gain[1] * lam[1]
                carry = tuple(delayed(scan_ref[2 * part + pole, :, here]) for part in range(2))
                gain_back = times(gain, back)
                y1 = gain[0] * carry[0] - gain[1] * carry[1]
                y2 = gain_back[0] * (carry[0] - before) - gain_back[1] * carry[1]
                coefs.append([a1, a2, gain[0], b1, y1, y2])
                reach = gain
                for level in range(3):
                    factor = pole_at(power_ref, SEGMENT + level, pole, here)
                    bit = (sublane // (1 << level)) % 2 == 1
                    reach = times(reach, (jnp.where(bit, factor[0], 1.0), jnp.where(bit, factor[1], 0.0)))
                for part in range(2):
                    enter_ref[2 * part + pole, :, put] = reach[part]
            previous = before
            for j, value in enumerate(products):
                total = skip * value
                for pole in range(POLES):
                    a1, a2, b0, b1, y1, y2 = coefs[pole]
                    y = a1 * y1 - a2 * y2 + (b0 * value - b1 * previous)
                    coefs[pole][4:] = [y, y1]
                    total = total + y
                previous = value
                local_ref[SEGMENTS * j : SEGMENTS * (j + 1), put] = total

        loop_columns(i, chunk, column)
        return 0

    lax.fori_loop(0, count, body, 0)


def gate_kernel(power_ref, got_ref, lead_ref, enter_ref, fix_ref, *rest, level, parts):
    tables = [rest[3 * i : 3 * i + 3] for i in range(len(parts))]
    out_hbm, order_ref, out_ref, gated_ref, state_ref, out_sem = rest[3 * len(parts) :]
    rows, channels = out_ref.shape
    chunk = gated_ref.shape[1]
    count = channels // chunk
    cols = slice(None)
    upper = (lax.axis_index("seq") >> level) % 2 == 1
    state = pair_at(enter_ref, 0, cols)
    add = times(pair_at(lead_ref, 0, cols), from_wire(got_ref))
    put_pair(state_ref, 0, cols, pick(upper, plus(state, add), state))
    order_ref[...] = order_matrix(rows, True)

    def send(i):
        place = span(i * chunk, chunk)
        return pltpu.make_async_copy(out_ref.at[:, place], out_hbm.at[:, place], out_sem.at[i])

    base = 0
    for part, (query_ref, local_ref, reach_ref) in zip(parts, tables):

        def body(i, _, base=base, query_ref=query_ref, local_ref=local_ref, reach_ref=reach_ref):
            def column(inner, outer):
                cols = slice(inner, inner + WIDTH)
                take = span(outer, WIDTH)
                here = span(base + outer, WIDTH)
                queries = steps_of(query_ref, take)
                local = steps_of(local_ref, take)
                for j in range(2):
                    local[j] = local[j] + jnp.where(first_mask(), wide(fix_ref[j : j + 1, here]), 0.0)
                    queries[j] = queries[j] + jnp.where(first_mask(), wide(fix_ref[2 + j : 3 + j, here]), 0.0)
                coefs = []
                for pole in range(POLES):
                    lam = pole_at(power_ref, LAM, pole, here)
                    back = pole_at(power_ref, BACK, pole, here)
                    state = times(pole_at(state_ref, 0, pole, here), (reach_ref[pole, :, take], reach_ref[2 + pole, :, take]))
                    y2 = state[0] * back[0] - state[1] * back[1]
                    coefs.append([*feedback(lam), state[0], y2])
                gated = []
                for j in range(len(queries)):
                    total = local[j]
                    for pole in range(POLES):
                        a1, a2, y1, y2 = coefs[pole]
                        y = a1 * y1 - a2 * y2
                        coefs[pole][2:] = [y, y1]
                        total = total + y
                    gated.append(queries[j] * total)
                    if j % 2:
                        both = jnp.concatenate(gated[-2:], axis=0)
                        gated_ref[SEGMENTS * (j - 1) : SEGMENTS * (j + 1), cols] = both.astype(bf16)

            loop_columns(i, chunk, column)
            out_ref[:, span(base + i * chunk, chunk)] = jnp.dot(
                order_ref[...], gated_ref[...], preferred_element_type=f32).astype(bf16)
            send(base // chunk + i).start()
            return 0

        lax.fori_loop(0, part // chunk, body, 0)
        base += part
    for i in range(count):
        send(i).wait()


def kernel_call(body, name, outs, scratch, operands, in_hbm, out_hbm=(), **options):
    def spec(far):
        return pl.BlockSpec(memory_space=pltpu.HBM if far else pltpu.VMEM)

    def bound(*refs):
        return body(*refs, **options)

    return pl.pallas_call(
        bound,
        in_specs=[spec(i in in_hbm) for i in range(len(operands))],
        out_specs=[spec(i in out_hbm) for i in range(len(outs))],
        out_shape=[jax.ShapeDtypeStruct(shape, dtype) for shape, dtype in outs],
        scratch_shapes=scratch,
        compiler_params=pltpu.CompilerParams(vmem_limit_bytes=32 << 20),
        name=name,
    )(*operands)


def on_device(projected, short_taps, skip_gain, residues, pole_angles, decay_rates):
    _, rows, channels = projected.shape
    chunk = min(CHUNK, channels)
    devices = lax.axis_size("seq")
    levels = devices.bit_length() - 1
    parts = [channels // sum(PARTS) * share for share in PARTS]
    arguments = [pole_angles, decay_rates, short_taps, residues, skip_gain[None], projected]
    arguments = [pltpu.with_memory_space_constraint(argument, pltpu.HBM) for argument in arguments]
    projected = arguments[-1]
    state = ((4, channels), f32)
    wire = ((4, channels), bf16)
    square = pltpu.VMEM((rows, rows), bf16)
    dma = pltpu.SemaphoreType.DMA

    products, scan, total, edges, tail, powers, taps, gains, skip = kernel_call(
        states_kernel, "states",
        [((rows, channels), bf16), ((4, SEGMENTS, channels), f32), state, ((10, channels), bf16),
         ((6, channels), bf16), ((4 * (SPAN + levels), channels), f32), (short_taps.shape, f32),
         (residues.shape, f32), ((1, channels), f32)],
        [square] + [pltpu.VMEM(pole_angles.shape, f32)] * 2 + [pltpu.VMEM((rows, channels), bf16)] * 2
        + [pltpu.VMEM((2, SUBROWS, channels), bf16), pltpu.VMEM((3, SUBROWS, channels), bf16)]
        + [pltpu.VMEM((rows, chunk), f32)] * 2 + [dma((7,)), dma((2, channels // chunk))],
        arguments, range(6), levels=levels)

    def move(array, pairs):
        return lax.ppermute(array, "seq", [(a, b) for a, b in pairs if b < devices])

    def exchange(array, level):
        return move(array, [(i, i ^ (1 << level)) for i in range(devices)])

    tails_even = move(tail, [(i, i + 1) for i in range(1, devices, 2)])
    tails_odd = move(tail, [(i, i + 2) for i in range(1, devices, 2)])
    mate_edges = exchange(edges, 0)
    mate_total = exchange(total, 0)
    ending, sent, lead, enter, fix = kernel_call(
        merge_kernel, "merge", [state, wire, state, state, state], [],
        [total, mate_total, edges, mate_edges, tails_even, tails_odd, powers, taps, gains, skip], ())

    tables = []
    base = 0
    for level in range(1, levels):
        got = exchange(sent, level)
        while len(tables) < len(parts) and (len(tables) < level or level == levels - 1):
            part = parts[len(tables)]
            plane = ((rows, part), f32)
            tables.append(kernel_call(
                local_kernel, "local", [plane, plane, ((4, SEGMENTS, part), f32)],
                [square, pltpu.VMEM((rows, part), bf16), pltpu.VMEM((rows, chunk), f32), dma((part // chunk,))],
                [taps, gains, skip, powers, scan, products, projected, ending], (6,), base=base))
            base += part
        if level + 1 < levels:
            ending, sent, lead, enter = kernel_call(
                join_kernel, "join", [state, wire, state, state], [], [ending, got, powers, lead, enter], (),
                level=level)

    (out,) = kernel_call(
        gate_kernel, "gate", [((rows, channels), bf16)],
        [square, pltpu.VMEM((rows, channels), bf16), pltpu.VMEM((rows, chunk), bf16),
         pltpu.VMEM((4, channels), f32), dma((channels // chunk,))],
        [powers, got, lead, enter, fix, *[array for table in tables for array in table]], (), (0,),
        level=levels - 1, parts=parts)
    return out


def solution(mesh):
    return jax.shard_map(
        on_device,
        mesh=mesh,
        in_specs=(P(None, ("grp", "seq"), None), P(), P(), P(), P(), P()),
        out_specs=P(("grp", "seq"), None),
        check_vma=False,
    )
```

```python
import jax
import jax.numpy as jnp
from jax import lax
from jax.experimental import pallas as pl
from jax.experimental.pallas import tpu as pltpu
from jax.sharding import PartitionSpec as P

SEGMENTS = 8
WIDTH = 256
CHUNK = 512
POLES = 2
SUBROWS = 16
PARTS = (1, 1, 2)
f32 = jnp.float32
bf16 = jnp.bfloat16

LAM, BACK, SEGMENT, SPAN = 0, 1, 2, 5


def order_matrix(row_count, inverse):
    length = row_count // SEGMENTS
    ordered = lax.broadcasted_iota(jnp.int32, (row_count, row_count), 1 if inverse else 0)
    natural = lax.broadcasted_iota(jnp.int32, (row_count, row_count), 0 if inverse else 1)
    wanted = length * (ordered % SEGMENTS) + ordered // SEGMENTS
    return (wanted == natural).astype(f32).astype(bf16)


def wide(value):
    return jnp.broadcast_to(value, (SEGMENTS, value.shape[1]))


def times(a, b):
    return (a[0] * b[0] - a[1] * b[1], a[0] * b[1] + a[1] * b[0])


def plus(a, b):
    return (a[0] + b[0], a[1] + b[1])


def pair_at(ref, index, cols):
    return (ref[4 * index : 4 * index + 2, cols], ref[4 * index + 2 : 4 * index + 4, cols])


def put_pair(ref, index, cols, value):
    ref[4 * index : 4 * index + 2, cols] = value[0]
    ref[4 * index + 2 : 4 * index + 4, cols] = value[1]


def pole_at(ref, index, pole, cols):
    return (wide(ref[pl.ds(4 * index + pole, 1), cols]), wide(ref[pl.ds(4 * index + 2 + pole, 1), cols]))


def half_angle(angle):
    x = 0.5 * angle
    u = x * x
    sine = 1.0 / 6227020800.0
    for term in (-1.0 / 39916800.0, 1.0 / 362880.0, -1.0 / 5040.0, 1.0 / 120.0, -1.0 / 6.0, 1.0):
        sine = sine * u + term
    cosine = -1.0 / 87178291200.0
    for term in (1.0 / 479001600.0, -1.0 / 3628800.0, 1.0 / 40320.0, -1.0 / 720.0, 1.0 / 24.0, -0.5, 1.0):
        cosine = cosine * u + term
    return cosine, sine * x


def fill_powers(power_ref, angle_ref, decay_ref, length, levels):
    cols = slice(None)
    cosine, sine = half_angle(angle_ref[...])
    turn = (1.0 - 2.0 * sine * sine, 2.0 * sine * cosine)
    decay = decay_ref[...]
    damping = jnp.exp(-decay)
    growth = jnp.exp(decay)
    value = (damping * turn[0], damping * turn[1])
    put_pair(power_ref, LAM, cols, value)
    put_pair(power_ref, BACK, cols, (growth * turn[0], -growth * turn[1]))
    for _ in range(length.bit_length() - 1):
        value = times(value, value)
    for level in range(3 + levels):
        put_pair(power_ref, SEGMENT + level, cols, value)
        value = times(value, value)


def steps_of(ref, cols):
    return [ref[SEGMENTS * j : SEGMENTS * (j + 1), cols] for j in range(ref.shape[0] // SEGMENTS)]


def first_mask():
    return lax.broadcasted_iota(jnp.int32, (SEGMENTS, WIDTH), 0) == 0


def delayed(value):
    return jnp.where(first_mask(), 0.0, pltpu.roll(value, 1, 0))


def short_filter(steps, taps_ref, which, cols):
    taps = [wide(taps_ref[tap, which : which + 1, cols]) for tap in range(3)]
    padded = [delayed(steps[-2]), delayed(steps[-1])] + steps
    return [
        taps[0] * padded[j] + taps[1] * padded[j + 1] + taps[2] * padded[j + 2]
        for j in range(len(steps))
    ]


def feedback(lam):
    return 2.0 * lam[0], lam[0] * lam[0] + lam[1] * lam[1]


def span(start, size):
    return pl.ds(pl.multiple_of(start, 128), size)


def loop_columns(chunk_index, chunk, body):
    for part in range(chunk // WIDTH):
        body(part * WIDTH, chunk_index * chunk + part * WIDTH)


def states_kernel(angle_hbm, decay_hbm, taps_hbm, gain_hbm, skip_hbm, proj_ref,
                  prod_ref, scan_ref, keep_total, give_total, keep_edge, give_edge, power_ref, taps_ref, gain_ref, skip_ref,
                  total_ref, edge_ref, order_ref, angle_ref, decay_ref, k_ref, v_ref, top_ref, end_ref, ks_ref, vs_ref,
                  small_sem, in_sem, *, levels):
    rows, channels = k_ref.shape
    chunk = ks_ref.shape[1]
    count = channels // chunk
    last = rows - SUBROWS
    smalls = [
        pltpu.make_async_copy(source, target, small_sem.at[i])
        for i, (source, target) in enumerate([
            (angle_hbm, angle_ref), (decay_hbm, decay_ref), (taps_hbm, taps_ref), (gain_hbm, gain_ref),
            (skip_hbm, skip_ref), (proj_ref.at[pl.ds(1, 2), pl.ds(0, SUBROWS)], top_ref),
            (proj_ref.at[:, pl.ds(last, SUBROWS)], end_ref)])
    ]

    def fetch(i, which, ref):
        cols = span(i * chunk, chunk)
        return pltpu.make_async_copy(proj_ref.at[which, :, cols], ref.at[:, cols], in_sem.at[which - 1, i])

    for copy in smalls[:3]:
        copy.start()
    for i in range(count):
        fetch(i, 1, k_ref).start()
        fetch(i, 2, v_ref).start()
    for copy in smalls[3:]:
        copy.start()
    order_ref[...] = order_matrix(rows, False)
    for copy in smalls[:3]:
        copy.wait()
    fill_powers(power_ref, angle_ref, decay_ref, rows // SEGMENTS, levels)

    def body(i, _):
        fetch(i, 1, k_ref).wait()
        fetch(i, 2, v_ref).wait()
        at = span(i * chunk, chunk)
        ks_ref[...] = jnp.dot(order_ref[...], k_ref[:, at], preferred_element_type=f32)
        vs_ref[...] = jnp.dot(order_ref[...], v_ref[:, at], preferred_element_type=f32)

        def column(inner, outer):
            cols = slice(inner, inner + WIDTH)
            here = span(outer, WIDTH)
            keys = short_filter(steps_of(ks_ref, cols), taps_ref, 1, here)
            values = short_filter(steps_of(vs_ref, cols), taps_ref, 2, here)
            products = [a * b for a, b in zip(keys, values)]
            for j in range(2):
                products[j] = jnp.where(first_mask(), 0.0, products[j])
            for j in range(0, len(products), 2):
                both = jnp.concatenate(products[j : j + 2], axis=0)
                prod_ref[SEGMENTS * j : SEGMENTS * (j + 2), here] = both.astype(bf16)
            sublane = lax.broadcasted_iota(jnp.int32, (SEGMENTS, WIDTH), 0)
            for pole in range(POLES):
                lam = pole_at(power_ref, LAM, pole, here)
                a1, a2 = feedback(lam)
                late = products[0]
                now = a1 * late + products[1]
                for value in products[2:]:
                    late, now = now, a1 * now - a2 * late + value
                state = (now - lam[0] * late, lam[1] * late)
                for level in range(3):
                    by = 1 << level
                    factor = pole_at(power_ref, SEGMENT + level, pole, here)
                    moved = tuple(jnp.where(sublane >= by, pltpu.roll(part, by, 0), 0.0) for part in state)
                    state = plus(state, times(factor, moved))
                for part in range(2):
                    scan_ref[2 * part + pole, :, here] = state[part]
                    total_ref[2 * part + pole : 2 * part + pole + 1, here] = state[part][SEGMENTS - 1 :]

        loop_columns(i, chunk, column)
        return 0

    lax.fori_loop(0, count, body, 0)
    for copy in smalls[3:]:
        copy.wait()
    for which in range(3):
        edge_ref[2 * which : 2 * which + 2] = end_ref[which, SUBROWS - 2 : SUBROWS]
    for which in range(2):
        edge_ref[6 + 2 * which : 8 + 2 * which] = top_ref[which, 0:2]
    own, other = halves(channels)
    keep_total[...] = total_ref[:, own]
    give_total[...] = total_ref[:, other]
    keep_edge[...] = edge_ref[:, own]
    give_edge[...] = edge_ref[:, other]


def halves(channels):
    half = channels // 2
    odd = lax.axis_index("seq") % 2
    return span(odd * half, half), span((1 - odd) * half, half)


def first_products(tail, heads, taps):
    def filtered(which, at):
        sequence = [tail[2 * which : 2 * which + 1], tail[2 * which + 1 : 2 * which + 2],
                    heads[2 * which - 2 : 2 * which - 1], heads[2 * which - 1 : 2 * which]]
        return sum(taps[tap, which : which + 1] * sequence[at + tap] for tap in range(3))

    return [filtered(1, at) * filtered(2, at) for at in range(2)]


def extra_state(products, back):
    first, second = products
    return times(back, (second * back[0] + first, second * back[1]))


def fixed_rows(products, tail, taps, skip, gain, back):
    first, second = products
    jump = sum(gain[0, pole : pole + 1] * back[0][pole : pole + 1] - gain[1, pole : pole + 1] * back[1][pole : pole + 1]
               for pole in range(POLES))
    return [skip * first - jump * second, skip * second,
            taps[0, 0:1] * tail[0:1] + taps[1, 0:1] * tail[1:2], taps[0, 0:1] * tail[1:2]]


def pick(condition, a, b):
    return tuple(jnp.where(condition, x, y) for x, y in zip(a, b))


def put_wire(wire_ref, value):
    for part in range(2):
        total = value[part][0:1] + value[part][1:2]
        difference = value[part][0:1] - value[part][1:2]
        wire_ref[2 * part : 2 * part + 2] = jnp.concatenate([total, difference], axis=0).astype(bf16)


def from_wire(wire_ref):
    value = []
    for part in range(2):
        both = wire_ref[2 * part : 2 * part + 2].astype(f32)
        total, difference = both[0:1], both[1:2]
        value.append(0.5 * jnp.concatenate([total + difference, total - difference], axis=0))
    return tuple(value)


ALL = slice(None)


def merge_kernel(total_ref, mate_ref, edge_ref, mate_edge_ref, power_ref, taps_ref, gain_ref, skip_ref,
                 joined_ref, wire_ref, lead_ref, enter_ref, base_ref, fix_ref, head_ref, *, channels):
    device = lax.axis_index("seq")
    odd = device % 2 == 1
    half = halves(channels)[0]
    taps, gain, skip = taps_ref[:, :, half], gain_ref[:, :, half], skip_ref[:, half]
    power, back = pair_at(power_ref, SPAN, half), pair_at(power_ref, BACK, half)
    mine, mates = edge_ref[...].astype(f32), mate_edge_ref[...].astype(f32)
    even_edge, odd_edge = jnp.where(odd, mates, mine), jnp.where(odd, mine, mates)
    own, mate = pair_at(total_ref, 0, ALL), pair_at(mate_ref, 0, ALL)
    even_total, odd_total = pick(odd, mate, own), pick(odd, own, mate)
    products = first_products(even_edge[0:6], odd_edge[6:10], taps)
    base = plus(even_total, extra_state(products, back))
    put_pair(base_ref, 0, ALL, base)
    for i, value in enumerate(fixed_rows(products, even_edge[0:6], taps, skip, gain, back)):
        fix_ref[i : i + 1] = value
    start = extra_state(first_products(jnp.zeros_like(even_edge[0:6]), even_edge[6:10], taps), back)
    enter = tuple(jnp.where(device < 2, part, 0.0) for part in start)
    put_pair(enter_ref, 0, ALL, enter)
    joined = plus(odd_total, times(power, plus(base, times(power, enter))))
    put_pair(joined_ref, 0, ALL, joined)
    put_pair(lead_ref, 0, ALL, (jnp.ones_like(power[0]), jnp.zeros_like(power[0])))
    put_wire(wire_ref, joined)
    wire_ref[4:10] = odd_edge[0:6].astype(bf16)
    wire_ref[10:14] = even_edge[6:10].astype(bf16)
    head_ref[...] = even_edge[6:10].astype(bf16)


def step_of(level, sent_ref, got_ref, power_ref, taps_ref, lead_ref, enter_ref, tail_before, half):
    device = lax.axis_index("seq")
    upper = (device >> level) % 2 == 1
    leads = jnp.logical_and(upper, (device % (1 << level)) < 2)
    back = pair_at(power_ref, BACK, half)
    early_tail = jnp.where(upper, got_ref[4:10].astype(f32), sent_ref[4:10].astype(f32))
    late_head = sent_ref[10:14].astype(f32)
    if got_ref.shape[0] > 10:
        late_head = jnp.where(upper, late_head, got_ref[10:14].astype(f32))
    extra = extra_state(first_products(early_tail, late_head, taps_ref[:, :, half]), back)
    other = from_wire(got_ref)
    lead, enter = pair_at(lead_ref, 0, ALL), pair_at(enter_ref, 0, ALL)
    enter = pick(upper, plus(enter, times(lead, plus(other, extra))), enter)
    return upper, other, extra, lead, enter, jnp.where(leads, early_tail, tail_before)


def join_kernel(ending_ref, sent_ref, got_ref, power_ref, taps_ref, lead_ref, enter_ref, before_ref,
                joined_ref, wire_ref, next_lead_ref, next_enter_ref, next_before_ref, *, level, channels):
    half = halves(channels)[0]
    upper, other, extra, lead, enter, before = step_of(
        level, sent_ref, got_ref, power_ref, taps_ref, lead_ref, enter_ref, before_ref[...].astype(f32), half)
    factor = pair_at(power_ref, SPAN + level, half)
    mine = pair_at(ending_ref, 0, ALL)
    early, late = pick(upper, other, mine), pick(upper, mine, other)
    joined = plus(times(factor, plus(early, extra)), late)
    put_pair(joined_ref, 0, ALL, joined)
    put_wire(wire_ref, joined)
    got, sent = got_ref[...].astype(f32), sent_ref[...].astype(f32)
    wire_ref[4:10] = jnp.where(upper, sent[4:10], got[4:10]).astype(bf16)
    wire_ref[10:14] = jnp.where(upper, got[10:14], sent[10:14]).astype(bf16)
    put_pair(next_lead_ref, 0, ALL, pick(upper, times(lead, factor), lead))
    put_pair(next_enter_ref, 0, ALL, enter)
    next_before_ref[...] = before.astype(bf16)


def last_kernel(sent_ref, got_ref, power_ref, taps_ref, gain_ref, skip_ref, lead_ref, enter_ref, before_ref,
                base_ref, fix_ref, head_ref, keep_ref, give_ref, *, level, channels):
    half = halves(channels)[0]
    odd = lax.axis_index("seq") % 2 == 1
    _, _, _, _, enter, before = step_of(
        level, sent_ref, got_ref, power_ref, taps_ref, lead_ref, enter_ref, before_ref[...].astype(f32), half)
    taps, gain, skip = taps_ref[:, :, half], gain_ref[:, :, half], skip_ref[:, half]
    power, back = pair_at(power_ref, SPAN, half), pair_at(power_ref, BACK, half)
    products = first_products(before, head_ref[...].astype(f32), taps)
    even = [*enter, *fixed_rows(products, before, taps, skip, gain, back)]
    odds = [*plus(times(power, enter), pair_at(base_ref, 0, ALL)), *(fix_ref[i : i + 1] for i in range(4))]
    row = 0
    for a, b in zip(even, odds):
        keep_ref[row : row + a.shape[0]] = jnp.where(odd, b, a)
        give_ref[row : row + a.shape[0]] = jnp.where(odd, a, b)
        row += a.shape[0]


def local_kernel(taps_ref, gain_ref, skip_ref, power_ref, scan_ref, prod_ref, proj_ref, after_ref,
                 query_ref, local_ref, enter_ref, order_ref, q_ref, qs_ref, in_sem, *, base):
    rows, channels = q_ref.shape
    chunk = qs_ref.shape[1]
    count = channels // chunk

    def fetch(i):
        return pltpu.make_async_copy(
            proj_ref.at[0, :, span(base + i * chunk, chunk)], q_ref.at[:, span(i * chunk, chunk)], in_sem.at[i])

    for i in range(count):
        fetch(i).start()
    order_ref[...] = order_matrix(rows, False)

    def body(i, _):
        fetch(i).wait()
        qs_ref[...] = jnp.dot(order_ref[...], q_ref[:, span(i * chunk, chunk)], preferred_element_type=f32)

        def column(inner, outer):
            cols = slice(inner, inner + WIDTH)
            put = span(outer, WIDTH)
            here = span(base + outer, WIDTH)
            queries = short_filter(steps_of(qs_ref, cols), taps_ref, 0, here)
            for j, value in enumerate(queries):
                query_ref[SEGMENTS * j : SEGMENTS * (j + 1), put] = value
            products = []
            for j in range(0, len(queries), 2):
                both = prod_ref[SEGMENTS * j : SEGMENTS * (j + 2), here].astype(f32)
                products += [both[:SEGMENTS], both[SEGMENTS:]]
            before = delayed(products[-1])
            skip = wide(skip_ref[0:1, here])
            sublane = lax.broadcasted_iota(jnp.int32, (SEGMENTS, WIDTH), 0)
            coefs = []
            for pole in range(POLES):
                lam = pole_at(power_ref, LAM, pole, here)
                back = pole_at(power_ref, BACK, pole, here)
                gain = tuple(wide(gain_ref[part, pole : pole + 1, here]) for part in range(2))
                a1, a2 = feedback(lam)
                b1 = gain[0] * lam[0] + gain[1] * lam[1]
                carry = tuple(delayed(scan_ref[2 * part + pole, :, here]) for part in range(2))
                gain_back = times(gain, back)
                y1 = gain[0] * carry[0] - gain[1] * carry[1]
                y2 = gain_back[0] * (carry[0] - before) - gain_back[1] * carry[1]
                coefs.append([a1, a2, gain[0], b1, y1, y2])
                reach = gain
                for level in range(3):
                    factor = pole_at(power_ref, SEGMENT + level, pole, here)
                    bit = (sublane // (1 << level)) % 2 == 1
                    reach = times(reach, (jnp.where(bit, factor[0], 1.0), jnp.where(bit, factor[1], 0.0)))
                for part in range(2):
                    enter_ref[2 * part + pole, :, put] = reach[part]
            previous = before
            for j, value in enumerate(products):
                total = skip * value
                for pole in range(POLES):
                    a1, a2, b0, b1, y1, y2 = coefs[pole]
                    y = a1 * y1 - a2 * y2 + (b0 * value - b1 * previous)
                    coefs[pole][4:] = [y, y1]
                    total = total + y
                previous = value
                local_ref[SEGMENTS * j : SEGMENTS * (j + 1), put] = total

        loop_columns(i, chunk, column)
        return 0

    lax.fori_loop(0, count, body, 0)


def gate_kernel(power_ref, keep_ref, got_ref, *rest, parts):
    tables = [rest[3 * i : 3 * i + 3] for i in range(len(parts))]
    out_hbm, order_ref, out_ref, gated_ref, state_ref, out_sem = rest[3 * len(parts) :]
    rows, channels = out_ref.shape
    chunk = gated_ref.shape[1]
    count = channels // chunk
    own, other = halves(channels)
    state_ref[:, own] = keep_ref[...]
    state_ref[:, other] = got_ref[...]
    order_ref[...] = order_matrix(rows, True)

    def send(i):
        place = span(i * chunk, chunk)
        return pltpu.make_async_copy(out_ref.at[:, place], out_hbm.at[:, place], out_sem.at[i])

    base = 0
    for part, (query_ref, local_ref, reach_ref) in zip(parts, tables):

        def body(i, _, base=base, query_ref=query_ref, local_ref=local_ref, reach_ref=reach_ref):
            def column(inner, outer):
                cols = slice(inner, inner + WIDTH)
                take = span(outer, WIDTH)
                here = span(base + outer, WIDTH)
                queries = steps_of(query_ref, take)
                local = steps_of(local_ref, take)
                for j in range(2):
                    local[j] = local[j] + jnp.where(first_mask(), wide(state_ref[4 + j : 5 + j, here]), 0.0)
                    queries[j] = queries[j] + jnp.where(first_mask(), wide(state_ref[6 + j : 7 + j, here]), 0.0)
                coefs = []
                for pole in range(POLES):
                    lam = pole_at(power_ref, LAM, pole, here)
                    back = pole_at(power_ref, BACK, pole, here)
                    state = times(pole_at(state_ref, 0, pole, here), (reach_ref[pole, :, take], reach_ref[2 + pole, :, take]))
                    y2 = state[0] * back[0] - state[1] * back[1]
                    coefs.append([*feedback(lam), state[0], y2])
                gated = []
                for j in range(len(queries)):
                    total = local[j]
                    for pole in range(POLES):
                        a1, a2, y1, y2 = coefs[pole]
                        y = a1 * y1 - a2 * y2
                        coefs[pole][2:] = [y, y1]
                        total = total + y
                    gated.append(queries[j] * total)
                    if j % 2:
                        both = jnp.concatenate(gated[-2:], axis=0)
                        gated_ref[SEGMENTS * (j - 1) : SEGMENTS * (j + 1), cols] = both.astype(bf16)

            loop_columns(i, chunk, column)
            out_ref[:, span(base + i * chunk, chunk)] = jnp.dot(
                order_ref[...], gated_ref[...], preferred_element_type=f32).astype(bf16)
            send(base // chunk + i).start()
            return 0

        lax.fori_loop(0, part // chunk, body, 0)
        base += part
    for i in range(count):
        send(i).wait()


def kernel_call(body, name, outs, scratch, operands, in_hbm, out_hbm=(), **options):
    def spec(far):
        return pl.BlockSpec(memory_space=pltpu.HBM if far else pltpu.VMEM)

    def bound(*refs):
        return body(*refs, **options)

    return pl.pallas_call(
        bound,
        in_specs=[spec(i in in_hbm) for i in range(len(operands))],
        out_specs=[spec(i in out_hbm) for i in range(len(outs))],
        out_shape=[jax.ShapeDtypeStruct(shape, dtype) for shape, dtype in outs],
        scratch_shapes=scratch,
        compiler_params=pltpu.CompilerParams(vmem_limit_bytes=32 << 20),
        name=name,
    )(*operands)


def on_device(projected, short_taps, skip_gain, residues, pole_angles, decay_rates):
    _, rows, channels = projected.shape
    chunk = min(CHUNK, channels)
    devices = lax.axis_size("seq")
    levels = devices.bit_length() - 1
    parts = [channels // sum(PARTS) * share for share in PARTS]
    arguments = [pole_angles, decay_rates, short_taps, residues, skip_gain[None], projected]
    arguments = [pltpu.with_memory_space_constraint(argument, pltpu.HBM) for argument in arguments]
    projected = arguments[-1]
    half = channels // 2
    state = ((4, half), f32)
    square = pltpu.VMEM((rows, rows), bf16)
    dma = pltpu.SemaphoreType.DMA

    products, scan, total, give_total, edge, give_edge, powers, taps, gains, skip = kernel_call(
        states_kernel, "states",
        [((rows, channels), bf16), ((4, SEGMENTS, channels), f32), state, state, ((10, half), bf16), ((10, half), bf16),
         ((4 * (SPAN + levels), channels), f32), (short_taps.shape, f32), (residues.shape, f32), ((1, channels), f32)],
        [pltpu.VMEM((4, channels), f32), pltpu.VMEM((10, channels), bf16), square]
        + [pltpu.VMEM(pole_angles.shape, f32)] * 2 + [pltpu.VMEM((rows, channels), bf16)] * 2
        + [pltpu.VMEM((2, SUBROWS, channels), bf16), pltpu.VMEM((3, SUBROWS, channels), bf16)]
        + [pltpu.VMEM((rows, chunk), f32)] * 2 + [dma((7,)), dma((2, channels // chunk))],
        arguments, range(6), levels=levels)

    def exchange(array, level):
        return lax.ppermute(array, "seq", [(i, i ^ (1 << level)) for i in range(devices)])

    mate_edge = exchange(give_edge, 0)
    mate_total = exchange(give_total, 0)
    ending, sent, lead, enter, base, fix, head = kernel_call(
        merge_kernel, "merge", [state, ((14, half), bf16), state, state, state, state, ((4, half), bf16)], [],
        [total, mate_total, edge, mate_edge, powers, taps, gains, skip], (), channels=channels)
    before = jnp.zeros((6, half), bf16)

    tables = []
    start = 0
    for level in range(1, levels):
        got = exchange(sent, level)
        while len(tables) < len(parts) and (len(tables) < level or level == levels - 1):
            part = parts[len(tables)]
            plane = ((rows, part), f32)
            tables.append(kernel_call(
                local_kernel, "local", [plane, plane, ((4, SEGMENTS, part), f32)],
                [square, pltpu.VMEM((rows, part), bf16), pltpu.VMEM((rows, chunk), f32), dma((part // chunk,))],
                [taps, gains, skip, powers, scan, products, projected, ending], (6,), base=start))
            start += part
        if level + 1 < levels:
            ending, sent, lead, enter, before = kernel_call(
                join_kernel, "join", [state, ((14, half), bf16), state, state, ((6, half), bf16)], [],
                [ending, sent, got, powers, taps, lead, enter, before], (), level=level, channels=channels)

    keep, give = kernel_call(
        last_kernel, "last", [((8, half), f32)] * 2, [],
        [sent, got, powers, taps, gains, skip, lead, enter, before, base, fix, head], (),
        level=levels - 1, channels=channels)
    got = exchange(give, 0)

    (out,) = kernel_call(
        gate_kernel, "gate", [((rows, channels), bf16)],
        [square, pltpu.VMEM((rows, channels), bf16), pltpu.VMEM((rows, chunk), bf16),
         pltpu.VMEM((8, channels), f32), dma((channels // chunk,))],
        [powers, keep, got, *[array for table in tables for array in table]], (), (0,), parts=parts)
    return out


def solution(mesh):
    return jax.shard_map(
        on_device,
        mesh=mesh,
        in_specs=(P(None, ("grp", "seq"), None), P(), P(), P(), P(), P()),
        out_specs=P(("grp", "seq"), None),
        check_vma=False,
    )
```

```python
import jax
import jax.numpy as jnp
from jax import lax
from jax.experimental import pallas as pl
from jax.experimental.pallas import tpu as pltpu
from jax.sharding import PartitionSpec as P

SEGMENTS = 8
WIDTH = 256
CHUNK = 512
POLES = 2
SUBROWS = 16
PARTS = (3, 3, 2)
f32 = jnp.float32
bf16 = jnp.bfloat16

LAM, BACK, SEGMENT, SPAN = 0, 1, 2, 5


def order_matrix(row_count, inverse):
    length = row_count // SEGMENTS
    ordered = lax.broadcasted_iota(jnp.int32, (row_count, row_count), 1 if inverse else 0)
    natural = lax.broadcasted_iota(jnp.int32, (row_count, row_count), 0 if inverse else 1)
    wanted = length * (ordered % SEGMENTS) + ordered // SEGMENTS
    return (wanted == natural).astype(f32).astype(bf16)


def wide(value):
    return jnp.broadcast_to(value, (SEGMENTS, value.shape[1]))


def times(a, b):
    return (a[0] * b[0] - a[1] * b[1], a[0] * b[1] + a[1] * b[0])


def plus(a, b):
    return (a[0] + b[0], a[1] + b[1])


def pair_at(ref, index, cols):
    return (ref[4 * index : 4 * index + 2, cols], ref[4 * index + 2 : 4 * index + 4, cols])


def put_pair(ref, index, cols, value):
    ref[4 * index : 4 * index + 2, cols] = value[0]
    ref[4 * index + 2 : 4 * index + 4, cols] = value[1]


def pole_at(ref, index, pole, cols):
    return (wide(ref[pl.ds(4 * index + pole, 1), cols]), wide(ref[pl.ds(4 * index + 2 + pole, 1), cols]))


def half_angle(angle):
    x = 0.5 * angle
    u = x * x
    sine = 1.0 / 6227020800.0
    for term in (-1.0 / 39916800.0, 1.0 / 362880.0, -1.0 / 5040.0, 1.0 / 120.0, -1.0 / 6.0, 1.0):
        sine = sine * u + term
    cosine = -1.0 / 87178291200.0
    for term in (1.0 / 479001600.0, -1.0 / 3628800.0, 1.0 / 40320.0, -1.0 / 720.0, 1.0 / 24.0, -0.5, 1.0):
        cosine = cosine * u + term
    return cosine, sine * x


def fill_powers(power_ref, angle_ref, decay_ref, length, levels):
    cols = slice(None)
    cosine, sine = half_angle(angle_ref[...])
    turn = (1.0 - 2.0 * sine * sine, 2.0 * sine * cosine)
    decay = decay_ref[...]
    damping = jnp.exp(-decay)
    growth = jnp.exp(decay)
    value = (damping * turn[0], damping * turn[1])
    put_pair(power_ref, LAM, cols, value)
    put_pair(power_ref, BACK, cols, (growth * turn[0], -growth * turn[1]))
    for _ in range(length.bit_length() - 1):
        value = times(value, value)
    for level in range(3 + levels):
        put_pair(power_ref, SEGMENT + level, cols, value)
        value = times(value, value)


def steps_of(ref, cols):
    return [ref[SEGMENTS * j : SEGMENTS * (j + 1), cols] for j in range(ref.shape[0] // SEGMENTS)]


def first_mask():
    return lax.broadcasted_iota(jnp.int32, (SEGMENTS, WIDTH), 0) == 0


def delayed(value):
    return jnp.where(first_mask(), 0.0, pltpu.roll(value, 1, 0))


def short_filter(steps, taps_ref, which, cols):
    taps = [wide(taps_ref[tap, which : which + 1, cols]) for tap in range(3)]
    padded = [delayed(steps[-2]), delayed(steps[-1])] + steps
    return [
        taps[0] * padded[j] + taps[1] * padded[j + 1] + taps[2] * padded[j + 2]
        for j in range(len(steps))
    ]


def feedback(lam):
    return 2.0 * lam[0], lam[0] * lam[0] + lam[1] * lam[1]


def span(start, size):
    return pl.ds(pl.multiple_of(start, 128), size)


def loop_columns(chunk_index, chunk, body):
    for part in range(chunk // WIDTH):
        body(part * WIDTH, chunk_index * chunk + part * WIDTH)


def states_kernel(angle_hbm, decay_hbm, taps_hbm, gain_hbm, skip_hbm, proj_ref,
                  prod_ref, scan_ref, keep_total, give_total, keep_edge, give_edge, power_ref, taps_ref, gain_ref, skip_ref,
                  q_ref, total_ref, edge_ref, order_ref, angle_ref, decay_ref, k_ref, v_ref, top_ref, end_ref, ks_ref, vs_ref,
                  small_sem, in_sem, *, levels):
    rows, channels = k_ref.shape
    chunk = ks_ref.shape[1]
    count = channels // chunk
    last = rows - SUBROWS
    smalls = [
        pltpu.make_async_copy(source, target, small_sem.at[i])
        for i, (source, target) in enumerate([
            (angle_hbm, angle_ref), (decay_hbm, decay_ref), (taps_hbm, taps_ref), (gain_hbm, gain_ref),
            (skip_hbm, skip_ref), (proj_ref.at[pl.ds(1, 2), pl.ds(0, SUBROWS)], top_ref),
            (proj_ref.at[:, pl.ds(last, SUBROWS)], end_ref), (proj_ref.at[0], q_ref)])
    ]

    def fetch(i, which, ref):
        cols = span(i * chunk, chunk)
        return pltpu.make_async_copy(proj_ref.at[which, :, cols], ref.at[:, cols], in_sem.at[which - 1, i])

    for copy in smalls[:3]:
        copy.start()
    for i in range(count):
        fetch(i, 1, k_ref).start()
        fetch(i, 2, v_ref).start()
    for copy in smalls[3:]:
        copy.start()
    order_ref[...] = order_matrix(rows, False)
    for copy in smalls[:3]:
        copy.wait()
    fill_powers(power_ref, angle_ref, decay_ref, rows // SEGMENTS, levels)

    def body(i, _):
        fetch(i, 1, k_ref).wait()
        fetch(i, 2, v_ref).wait()
        at = span(i * chunk, chunk)
        ks_ref[...] = jnp.dot(order_ref[...], k_ref[:, at], preferred_element_type=f32)
        vs_ref[...] = jnp.dot(order_ref[...], v_ref[:, at], preferred_element_type=f32)

        def column(inner, outer):
            cols = slice(inner, inner + WIDTH)
            here = span(outer, WIDTH)
            keys = short_filter(steps_of(ks_ref, cols), taps_ref, 1, here)
            values = short_filter(steps_of(vs_ref, cols), taps_ref, 2, here)
            products = [a * b for a, b in zip(keys, values)]
            for j in range(2):
                products[j] = jnp.where(first_mask(), 0.0, products[j])
            for j in range(0, len(products), 2):
                both = jnp.concatenate(products[j : j + 2], axis=0)
                prod_ref[SEGMENTS * j : SEGMENTS * (j + 2), here] = both.astype(bf16)
            sublane = lax.broadcasted_iota(jnp.int32, (SEGMENTS, WIDTH), 0)
            for pole in range(POLES):
                lam = pole_at(power_ref, LAM, pole, here)
                a1, a2 = feedback(lam)
                late = products[0]
                now = a1 * late + products[1]
                for value in products[2:]:
                    late, now = now, a1 * now - a2 * late + value
                state = (now - lam[0] * late, lam[1] * late)
                for level in range(3):
                    by = 1 << level
                    factor = pole_at(power_ref, SEGMENT + level, pole, here)
                    moved = tuple(jnp.where(sublane >= by, pltpu.roll(part, by, 0), 0.0) for part in state)
                    state = plus(state, times(factor, moved))
                for part in range(2):
                    scan_ref[2 * part + pole, :, here] = state[part]
                    total_ref[2 * part + pole : 2 * part + pole + 1, here] = state[part][SEGMENTS - 1 :]

        loop_columns(i, chunk, column)
        return 0

    lax.fori_loop(0, count, body, 0)
    for copy in smalls[3:]:
        copy.wait()
    for which in range(3):
        edge_ref[2 * which : 2 * which + 2] = end_ref[which, SUBROWS - 2 : SUBROWS]
    for which in range(2):
        edge_ref[6 + 2 * which : 8 + 2 * which] = top_ref[which, 0:2]
    own, other = halves(channels)
    keep_total[...] = total_ref[:, own]
    give_total[...] = total_ref[:, other]
    keep_edge[...] = edge_ref[:, own]
    give_edge[...] = edge_ref[:, other]


def halves(channels):
    half = channels // 2
    odd = lax.axis_index("seq") % 2
    return span(odd * half, half), span((1 - odd) * half, half)


def first_products(tail, heads, taps):
    def filtered(which, at):
        sequence = [tail[2 * which : 2 * which + 1], tail[2 * which + 1 : 2 * which + 2],
                    heads[2 * which - 2 : 2 * which - 1], heads[2 * which - 1 : 2 * which]]
        return sum(taps[tap, which : which + 1] * sequence[at + tap] for tap in range(3))

    return [filtered(1, at) * filtered(2, at) for at in range(2)]


def extra_state(products, back):
    first, second = products
    return times(back, (second * back[0] + first, second * back[1]))


def fixed_rows(products, tail, taps, skip, gain, back):
    first, second = products
    jump = sum(gain[0, pole : pole + 1] * back[0][pole : pole + 1] - gain[1, pole : pole + 1] * back[1][pole : pole + 1]
               for pole in range(POLES))
    return [skip * first - jump * second, skip * second,
            taps[0, 0:1] * tail[0:1] + taps[1, 0:1] * tail[1:2], taps[0, 0:1] * tail[1:2]]


def pick(condition, a, b):
    return tuple(jnp.where(condition, x, y) for x, y in zip(a, b))


def put_wire(wire_ref, value):
    for part in range(2):
        total = value[part][0:1] + value[part][1:2]
        difference = value[part][0:1] - value[part][1:2]
        wire_ref[2 * part : 2 * part + 2] = jnp.concatenate([total, difference], axis=0).astype(bf16)


def from_wire(wire_ref):
    value = []
    for part in range(2):
        both = wire_ref[2 * part : 2 * part + 2].astype(f32)
        total, difference = both[0:1], both[1:2]
        value.append(0.5 * jnp.concatenate([total + difference, total - difference], axis=0))
    return tuple(value)


ALL = slice(None)


def merge_kernel(total_ref, mate_ref, edge_ref, mate_edge_ref, power_ref, taps_ref, gain_ref, skip_ref,
                 joined_ref, wire_ref, lead_ref, enter_ref, base_ref, fix_ref, head_ref, *, channels):
    device = lax.axis_index("seq")
    odd = device % 2 == 1
    half = halves(channels)[0]
    taps, gain, skip = taps_ref[:, :, half], gain_ref[:, :, half], skip_ref[:, half]
    power, back = pair_at(power_ref, SPAN, half), pair_at(power_ref, BACK, half)
    mine, mates = edge_ref[...].astype(f32), mate_edge_ref[...].astype(f32)
    even_edge, odd_edge = jnp.where(odd, mates, mine), jnp.where(odd, mine, mates)
    own, mate = pair_at(total_ref, 0, ALL), pair_at(mate_ref, 0, ALL)
    even_total, odd_total = pick(odd, mate, own), pick(odd, own, mate)
    products = first_products(even_edge[0:6], odd_edge[6:10], taps)
    base = plus(even_total, extra_state(products, back))
    put_pair(base_ref, 0, ALL, base)
    for i, value in enumerate(fixed_rows(products, even_edge[0:6], taps, skip, gain, back)):
        fix_ref[i : i + 1] = value
    start = extra_state(first_products(jnp.zeros_like(even_edge[0:6]), even_edge[6:10], taps), back)
    enter = tuple(jnp.where(device < 2, part, 0.0) for part in start)
    put_pair(enter_ref, 0, ALL, enter)
    joined = plus(odd_total, times(power, plus(base, times(power, enter))))
    put_pair(joined_ref, 0, ALL, joined)
    put_pair(lead_ref, 0, ALL, (jnp.ones_like(power[0]), jnp.zeros_like(power[0])))
    put_wire(wire_ref, joined)
    wire_ref[4:10] = odd_edge[0:6].astype(bf16)
    wire_ref[10:14] = even_edge[6:10].astype(bf16)
    head_ref[...] = even_edge[6:10].astype(bf16)


def step_of(level, sent_ref, got_ref, power_ref, taps_ref, lead_ref, enter_ref, tail_before, half):
    device = lax.axis_index("seq")
    upper = (device >> level) % 2 == 1
    leads = jnp.logical_and(upper, (device % (1 << level)) < 2)
    back = pair_at(power_ref, BACK, half)
    early_tail = jnp.where(upper, got_ref[4:10].astype(f32), sent_ref[4:10].astype(f32))
    late_head = sent_ref[10:14].astype(f32)
    if got_ref.shape[0] > 10:
        late_head = jnp.where(upper, late_head, got_ref[10:14].astype(f32))
    extra = extra_state(first_products(early_tail, late_head, taps_ref[:, :, half]), back)
    other = from_wire(got_ref)
    lead, enter = pair_at(lead_ref, 0, ALL), pair_at(enter_ref, 0, ALL)
    enter = pick(upper, plus(enter, times(lead, plus(other, extra))), enter)
    return upper, other, extra, lead, enter, jnp.where(leads, early_tail, tail_before)


def join_kernel(ending_ref, sent_ref, got_ref, power_ref, taps_ref, lead_ref, enter_ref, before_ref, after_ref,
                joined_ref, wire_ref, next_lead_ref, next_enter_ref, next_before_ref, *, level, channels):
    half = halves(channels)[0]
    upper, other, extra, lead, enter, before = step_of(
        level, sent_ref, got_ref, power_ref, taps_ref, lead_ref, enter_ref, before_ref[...].astype(f32), half)
    factor = pair_at(power_ref, SPAN + level, half)
    mine = pair_at(ending_ref, 0, ALL)
    early, late = pick(upper, other, mine), pick(upper, mine, other)
    joined = plus(times(factor, plus(early, extra)), late)
    put_pair(joined_ref, 0, ALL, joined)
    put_wire(wire_ref, joined)
    got, sent = got_ref[...].astype(f32), sent_ref[...].astype(f32)
    wire_ref[4:10] = jnp.where(upper, sent[4:10], got[4:10]).astype(bf16)
    wire_ref[10:14] = jnp.where(upper, got[10:14], sent[10:14]).astype(bf16)
    put_pair(next_lead_ref, 0, ALL, pick(upper, times(lead, factor), lead))
    put_pair(next_enter_ref, 0, ALL, enter)
    next_before_ref[...] = before.astype(bf16)


def last_kernel(sent_ref, got_ref, power_ref, taps_ref, gain_ref, skip_ref, lead_ref, enter_ref, before_ref,
                base_ref, fix_ref, head_ref, after_ref, keep_ref, give_ref, *, level, channels):
    half = halves(channels)[0]
    odd = lax.axis_index("seq") % 2 == 1
    _, _, _, _, enter, before = step_of(
        level, sent_ref, got_ref, power_ref, taps_ref, lead_ref, enter_ref, before_ref[...].astype(f32), half)
    taps, gain, skip = taps_ref[:, :, half], gain_ref[:, :, half], skip_ref[:, half]
    power, back = pair_at(power_ref, SPAN, half), pair_at(power_ref, BACK, half)
    products = first_products(before, head_ref[...].astype(f32), taps)
    even = [*enter, *fixed_rows(products, before, taps, skip, gain, back)]
    odds = [*plus(times(power, enter), pair_at(base_ref, 0, ALL)), *(fix_ref[i : i + 1] for i in range(4))]
    row = 0
    for a, b in zip(even, odds):
        keep_ref[row : row + a.shape[0]] = jnp.where(odd, b, a)
        give_ref[row : row + a.shape[0]] = jnp.where(odd, a, b)
        row += a.shape[0]


def local_kernel(taps_ref, gain_ref, skip_ref, power_ref, scan_ref, prod_ref, q_ref, after_ref,
                 query_ref, local_ref, enter_ref, order_ref, qs_ref, *, base):
    rows, channels = query_ref.shape
    chunk = qs_ref.shape[1]
    order_ref[...] = order_matrix(rows, False)

    def body(i, _):
        qs_ref[...] = jnp.dot(order_ref[...], q_ref[:, span(base + i * chunk, chunk)], preferred_element_type=f32)

        def column(inner, outer):
            cols = slice(inner, inner + WIDTH)
            put = span(outer, WIDTH)
            here = span(base + outer, WIDTH)
            queries = short_filter(steps_of(qs_ref, cols), taps_ref, 0, here)
            for j, value in enumerate(queries):
                query_ref[SEGMENTS * j : SEGMENTS * (j + 1), put] = value
            products = []
            for j in range(0, len(queries), 2):
                both = prod_ref[SEGMENTS * j : SEGMENTS * (j + 2), here].astype(f32)
                products += [both[:SEGMENTS], both[SEGMENTS:]]
            before = delayed(products[-1])
            skip = wide(skip_ref[0:1, here])
            sublane = lax.broadcasted_iota(jnp.int32, (SEGMENTS, WIDTH), 0)
            coefs = []
            for pole in range(POLES):
                lam = pole_at(power_ref, LAM, pole, here)
                back = pole_at(power_ref, BACK, pole, here)
                gain = tuple(wide(gain_ref[part, pole : pole + 1, here]) for part in range(2))
                a1, a2 = feedback(lam)
                b1 = gain[0] * lam[0] + gain[1] * lam[1]
                carry = tuple(delayed(scan_ref[2 * part + pole, :, here]) for part in range(2))
                gain_back = times(gain, back)
                y1 = gain[0] * carry[0] - gain[1] * carry[1]
                y2 = gain_back[0] * (carry[0] - before) - gain_back[1] * carry[1]
                coefs.append([a1, a2, gain[0], b1, y1, y2])
                reach = gain
                for level in range(3):
                    factor = pole_at(power_ref, SEGMENT + level, pole, here)
                    bit = (sublane // (1 << level)) % 2 == 1
                    reach = times(reach, (jnp.where(bit, factor[0], 1.0), jnp.where(bit, factor[1], 0.0)))
                for part in range(2):
                    enter_ref[2 * part + pole, :, put] = reach[part]
            previous = before
            for j, value in enumerate(products):
                total = skip * value
                for pole in range(POLES):
                    a1, a2, b0, b1, y1, y2 = coefs[pole]
                    y = a1 * y1 - a2 * y2 + (b0 * value - b1 * previous)
                    coefs[pole][4:] = [y, y1]
                    total = total + y
                previous = value
                local_ref[SEGMENTS * j : SEGMENTS * (j + 1), put] = total

        loop_columns(i, chunk, column)
        return 0

    lax.fori_loop(0, channels // chunk, body, 0)


def gate_kernel(power_ref, keep_ref, got_ref, *rest, parts):
    tables = [rest[3 * i : 3 * i + 3] for i in range(len(parts))]
    out_hbm, order_ref, out_ref, gated_ref, state_ref, out_sem = rest[3 * len(parts) :]
    rows, channels = out_ref.shape
    chunk = gated_ref.shape[1]
    count = channels // chunk
    own, other = halves(channels)
    state_ref[:, own] = keep_ref[...]
    state_ref[:, other] = got_ref[...]
    order_ref[...] = order_matrix(rows, True)

    def send(i):
        place = span(i * chunk, chunk)
        return pltpu.make_async_copy(out_ref.at[:, place], out_hbm.at[:, place], out_sem.at[i])

    base = 0
    for part, (query_ref, local_ref, reach_ref) in zip(parts, tables):

        def body(i, _, base=base, query_ref=query_ref, local_ref=local_ref, reach_ref=reach_ref):
            def column(inner, outer):
                cols = slice(inner, inner + WIDTH)
                take = span(outer, WIDTH)
                here = span(base + outer, WIDTH)
                queries = steps_of(query_ref, take)
                local = steps_of(local_ref, take)
                for j in range(2):
                    local[j] = local[j] + jnp.where(first_mask(), wide(state_ref[4 + j : 5 + j, here]), 0.0)
                    queries[j] = queries[j] + jnp.where(first_mask(), wide(state_ref[6 + j : 7 + j, here]), 0.0)
                coefs = []
                for pole in range(POLES):
                    lam = pole_at(power_ref, LAM, pole, here)
                    back = pole_at(power_ref, BACK, pole, here)
                    state = times(pole_at(state_ref, 0, pole, here), (reach_ref[pole, :, take], reach_ref[2 + pole, :, take]))
                    y2 = state[0] * back[0] - state[1] * back[1]
                    coefs.append([*feedback(lam), state[0], y2])
                gated = []
                for j in range(len(queries)):
                    total = local[j]
                    for pole in range(POLES):
                        a1, a2, y1, y2 = coefs[pole]
                        y = a1 * y1 - a2 * y2
                        coefs[pole][2:] = [y, y1]
                        total = total + y
                    gated.append(queries[j] * total)
                    if j % 2:
                        both = jnp.concatenate(gated[-2:], axis=0)
                        gated_ref[SEGMENTS * (j - 1) : SEGMENTS * (j + 1), cols] = both.astype(bf16)

            loop_columns(i, chunk, column)
            out_ref[:, span(base + i * chunk, chunk)] = jnp.dot(
                order_ref[...], gated_ref[...], preferred_element_type=f32).astype(bf16)
            send(base // chunk + i).start()
            return 0

        lax.fori_loop(0, part // chunk, body, 0)
        base += part
    for i in range(count):
        send(i).wait()


def kernel_call(body, name, outs, scratch, operands, in_hbm, out_hbm=(), **options):
    def spec(far):
        return pl.BlockSpec(memory_space=pltpu.HBM if far else pltpu.VMEM)

    def bound(*refs):
        return body(*refs, **options)

    return pl.pallas_call(
        bound,
        in_specs=[spec(i in in_hbm) for i in range(len(operands))],
        out_specs=[spec(i in out_hbm) for i in range(len(outs))],
        out_shape=[jax.ShapeDtypeStruct(shape, dtype) for shape, dtype in outs],
        scratch_shapes=scratch,
        compiler_params=pltpu.CompilerParams(vmem_limit_bytes=32 << 20),
        name=name,
    )(*operands)


def on_device(projected, short_taps, skip_gain, residues, pole_angles, decay_rates):
    _, rows, channels = projected.shape
    chunk = min(CHUNK, channels)
    devices = lax.axis_size("seq")
    levels = devices.bit_length() - 1
    parts = [channels // sum(PARTS) * share for share in PARTS]
    arguments = [pole_angles, decay_rates, short_taps, residues, skip_gain[None], projected]
    arguments = [pltpu.with_memory_space_constraint(argument, pltpu.HBM) for argument in arguments]
    half = channels // 2
    state = ((4, half), f32)
    square = pltpu.VMEM((rows, rows), bf16)
    dma = pltpu.SemaphoreType.DMA

    products, scan, total, give_total, edge, give_edge, powers, taps, gains, skip, query_rows = kernel_call(
        states_kernel, "states",
        [((rows, channels), bf16), ((4, SEGMENTS, channels), f32), state, state, ((10, half), bf16), ((10, half), bf16),
         ((4 * (SPAN + levels), channels), f32), (short_taps.shape, f32), (residues.shape, f32), ((1, channels), f32), ((rows, channels), bf16)],
        [pltpu.VMEM((4, channels), f32), pltpu.VMEM((10, channels), bf16), square]
        + [pltpu.VMEM(pole_angles.shape, f32)] * 2 + [pltpu.VMEM((rows, channels), bf16)] * 2
        + [pltpu.VMEM((2, SUBROWS, channels), bf16), pltpu.VMEM((3, SUBROWS, channels), bf16)]
        + [pltpu.VMEM((rows, chunk), f32)] * 2 + [dma((8,)), dma((2, channels // chunk))],
        arguments, range(6), levels=levels)

    def exchange(array, level):
        return lax.ppermute(array, "seq", [(i, i ^ (1 << level)) for i in range(devices)])

    mate_edge = exchange(give_edge, 0)
    mate_total = exchange(give_total, 0)
    ending, sent, lead, enter, base, fix, head = kernel_call(
        merge_kernel, "merge", [state, ((14, half), bf16), state, state, state, state, ((4, half), bf16)], [],
        [total, mate_total, edge, mate_edge, powers, taps, gains, skip], (), channels=channels)
    before = jnp.zeros((6, half), bf16)

    tables = []
    start = 0
    for level in range(1, levels):
        got = exchange(sent, level)
        while len(tables) < len(parts) and (len(tables) < level or level == levels - 1):
            part = parts[len(tables)]
            plane = ((rows, part), f32)
            tables.append(kernel_call(
                local_kernel, "local", [plane, plane, ((4, SEGMENTS, part), f32)],
                [square, pltpu.VMEM((rows, chunk), f32)],
                [taps, gains, skip, powers, scan, products, query_rows, ending], (), base=start))
            start += part
        if level + 1 < levels:
            ending, sent, lead, enter, before = kernel_call(
                join_kernel, "join", [state, ((14, half), bf16), state, state, ((6, half), bf16)], [],
                [ending, sent, got, powers, taps, lead, enter, before, tables[-1][2]], (8,), level=level, channels=channels)

    keep, give = kernel_call(
        last_kernel, "last", [((8, half), f32)] * 2, [],
        [sent, got, powers, taps, gains, skip, lead, enter, before, base, fix, head, tables[-1][2]], (12,),
        level=levels - 1, channels=channels)
    got = exchange(give, 0)

    (out,) = kernel_call(
        gate_kernel, "gate", [((rows, channels), bf16)],
        [square, pltpu.VMEM((rows, channels), bf16), pltpu.VMEM((rows, chunk), bf16),
         pltpu.VMEM((8, channels), f32), dma((channels // chunk,))],
        [powers, keep, got, *[array for table in tables for array in table]], (), (0,), parts=parts)
    return out


def solution(mesh):
    return jax.shard_map(
        on_device,
        mesh=mesh,
        in_specs=(P(None, ("grp", "seq"), None), P(), P(), P(), P(), P()),
        out_specs=P(("grp", "seq"), None),
        check_vma=False,
    )
```

```python
import jax
import jax.numpy as jnp
from jax import lax
from jax.experimental import pallas as pl
from jax.experimental.pallas import tpu as pltpu
from jax.sharding import PartitionSpec as P

SEGMENTS = 8
WIDTH = 256
CHUNK = 1024
POLES = 2
SUBROWS = 16
LOCAL_CHUNK = 512
PARTS = (2, 1, 1)
f32 = jnp.float32
bf16 = jnp.bfloat16

LAM, BACK, SEGMENT, SPAN = 0, 1, 2, 5


def order_matrix(row_count, inverse):
    length = row_count // SEGMENTS
    ordered = lax.broadcasted_iota(jnp.int32, (row_count, row_count), 1 if inverse else 0)
    natural = lax.broadcasted_iota(jnp.int32, (row_count, row_count), 0 if inverse else 1)
    wanted = length * (ordered % SEGMENTS) + ordered // SEGMENTS
    return (wanted == natural).astype(f32).astype(bf16)


def wide(value):
    return jnp.broadcast_to(value, (SEGMENTS, value.shape[1]))


def times(a, b):
    return (a[0] * b[0] - a[1] * b[1], a[0] * b[1] + a[1] * b[0])


def plus(a, b):
    return (a[0] + b[0], a[1] + b[1])


def pair_at(ref, index, cols):
    return (ref[2 * index, :, cols], ref[2 * index + 1, :, cols])


def put_pair(ref, index, cols, value):
    ref[2 * index, :, cols] = value[0]
    ref[2 * index + 1, :, cols] = value[1]


def pole_at(ref, index, pole, cols):
    return (wide(ref[2 * index, pole : pole + 1, cols]), wide(ref[2 * index + 1, pole : pole + 1, cols]))


def half_angle(angle):
    x = 0.5 * angle
    u = x * x
    sine = 1.0 / 6227020800.0
    for term in (-1.0 / 39916800.0, 1.0 / 362880.0, -1.0 / 5040.0, 1.0 / 120.0, -1.0 / 6.0, 1.0):
        sine = sine * u + term
    cosine = -1.0 / 87178291200.0
    for term in (1.0 / 479001600.0, -1.0 / 3628800.0, 1.0 / 40320.0, -1.0 / 720.0, 1.0 / 24.0, -0.5, 1.0):
        cosine = cosine * u + term
    return cosine, sine * x


def fill_powers(power_ref, angle_ref, decay_ref, length, levels):
    cols = slice(None)
    cosine, sine = half_angle(angle_ref[...])
    turn = (1.0 - 2.0 * sine * sine, 2.0 * sine * cosine)
    decay = decay_ref[...]
    damping = jnp.exp(-decay)
    growth = jnp.exp(decay)
    value = (damping * turn[0], damping * turn[1])
    put_pair(power_ref, LAM, cols, value)
    put_pair(power_ref, BACK, cols, (growth * turn[0], -growth * turn[1]))
    for _ in range(length.bit_length() - 1):
        value = times(value, value)
    for level in range(3 + levels):
        put_pair(power_ref, SEGMENT + level, cols, value)
        value = times(value, value)


def steps_of(ref, cols):
    return [ref[SEGMENTS * j : SEGMENTS * (j + 1), cols] for j in range(ref.shape[0] // SEGMENTS)]


def first_mask():
    return lax.broadcasted_iota(jnp.int32, (SEGMENTS, WIDTH), 0) == 0


def delayed(value):
    return jnp.where(first_mask(), 0.0, pltpu.roll(value, 1, 0))


def short_filter(steps, taps_ref, which, cols):
    taps = [wide(taps_ref[tap, which : which + 1, cols]) for tap in range(3)]
    padded = [delayed(steps[-2]), delayed(steps[-1])] + steps
    return [
        taps[0] * padded[j] + taps[1] * padded[j + 1] + taps[2] * padded[j + 2]
        for j in range(len(steps))
    ]


def feedback(lam):
    return 2.0 * lam[0], lam[0] * lam[0] + lam[1] * lam[1]


def span(start, size):
    return pl.ds(pl.multiple_of(start, 128), size)


def loop_columns(chunk_index, chunk, body):
    for part in range(chunk // WIDTH):
        body(part * WIDTH, chunk_index * chunk + part * WIDTH)


def states_kernel(angle_hbm, decay_hbm, taps_hbm, gain_hbm, skip_hbm, proj_ref,
                  prod_ref, scan_ref, keep_total, give_total, keep_edge, give_edge, power_ref, taps_ref, gain_ref, skip_ref,
                  q_ref, total_ref, edge_ref, order_ref, angle_ref, decay_ref, k_ref, v_ref, top_ref, end_ref, ks_ref, vs_ref,
                  small_sem, in_sem, *, levels):
    rows, channels = k_ref.shape
    chunk = ks_ref.shape[1]
    count = channels // chunk
    last = rows - SUBROWS
    smalls = [
        pltpu.make_async_copy(source, target, small_sem.at[i])
        for i, (source, target) in enumerate([
            (angle_hbm, angle_ref), (decay_hbm, decay_ref), (taps_hbm, taps_ref), (gain_hbm, gain_ref),
            (skip_hbm, skip_ref), (proj_ref.at[pl.ds(1, 2), pl.ds(0, SUBROWS)], top_ref),
            (proj_ref.at[:, pl.ds(last, SUBROWS)], end_ref), (proj_ref.at[0], q_ref)])
    ]

    def fetch(i, which, ref):
        cols = span(i * chunk, chunk)
        return pltpu.make_async_copy(proj_ref.at[which, :, cols], ref.at[:, cols], in_sem.at[which - 1, i])

    for copy in smalls[:3]:
        copy.start()
    for i in range(count):
        fetch(i, 1, k_ref).start()
        fetch(i, 2, v_ref).start()
    for copy in smalls[3:]:
        copy.start()
    order_ref[...] = order_matrix(rows, False)
    for copy in smalls[:3]:
        copy.wait()
    fill_powers(power_ref, angle_ref, decay_ref, rows // SEGMENTS, levels)

    def body(i, _):
        fetch(i, 1, k_ref).wait()
        fetch(i, 2, v_ref).wait()
        at = span(i * chunk, chunk)
        ks_ref[...] = jnp.dot(order_ref[...], k_ref[:, at], preferred_element_type=f32)
        vs_ref[...] = jnp.dot(order_ref[...], v_ref[:, at], preferred_element_type=f32)

        def column(inner, outer):
            cols = slice(inner, inner + WIDTH)
            here = span(outer, WIDTH)
            keys = short_filter(steps_of(ks_ref, cols), taps_ref, 1, here)
            values = short_filter(steps_of(vs_ref, cols), taps_ref, 2, here)
            products = [a * b for a, b in zip(keys, values)]
            for j in range(2):
                products[j] = jnp.where(first_mask(), 0.0, products[j])
            for j in range(0, len(products), 2):
                both = jnp.concatenate(products[j : j + 2], axis=0)
                prod_ref[SEGMENTS * j : SEGMENTS * (j + 2), here] = both.astype(bf16)
            sublane = lax.broadcasted_iota(jnp.int32, (SEGMENTS, WIDTH), 0)
            for pole in range(POLES):
                lam = pole_at(power_ref, LAM, pole, here)
                a1, a2 = feedback(lam)
                late = products[0]
                now = a1 * late + products[1]
                for value in products[2:]:
                    late, now = now, a1 * now - a2 * late + value
                state = (now - lam[0] * late, lam[1] * late)
                for level in range(3):
                    by = 1 << level
                    factor = pole_at(power_ref, SEGMENT + level, pole, here)
                    moved = tuple(jnp.where(sublane >= by, pltpu.roll(part, by, 0), 0.0) for part in state)
                    state = plus(state, times(factor, moved))
                for part in range(2):
                    scan_ref[2 * part + pole, :, here] = state[part]
                    total_ref[part, pole : pole + 1, here] = state[part][SEGMENTS - 1 :]

        loop_columns(i, chunk, column)
        return 0

    lax.fori_loop(0, count, body, 0)
    for copy in smalls[3:]:
        copy.wait()
    for which in range(3):
        edge_ref[which] = end_ref[which, SUBROWS - 2 : SUBROWS]
    for which in range(2):
        edge_ref[3 + which] = top_ref[which, 0:2]
    own, other = halves(channels)
    keep_total[...] = total_ref[:, :, own]
    give_total[...] = total_ref[:, :, other]
    keep_edge[...] = edge_ref[:, :, own]
    give_edge[...] = edge_ref[:, :, other]


def halves(channels):
    half = channels // 2
    odd = lax.axis_index("seq") % 2
    return span(odd * half, half), span((1 - odd) * half, half)


def first_products(tail, heads, taps):
    def filtered(which):
        before, after = tail[which], heads[which - 1]
        middle = jnp.concatenate([before[1:2], after[0:1]], axis=0)
        planes = (before, middle, after)
        return sum(taps[tap, which : which + 1] * planes[tap] for tap in range(3))

    return filtered(1) * filtered(2)


def extra_state(products, back):
    first, second = products[0:1], products[1:2]
    return times(back, (second * back[0] + first, second * back[1]))


def fixed_rows(products, tail, taps, skip, gain, back):
    jump = sum(gain[0, pole : pole + 1] * back[0][pole : pole + 1] - gain[1, pole : pole + 1] * back[1][pole : pole + 1]
               for pole in range(POLES))
    none = jnp.zeros_like(jump)
    local = skip * products - jnp.concatenate([jump * products[1:2], none], axis=0)
    query = taps[0, 0:1] * tail[0] + jnp.concatenate([taps[1, 0:1] * tail[0][1:2], none], axis=0)
    return local, query


def planes_of(ref, start, stop):
    return [ref[i].astype(f32) for i in range(start, stop)]


def pick(condition, a, b):
    return tuple(jnp.where(condition, x, y) for x, y in zip(a, b))


def mixed(value):
    return jnp.concatenate([value[0:1] + value[1:2], value[0:1] - value[1:2]], axis=0)


def put_wire(wire_ref, value):
    for part in range(2):
        wire_ref[part] = mixed(value[part]).astype(bf16)


def from_wire(wire_ref):
    return tuple(0.5 * mixed(wire_ref[part].astype(f32)) for part in range(2))


ALL = slice(None)


def merge_kernel(total_ref, mate_ref, edge_ref, mate_edge_ref, power_ref, taps_ref, gain_ref, skip_ref,
                 joined_ref, wire_ref, lead_ref, enter_ref, base_ref, fix_ref, head_ref, *, channels):
    device = lax.axis_index("seq")
    odd = device % 2 == 1
    half = halves(channels)[0]
    taps, gain, skip = taps_ref[:, :, half], gain_ref[:, :, half], skip_ref[:, half]
    power, back = pair_at(power_ref, SPAN, half), pair_at(power_ref, BACK, half)
    mine, mates = planes_of(edge_ref, 0, 5), planes_of(mate_edge_ref, 0, 5)
    even_edge, odd_edge = pick(odd, mates, mine), pick(odd, mine, mates)
    own, mate = pair_at(total_ref, 0, ALL), pair_at(mate_ref, 0, ALL)
    even_total, odd_total = pick(odd, mate, own), pick(odd, own, mate)
    products = first_products(even_edge[0:3], odd_edge[3:5], taps)
    base = plus(even_total, extra_state(products, back))
    put_pair(base_ref, 0, ALL, base)
    fix_ref[0], fix_ref[1] = fixed_rows(products, even_edge[0:3], taps, skip, gain, back)
    start = extra_state(first_products([jnp.zeros_like(power[0])] * 3, even_edge[3:5], taps), back)
    enter = tuple(jnp.where(device < 2, part, 0.0) for part in start)
    put_pair(enter_ref, 0, ALL, enter)
    joined = plus(odd_total, times(power, plus(base, times(power, enter))))
    put_pair(joined_ref, 0, ALL, joined)
    put_pair(lead_ref, 0, ALL, (jnp.ones_like(power[0]), jnp.zeros_like(power[0])))
    put_wire(wire_ref, joined)
    for i in range(3):
        wire_ref[2 + i] = odd_edge[i].astype(bf16)
    for i in range(2):
        head = even_edge[3 + i].astype(bf16)
        head_ref[i] = head
        wire_ref[5 + i] = head


def step_of(level, sent_ref, got_ref, own_head, power_ref, taps_ref, lead_ref, enter_ref, tail_before, half):
    device = lax.axis_index("seq")
    upper = (device >> level) % 2 == 1
    leads = jnp.logical_and(upper, (device % (1 << level)) < 2)
    back = pair_at(power_ref, BACK, half)
    early_tail = pick(upper, planes_of(got_ref, 2, 5), planes_of(sent_ref, 2, 5))
    late_head = own_head
    if got_ref.shape[0] > 5:
        late_head = pick(upper, own_head, planes_of(got_ref, 5, 7))
    extra = extra_state(first_products(early_tail, late_head, taps_ref[:, :, half]), back)
    other = from_wire(got_ref)
    lead, enter = pair_at(lead_ref, 0, ALL), pair_at(enter_ref, 0, ALL)
    enter = pick(upper, plus(enter, times(lead, plus(other, extra))), enter)
    return upper, other, extra, lead, enter, pick(leads, early_tail, tail_before)


def join_kernel(ending_ref, sent_ref, got_ref, head_ref, power_ref, taps_ref, lead_ref, enter_ref, before_ref, after_ref,
                joined_ref, wire_ref, next_head_ref, next_lead_ref, next_enter_ref, next_before_ref, *, level, channels):
    half = halves(channels)[0]
    own_head = planes_of(head_ref, 0, 2)
    upper, other, extra, lead, enter, before = step_of(
        level, sent_ref, got_ref, own_head, power_ref, taps_ref, lead_ref, enter_ref, planes_of(before_ref, 0, 3), half)
    factor = pair_at(power_ref, SPAN + level, half)
    mine = pair_at(ending_ref, 0, ALL)
    early, late = pick(upper, other, mine), pick(upper, mine, other)
    joined = plus(times(factor, plus(early, extra)), late)
    put_pair(joined_ref, 0, ALL, joined)
    put_wire(wire_ref, joined)
    for i, plane in enumerate(pick(upper, planes_of(sent_ref, 2, 5), planes_of(got_ref, 2, 5))):
        wire_ref[2 + i] = plane.astype(bf16)
    for i, plane in enumerate(pick(upper, planes_of(got_ref, 5, 7), own_head)):
        head = plane.astype(bf16)
        next_head_ref[i] = head
        if wire_ref.shape[0] > 5:
            wire_ref[5 + i] = head
    put_pair(next_lead_ref, 0, ALL, pick(upper, times(lead, factor), lead))
    put_pair(next_enter_ref, 0, ALL, enter)
    for i in range(3):
        next_before_ref[i] = before[i].astype(bf16)


def last_kernel(sent_ref, got_ref, head_ref, power_ref, taps_ref, gain_ref, skip_ref, lead_ref, enter_ref, before_ref,
                base_ref, fix_ref, first_ref, after_ref, keep_ref, give_ref, *, level, channels):
    half = halves(channels)[0]
    odd = lax.axis_index("seq") % 2 == 1
    _, _, _, _, enter, before = step_of(
        level, sent_ref, got_ref, planes_of(head_ref, 0, 2), power_ref, taps_ref, lead_ref, enter_ref,
        planes_of(before_ref, 0, 3), half)
    taps, gain, skip = taps_ref[:, :, half], gain_ref[:, :, half], skip_ref[:, half]
    power, back = pair_at(power_ref, SPAN, half), pair_at(power_ref, BACK, half)
    products = first_products(before, planes_of(first_ref, 0, 2), taps)
    even = [*enter, *fixed_rows(products, before, taps, skip, gain, back)]
    odds = [*plus(times(power, enter), pair_at(base_ref, 0, ALL)), fix_ref[0], fix_ref[1]]
    for i, (a, b) in enumerate(zip(even, odds)):
        keep_ref[i] = jnp.where(odd, b, a)
        give_ref[i] = jnp.where(odd, a, b)


def local_kernel(taps_ref, gain_ref, skip_ref, power_ref, scan_ref, prod_ref, q_ref, after_ref,
                 query_ref, local_ref, enter_ref, order_ref, qs_ref, *, base):
    rows, channels = query_ref.shape
    chunk = qs_ref.shape[1]
    order_ref[...] = order_matrix(rows, False)

    def body(i, _):
        qs_ref[...] = jnp.dot(order_ref[...], q_ref[:, span(base + i * chunk, chunk)], preferred_element_type=f32)

        def column(inner, outer):
            cols = slice(inner, inner + WIDTH)
            put = span(outer, WIDTH)
            here = span(base + outer, WIDTH)
            queries = short_filter(steps_of(qs_ref, cols), taps_ref, 0, here)
            for j, value in enumerate(queries):
                query_ref[SEGMENTS * j : SEGMENTS * (j + 1), put] = value
            products = []
            for j in range(0, len(queries), 2):
                both = prod_ref[SEGMENTS * j : SEGMENTS * (j + 2), here].astype(f32)
                products += [both[:SEGMENTS], both[SEGMENTS:]]
            before = delayed(products[-1])
            skip = wide(skip_ref[0:1, here])
            sublane = lax.broadcasted_iota(jnp.int32, (SEGMENTS, WIDTH), 0)
            coefs = []
            for pole in range(POLES):
                lam = pole_at(power_ref, LAM, pole, here)
                back = pole_at(power_ref, BACK, pole, here)
                gain = tuple(wide(gain_ref[part, pole : pole + 1, here]) for part in range(2))
                a1, a2 = feedback(lam)
                b1 = gain[0] * lam[0] + gain[1] * lam[1]
                carry = tuple(delayed(scan_ref[2 * part + pole, :, here]) for part in range(2))
                gain_back = times(gain, back)
                y1 = gain[0] * carry[0] - gain[1] * carry[1]
                y2 = gain_back[0] * (carry[0] - before) - gain_back[1] * carry[1]
                coefs.append([a1, a2, gain[0], b1, y1, y2])
                reach = gain
                for level in range(3):
                    factor = pole_at(power_ref, SEGMENT + level, pole, here)
                    bit = (sublane // (1 << level)) % 2 == 1
                    reach = times(reach, (jnp.where(bit, factor[0], 1.0), jnp.where(bit, factor[1], 0.0)))
                for part in range(2):
                    enter_ref[2 * part + pole, :, put] = reach[part]
            previous = before
            for j, value in enumerate(products):
                total = skip * value
                for pole in range(POLES):
                    a1, a2, b0, b1, y1, y2 = coefs[pole]
                    y = a1 * y1 - a2 * y2 + (b0 * value - b1 * previous)
                    coefs[pole][4:] = [y, y1]
                    total = total + y
                previous = value
                local_ref[SEGMENTS * j : SEGMENTS * (j + 1), put] = total

        loop_columns(i, chunk, column)
        return 0

    lax.fori_loop(0, channels // chunk, body, 0)


def gate_kernel(power_ref, keep_ref, got_ref, *rest, parts):
    tables = [rest[3 * i : 3 * i + 3] for i in range(len(parts))]
    out_hbm, order_ref, out_ref, gated_ref, state_ref, out_sem = rest[3 * len(parts) :]
    rows, channels = out_ref.shape
    chunk = gated_ref.shape[1]
    count = channels // chunk
    own, other = halves(channels)
    state_ref[:, :, own] = keep_ref[...]
    state_ref[:, :, other] = got_ref[...]
    order_ref[...] = order_matrix(rows, True)

    def send(i):
        place = span(i * chunk, chunk)
        return pltpu.make_async_copy(out_ref.at[:, place], out_hbm.at[:, place], out_sem.at[i])

    base = 0
    for part, (query_ref, local_ref, reach_ref) in zip(parts, tables):

        def body(i, _, base=base, query_ref=query_ref, local_ref=local_ref, reach_ref=reach_ref):
            def column(inner, outer):
                cols = slice(inner, inner + WIDTH)
                take = span(outer, WIDTH)
                here = span(base + outer, WIDTH)
                queries = steps_of(query_ref, take)
                local = steps_of(local_ref, take)
                for j in range(2):
                    local[j] = local[j] + jnp.where(first_mask(), wide(state_ref[2, j : j + 1, here]), 0.0)
                    queries[j] = queries[j] + jnp.where(first_mask(), wide(state_ref[3, j : j + 1, here]), 0.0)
                coefs = []
                for pole in range(POLES):
                    lam = pole_at(power_ref, LAM, pole, here)
                    back = pole_at(power_ref, BACK, pole, here)
                    state = times(pole_at(state_ref, 0, pole, here), (reach_ref[pole, :, take], reach_ref[2 + pole, :, take]))
                    y2 = state[0] * back[0] - state[1] * back[1]
                    coefs.append([*feedback(lam), state[0], y2])
                gated = []
                for j in range(len(queries)):
                    total = local[j]
                    for pole in range(POLES):
                        a1, a2, y1, y2 = coefs[pole]
                        y = a1 * y1 - a2 * y2
                        coefs[pole][2:] = [y, y1]
                        total = total + y
                    gated.append(queries[j] * total)
                    if j % 2:
                        both = jnp.concatenate(gated[-2:], axis=0)
                        gated_ref[SEGMENTS * (j - 1) : SEGMENTS * (j + 1), cols] = both.astype(bf16)

            loop_columns(i, chunk, column)
            out_ref[:, span(base + i * chunk, chunk)] = jnp.dot(
                order_ref[...], gated_ref[...], preferred_element_type=f32).astype(bf16)
            send(base // chunk + i).start()
            return 0

        lax.fori_loop(0, part // chunk, body, 0)
        base += part
    for i in range(count):
        send(i).wait()


def kernel_call(body, name, outs, scratch, operands, in_hbm, out_hbm=(), **options):
    def spec(far):
        return pl.BlockSpec(memory_space=pltpu.HBM if far else pltpu.VMEM)

    def bound(*refs):
        return body(*refs, **options)

    return pl.pallas_call(
        bound,
        in_specs=[spec(i in in_hbm) for i in range(len(operands))],
        out_specs=[spec(i in out_hbm) for i in range(len(outs))],
        out_shape=[jax.ShapeDtypeStruct(shape, dtype) for shape, dtype in outs],
        scratch_shapes=scratch,
        compiler_params=pltpu.CompilerParams(vmem_limit_bytes=32 << 20),
        name=name,
    )(*operands)


def on_device(projected, short_taps, skip_gain, residues, pole_angles, decay_rates):
    _, rows, channels = projected.shape
    chunk = min(CHUNK, channels)
    devices = lax.axis_size("seq")
    levels = devices.bit_length() - 1
    parts = [channels // sum(PARTS) * share for share in PARTS]
    arguments = [pole_angles, decay_rates, short_taps, residues, skip_gain[None], projected]
    arguments = [pltpu.with_memory_space_constraint(argument, pltpu.HBM) for argument in arguments]
    half = channels // 2
    local_chunk = min(LOCAL_CHUNK, channels)
    square = pltpu.VMEM((rows, rows), bf16)
    dma = pltpu.SemaphoreType.DMA

    def pairs(count, dtype=f32, extent=half):
        return (count, POLES, extent), dtype

    state = pairs(2)
    products, scan, total, give_total, edge, give_edge, powers, taps, gains, skip, query_rows = kernel_call(
        states_kernel, "states",
        [((rows, channels), bf16), ((4, SEGMENTS, channels), f32), state, state, pairs(5, bf16), pairs(5, bf16),
         pairs(2 * (SPAN + levels), f32, channels), (short_taps.shape, f32), (residues.shape, f32),
         ((1, channels), f32), ((rows, channels), bf16)],
        [pltpu.VMEM(*pairs(2, f32, channels)), pltpu.VMEM(*pairs(5, bf16, channels)), square]
        + [pltpu.VMEM(pole_angles.shape, f32)] * 2 + [pltpu.VMEM((rows, channels), bf16)] * 2
        + [pltpu.VMEM((2, SUBROWS, channels), bf16), pltpu.VMEM((3, SUBROWS, channels), bf16)]
        + [pltpu.VMEM((rows, chunk), f32)] * 2 + [dma((8,)), dma((2, channels // chunk))],
        arguments, range(6), levels=levels)

    def exchange(array, level):
        return lax.ppermute(array, "seq", [(i, i ^ (1 << level)) for i in range(devices)])

    def message(level):
        return pairs(5 if level == levels - 1 else 7, bf16)

    mate_edge = exchange(give_edge, 0)
    mate_total = exchange(give_total, 0)
    ending, sent, lead, enter, base, fix, first = kernel_call(
        merge_kernel, "merge", [state, pairs(7, bf16), state, state, state, state, pairs(2, bf16)], [],
        [total, mate_total, edge, mate_edge, powers, taps, gains, skip], (), channels=channels)
    head = first
    before = jnp.zeros(*pairs(3, bf16))

    tables = []
    start = 0
    for level in range(1, levels):
        got = exchange(sent, level)
        while len(tables) < len(parts) and (len(tables) < level or level == levels - 1):
            part = parts[len(tables)]
            plane = ((rows, part), f32)
            tables.append(kernel_call(
                local_kernel, "local", [plane, plane, ((4, SEGMENTS, part), f32)],
                [square, pltpu.VMEM((rows, local_chunk), f32)],
                [taps, gains, skip, powers, scan, products, query_rows, ending], (), base=start))
            start += part
        after = tables[-1][2]
        if level + 1 < levels:
            ending, sent, head, lead, enter, before = kernel_call(
                join_kernel, "join", [state, message(level + 1), pairs(2, bf16), state, state, pairs(3, bf16)], [],
                [ending, sent, got, head, powers, taps, lead, enter, before, after], (9,), level=level, channels=channels)

    keep, give = kernel_call(
        last_kernel, "last", [pairs(4)] * 2, [],
        [sent, got, head, powers, taps, gains, skip, lead, enter, before, base, fix, first, after], (13,),
        level=levels - 1, channels=channels)
    got = exchange(give, 0)

    (out,) = kernel_call(
        gate_kernel, "gate", [((rows, channels), bf16)],
        [square, pltpu.VMEM((rows, channels), bf16), pltpu.VMEM((rows, chunk), bf16),
         pltpu.VMEM(*pairs(4, f32, channels)), dma((channels // chunk,))],
        [powers, keep, got, *[array for table in tables for array in table]], (), (0,), parts=parts)
    return out


def solution(mesh):
    return jax.shard_map(
        on_device,
        mesh=mesh,
        in_specs=(P(None, ("grp", "seq"), None), P(), P(), P(), P(), P()),
        out_specs=P(("grp", "seq"), None),
        check_vma=False,
    )
```

```python
import jax
import jax.numpy as jnp
from jax import lax
from jax.experimental import pallas as pl
from jax.experimental.pallas import tpu as pltpu
from jax.sharding import PartitionSpec as P

SEGMENTS = 8
WIDTH = 256
CHUNK = 1024
POLES = 2
SUBROWS = 16
LOCAL_CHUNK = 512
PARTS = (2, 1, 1)
f32 = jnp.float32
bf16 = jnp.bfloat16

LAM, BACK, SEGMENT, SPAN = 0, 1, 2, 5


def order_matrix(row_count, inverse):
    length = row_count // SEGMENTS
    ordered = lax.broadcasted_iota(jnp.int32, (row_count, row_count), 1 if inverse else 0)
    natural = lax.broadcasted_iota(jnp.int32, (row_count, row_count), 0 if inverse else 1)
    wanted = length * (ordered % SEGMENTS) + ordered // SEGMENTS
    return (wanted == natural).astype(f32).astype(bf16)


def wide(value):
    return jnp.broadcast_to(value, (SEGMENTS, value.shape[1]))


def times(a, b):
    return (a[0] * b[0] - a[1] * b[1], a[0] * b[1] + a[1] * b[0])


def plus(a, b):
    return (a[0] + b[0], a[1] + b[1])


def pair_at(ref, index, cols):
    return (ref[2 * index, :, cols], ref[2 * index + 1, :, cols])


def put_pair(ref, index, cols, value):
    ref[2 * index, :, cols] = value[0]
    ref[2 * index + 1, :, cols] = value[1]


def pole_at(ref, index, pole, cols):
    return (wide(ref[2 * index, pole : pole + 1, cols]), wide(ref[2 * index + 1, pole : pole + 1, cols]))


def half_angle(angle):
    x = 0.5 * angle
    u = x * x
    sine = 1.0 / 6227020800.0
    for term in (-1.0 / 39916800.0, 1.0 / 362880.0, -1.0 / 5040.0, 1.0 / 120.0, -1.0 / 6.0, 1.0):
        sine = sine * u + term
    cosine = -1.0 / 87178291200.0
    for term in (1.0 / 479001600.0, -1.0 / 3628800.0, 1.0 / 40320.0, -1.0 / 720.0, 1.0 / 24.0, -0.5, 1.0):
        cosine = cosine * u + term
    return cosine, sine * x


def fill_powers(power_ref, angle_ref, decay_ref, length, levels):
    cols = slice(None)
    cosine, sine = half_angle(angle_ref[...])
    turn = (1.0 - 2.0 * sine * sine, 2.0 * sine * cosine)
    decay = decay_ref[...]
    damping = jnp.exp(-decay)
    growth = jnp.exp(decay)
    value = (damping * turn[0], damping * turn[1])
    put_pair(power_ref, LAM, cols, value)
    put_pair(power_ref, BACK, cols, (growth * turn[0], -growth * turn[1]))
    for _ in range(length.bit_length() - 1):
        value = times(value, value)
    for level in range(3 + levels):
        put_pair(power_ref, SEGMENT + level, cols, value)
        value = times(value, value)


def steps_of(ref, cols):
    return [ref[SEGMENTS * j : SEGMENTS * (j + 1), cols] for j in range(ref.shape[0] // SEGMENTS)]


def first_mask():
    return lax.broadcasted_iota(jnp.int32, (SEGMENTS, WIDTH), 0) == 0


def delayed(value):
    return jnp.where(first_mask(), 0.0, pltpu.roll(value, 1, 0))


def short_filter(steps, taps_ref, which, cols):
    taps = [wide(taps_ref[tap, which : which + 1, cols]) for tap in range(3)]
    padded = [delayed(steps[-2]), delayed(steps[-1])] + steps
    return [
        taps[0] * padded[j] + taps[1] * padded[j + 1] + taps[2] * padded[j + 2]
        for j in range(len(steps))
    ]


def feedback(lam):
    return 2.0 * lam[0], lam[0] * lam[0] + lam[1] * lam[1]


def span(start, size):
    return pl.ds(pl.multiple_of(start, 128), size)


def loop_columns(chunk_index, chunk, body):
    for part in range(chunk // WIDTH):
        body(part * WIDTH, chunk_index * chunk + part * WIDTH)


def states_kernel(angle_hbm, decay_hbm, taps_hbm, gain_hbm, skip_hbm, proj_ref,
                  prod_ref, scan_ref, keep_ref, give_ref, power_ref, taps_ref, gain_ref, skip_ref,
                  q_ref, total_ref, order_ref, angle_ref, decay_ref, k_ref, v_ref, top_ref, end_ref, ks_ref, vs_ref,
                  small_sem, in_sem, *, levels):
    rows, channels = k_ref.shape
    chunk = ks_ref.shape[1]
    count = channels // chunk
    last = rows - SUBROWS
    smalls = [
        pltpu.make_async_copy(source, target, small_sem.at[i])
        for i, (source, target) in enumerate([
            (angle_hbm, angle_ref), (decay_hbm, decay_ref), (taps_hbm, taps_ref), (gain_hbm, gain_ref),
            (skip_hbm, skip_ref), (proj_ref.at[pl.ds(1, 2), pl.ds(0, SUBROWS)], top_ref),
            (proj_ref.at[:, pl.ds(last, SUBROWS)], end_ref), (proj_ref.at[0], q_ref)])
    ]

    def fetch(i, which, ref):
        cols = span(i * chunk, chunk)
        return pltpu.make_async_copy(proj_ref.at[which, :, cols], ref.at[:, cols], in_sem.at[which - 1, i])

    for copy in smalls[:3]:
        copy.start()
    for i in range(count):
        fetch(i, 1, k_ref).start()
        fetch(i, 2, v_ref).start()
    for copy in smalls[3:]:
        copy.start()
    order_ref[...] = order_matrix(rows, False)
    for copy in smalls[:3]:
        copy.wait()
    fill_powers(power_ref, angle_ref, decay_ref, rows // SEGMENTS, levels)

    def body(i, _):
        fetch(i, 1, k_ref).wait()
        fetch(i, 2, v_ref).wait()
        at = span(i * chunk, chunk)
        ks_ref[...] = jnp.dot(order_ref[...], k_ref[:, at], preferred_element_type=f32)
        vs_ref[...] = jnp.dot(order_ref[...], v_ref[:, at], preferred_element_type=f32)

        def column(inner, outer):
            cols = slice(inner, inner + WIDTH)
            here = span(outer, WIDTH)
            keys = short_filter(steps_of(ks_ref, cols), taps_ref, 1, here)
            values = short_filter(steps_of(vs_ref, cols), taps_ref, 2, here)
            products = [a * b for a, b in zip(keys, values)]
            for j in range(2):
                products[j] = jnp.where(first_mask(), 0.0, products[j])
            for j in range(0, len(products), 2):
                both = jnp.concatenate(products[j : j + 2], axis=0)
                prod_ref[SEGMENTS * j : SEGMENTS * (j + 2), here] = both.astype(bf16)
            sublane = lax.broadcasted_iota(jnp.int32, (SEGMENTS, WIDTH), 0)
            for pole in range(POLES):
                lam = pole_at(power_ref, LAM, pole, here)
                a1, a2 = feedback(lam)
                late = products[0]
                now = a1 * late + products[1]
                for value in products[2:]:
                    late, now = now, a1 * now - a2 * late + value
                state = (now - lam[0] * late, lam[1] * late)
                for level in range(3):
                    by = 1 << level
                    factor = pole_at(power_ref, SEGMENT + level, pole, here)
                    moved = tuple(jnp.where(sublane >= by, pltpu.roll(part, by, 0), 0.0) for part in state)
                    state = plus(state, times(factor, moved))
                for part in range(2):
                    scan_ref[2 * part + pole, :, here] = state[part]
                    total_ref[part, pole : pole + 1, here] = state[part][SEGMENTS - 1 :]

        loop_columns(i, chunk, column)
        return 0

    lax.fori_loop(0, count, body, 0)
    for copy in smalls[3:]:
        copy.wait()
    for which in range(3):
        total_ref[2 + which] = end_ref[which, SUBROWS - 2 : SUBROWS].astype(f32)
    for which in range(2):
        total_ref[5 + which] = top_ref[which, 0:2].astype(f32)
    own, other = halves(channels)
    keep_ref[...] = total_ref[:, :, own]
    give_ref[...] = total_ref[:, :, other]


def halves(channels):
    half = channels // 2
    odd = lax.axis_index("seq") % 2
    return span(odd * half, half), span((1 - odd) * half, half)


def first_products(tail, heads, taps):
    def filtered(which):
        before, after = tail[which], heads[which - 1]
        middle = jnp.concatenate([before[1:2], after[0:1]], axis=0)
        planes = (before, middle, after)
        return sum(taps[tap, which : which + 1] * planes[tap] for tap in range(3))

    return filtered(1) * filtered(2)


def extra_state(products, back):
    first, second = products[0:1], products[1:2]
    return times(back, (second * back[0] + first, second * back[1]))


def fixed_rows(products, tail, taps, skip, gain, back):
    jump = sum(gain[0, pole : pole + 1] * back[0][pole : pole + 1] - gain[1, pole : pole + 1] * back[1][pole : pole + 1]
               for pole in range(POLES))
    none = jnp.zeros_like(jump)
    local = skip * products - jnp.concatenate([jump * products[1:2], none], axis=0)
    query = taps[0, 0:1] * tail[0] + jnp.concatenate([taps[1, 0:1] * tail[0][1:2], none], axis=0)
    return local, query


def planes_of(ref, start, stop):
    return [ref[i].astype(f32) for i in range(start, stop)]


def pick(condition, a, b):
    return tuple(jnp.where(condition, x, y) for x, y in zip(a, b))


def mixed(value):
    return jnp.concatenate([value[0:1] + value[1:2], value[0:1] - value[1:2]], axis=0)


def put_wire(wire_ref, value):
    for part in range(2):
        wire_ref[part] = mixed(value[part]).astype(bf16)


def from_wire(wire_ref):
    return tuple(0.5 * mixed(wire_ref[part].astype(f32)) for part in range(2))


ALL = slice(None)


def merge_kernel(own_ref, mate_ref, power_ref, taps_ref, gain_ref, skip_ref,
                 joined_ref, wire_ref, lead_ref, enter_ref, base_ref, fix_ref, head_ref, *, channels):
    device = lax.axis_index("seq")
    odd = device % 2 == 1
    half = halves(channels)[0]
    taps, gain, skip = taps_ref[:, :, half], gain_ref[:, :, half], skip_ref[:, half]
    power, back = pair_at(power_ref, SPAN, half), pair_at(power_ref, BACK, half)
    mine, mates = planes_of(own_ref, 2, 7), planes_of(mate_ref, 2, 7)
    even_edge, odd_edge = pick(odd, mates, mine), pick(odd, mine, mates)
    own, mate = pair_at(own_ref, 0, ALL), pair_at(mate_ref, 0, ALL)
    even_total, odd_total = pick(odd, mate, own), pick(odd, own, mate)
    products = first_products(even_edge[0:3], odd_edge[3:5], taps)
    base = plus(even_total, extra_state(products, back))
    put_pair(base_ref, 0, ALL, base)
    fix_ref[0], fix_ref[1] = fixed_rows(products, even_edge[0:3], taps, skip, gain, back)
    start = extra_state(first_products([jnp.zeros_like(power[0])] * 3, even_edge[3:5], taps), back)
    enter = tuple(jnp.where(device < 2, part, 0.0) for part in start)
    put_pair(enter_ref, 0, ALL, enter)
    joined = plus(odd_total, times(power, plus(base, times(power, enter))))
    put_pair(joined_ref, 0, ALL, joined)
    put_pair(lead_ref, 0, ALL, (jnp.ones_like(power[0]), jnp.zeros_like(power[0])))
    put_wire(wire_ref, joined)
    for i in range(3):
        wire_ref[2 + i] = odd_edge[i].astype(bf16)
    for i in range(2):
        head = even_edge[3 + i].astype(bf16)
        head_ref[i] = head
        wire_ref[5 + i] = head


def step_of(level, sent_ref, got_ref, own_head, power_ref, taps_ref, lead_ref, enter_ref, tail_before, half):
    device = lax.axis_index("seq")
    upper = (device >> level) % 2 == 1
    leads = jnp.logical_and(upper, (device % (1 << level)) < 2)
    back = pair_at(power_ref, BACK, half)
    early_tail = pick(upper, planes_of(got_ref, 2, 5), planes_of(sent_ref, 2, 5))
    late_head = own_head
    if got_ref.shape[0] > 5:
        late_head = pick(upper, own_head, planes_of(got_ref, 5, 7))
    extra = extra_state(first_products(early_tail, late_head, taps_ref[:, :, half]), back)
    other = from_wire(got_ref)
    lead, enter = pair_at(lead_ref, 0, ALL), pair_at(enter_ref, 0, ALL)
    enter = pick(upper, plus(enter, times(lead, plus(other, extra))), enter)
    return upper, other, extra, lead, enter, pick(leads, early_tail, tail_before)


def join_kernel(ending_ref, sent_ref, got_ref, head_ref, power_ref, taps_ref, lead_ref, enter_ref, before_ref, after_ref,
                joined_ref, wire_ref, next_head_ref, next_lead_ref, next_enter_ref, next_before_ref, *, level, channels):
    half = halves(channels)[0]
    own_head = planes_of(head_ref, 0, 2)
    upper, other, extra, lead, enter, before = step_of(
        level, sent_ref, got_ref, own_head, power_ref, taps_ref, lead_ref, enter_ref, planes_of(before_ref, 0, 3), half)
    factor = pair_at(power_ref, SPAN + level, half)
    mine = pair_at(ending_ref, 0, ALL)
    early, late = pick(upper, other, mine), pick(upper, mine, other)
    joined = plus(times(factor, plus(early, extra)), late)
    put_pair(joined_ref, 0, ALL, joined)
    put_wire(wire_ref, joined)
    for i, plane in enumerate(pick(upper, planes_of(sent_ref, 2, 5), planes_of(got_ref, 2, 5))):
        wire_ref[2 + i] = plane.astype(bf16)
    for i, plane in enumerate(pick(upper, planes_of(got_ref, 5, 7), own_head)):
        head = plane.astype(bf16)
        next_head_ref[i] = head
        if wire_ref.shape[0] > 5:
            wire_ref[5 + i] = head
    put_pair(next_lead_ref, 0, ALL, pick(upper, times(lead, factor), lead))
    put_pair(next_enter_ref, 0, ALL, enter)
    for i in range(3):
        next_before_ref[i] = before[i].astype(bf16)


def last_kernel(sent_ref, got_ref, head_ref, power_ref, taps_ref, gain_ref, skip_ref, lead_ref, enter_ref, before_ref,
                base_ref, fix_ref, first_ref, after_ref, keep_ref, give_ref, *, level, channels):
    half = halves(channels)[0]
    odd = lax.axis_index("seq") % 2 == 1
    _, _, _, _, enter, before = step_of(
        level, sent_ref, got_ref, planes_of(head_ref, 0, 2), power_ref, taps_ref, lead_ref, enter_ref,
        planes_of(before_ref, 0, 3), half)
    taps, gain, skip = taps_ref[:, :, half], gain_ref[:, :, half], skip_ref[:, half]
    power, back = pair_at(power_ref, SPAN, half), pair_at(power_ref, BACK, half)
    products = first_products(before, planes_of(first_ref, 0, 2), taps)
    even = [*enter, *fixed_rows(products, before, taps, skip, gain, back)]
    odds = [*plus(times(power, enter), pair_at(base_ref, 0, ALL)), fix_ref[0], fix_ref[1]]
    for i, (a, b) in enumerate(zip(even, odds)):
        keep_ref[i] = jnp.where(odd, b, a)
        give_ref[i] = jnp.where(odd, a, b)


def local_kernel(taps_ref, gain_ref, skip_ref, power_ref, scan_ref, prod_ref, q_ref, after_ref,
                 query_ref, local_ref, enter_ref, order_ref, qs_ref, *, base):
    rows, channels = query_ref.shape
    chunk = qs_ref.shape[1]
    order_ref[...] = order_matrix(rows, False)

    def body(i, _):
        qs_ref[...] = jnp.dot(order_ref[...], q_ref[:, span(base + i * chunk, chunk)], preferred_element_type=f32)

        def column(inner, outer):
            cols = slice(inner, inner + WIDTH)
            put = span(outer, WIDTH)
            here = span(base + outer, WIDTH)
            queries = short_filter(steps_of(qs_ref, cols), taps_ref, 0, here)
            for j, value in enumerate(queries):
                query_ref[SEGMENTS * j : SEGMENTS * (j + 1), put] = value
            products = []
            for j in range(0, len(queries), 2):
                both = prod_ref[SEGMENTS * j : SEGMENTS * (j + 2), here].astype(f32)
                products += [both[:SEGMENTS], both[SEGMENTS:]]
            before = delayed(products[-1])
            skip = wide(skip_ref[0:1, here])
            sublane = lax.broadcasted_iota(jnp.int32, (SEGMENTS, WIDTH), 0)
            coefs = []
            for pole in range(POLES):
                lam = pole_at(power_ref, LAM, pole, here)
                back = pole_at(power_ref, BACK, pole, here)
                gain = tuple(wide(gain_ref[part, pole : pole + 1, here]) for part in range(2))
                a1, a2 = feedback(lam)
                b1 = gain[0] * lam[0] + gain[1] * lam[1]
                carry = tuple(delayed(scan_ref[2 * part + pole, :, here]) for part in range(2))
                gain_back = times(gain, back)
                y1 = gain[0] * carry[0] - gain[1] * carry[1]
                y2 = gain_back[0] * (carry[0] - before) - gain_back[1] * carry[1]
                coefs.append([a1, a2, gain[0], b1, y1, y2])
                reach = gain
                for level in range(3):
                    factor = pole_at(power_ref, SEGMENT + level, pole, here)
                    bit = (sublane // (1 << level)) % 2 == 1
                    reach = times(reach, (jnp.where(bit, factor[0], 1.0), jnp.where(bit, factor[1], 0.0)))
                for part in range(2):
                    enter_ref[2 * part + pole, :, put] = reach[part]
            previous = before
            for j, value in enumerate(products):
                total = skip * value
                for pole in range(POLES):
                    a1, a2, b0, b1, y1, y2 = coefs[pole]
                    y = a1 * y1 - a2 * y2 + (b0 * value - b1 * previous)
                    coefs[pole][4:] = [y, y1]
                    total = total + y
                previous = value
                local_ref[SEGMENTS * j : SEGMENTS * (j + 1), put] = total

        loop_columns(i, chunk, column)
        return 0

    lax.fori_loop(0, channels // chunk, body, 0)


def gate_kernel(power_ref, state_ref, *rest, parts, ready):
    count = 3 * len(parts)
    tables, rest = rest[:count], rest[count:]
    if ready:
        ready_ref, out_hbm, order_ref, out_ref, gated_ref, out_sem = rest
    else:
        out_ref, order_ref, gated_ref = rest
    half = out_ref.shape[1]
    chunk = gated_ref.shape[1]
    own, other = halves(2 * half)
    odd = lax.axis_index("seq") % 2
    side = 1 - odd if ready else odd
    begin = side * half

    def send(i):
        place = span(i * chunk, chunk)
        return pltpu.make_async_copy(
            out_ref.at[:, place], out_hbm.at[:, span(begin + i * chunk, chunk)], out_sem.at[i])

    if ready:
        finished = pltpu.make_async_copy(ready_ref, out_hbm.at[:, own], out_sem.at[half // chunk])
        finished.start()
    order_ref[...] = order_matrix(gated_ref.shape[0], True)

    def gate_part(base, part, query_ref, local_ref, reach_ref):
        def body(i, _):
            def column(inner, outer):
                cols = slice(inner, inner + WIDTH)
                take = span(outer, WIDTH)
                there = span(base % half + outer, WIDTH)
                here = span(base + outer, WIDTH)
                queries = steps_of(query_ref, take)
                local = steps_of(local_ref, take)
                for j in range(2):
                    local[j] = local[j] + jnp.where(first_mask(), wide(state_ref[2, j : j + 1, there]), 0.0)
                    queries[j] = queries[j] + jnp.where(first_mask(), wide(state_ref[3, j : j + 1, there]), 0.0)
                coefs = []
                for pole in range(POLES):
                    lam = pole_at(power_ref, LAM, pole, here)
                    back = pole_at(power_ref, BACK, pole, here)
                    state = times(pole_at(state_ref, 0, pole, there), (reach_ref[pole, :, take], reach_ref[2 + pole, :, take]))
                    y2 = state[0] * back[0] - state[1] * back[1]
                    coefs.append([*feedback(lam), state[0], y2])
                gated = []
                for j in range(len(queries)):
                    total = local[j]
                    for pole in range(POLES):
                        a1, a2, y1, y2 = coefs[pole]
                        y = a1 * y1 - a2 * y2
                        coefs[pole][2:] = [y, y1]
                        total = total + y
                    gated.append(queries[j] * total)
                    if j % 2:
                        both = jnp.concatenate(gated[-2:], axis=0)
                        gated_ref[SEGMENTS * (j - 1) : SEGMENTS * (j + 1), cols] = both.astype(bf16)

            loop_columns(i, chunk, column)
            place = base % half // chunk + i
            out_ref[:, span(place * chunk, chunk)] = jnp.dot(
                order_ref[...], gated_ref[...], preferred_element_type=f32).astype(bf16)
            if ready:
                send(place).start()
            return 0

        lax.fori_loop(0, part // chunk, body, 0)

    base = 0
    for index, part in enumerate(parts):

        @pl.when(side == base // half)
        def _(base=base, part=part, refs=tables[3 * index : 3 * index + 3]):
            gate_part(base, part, *refs)

        base += part
    if ready:
        for i in range(half // chunk):
            send(i).wait()
        finished.wait()


def kernel_call(body, name, outs, scratch, operands, in_hbm, out_hbm=(), **options):
    def spec(far):
        return pl.BlockSpec(memory_space=pltpu.HBM if far else pltpu.VMEM)

    def bound(*refs):
        return body(*refs, **options)

    return pl.pallas_call(
        bound,
        in_specs=[spec(i in in_hbm) for i in range(len(operands))],
        out_specs=[spec(i in out_hbm) for i in range(len(outs))],
        out_shape=[jax.ShapeDtypeStruct(shape, dtype) for shape, dtype in outs],
        scratch_shapes=scratch,
        compiler_params=pltpu.CompilerParams(vmem_limit_bytes=32 << 20),
        name=name,
    )(*operands)


def on_device(projected, short_taps, skip_gain, residues, pole_angles, decay_rates):
    _, rows, channels = projected.shape
    chunk = min(CHUNK, channels)
    devices = lax.axis_size("seq")
    levels = devices.bit_length() - 1
    parts = [channels // sum(PARTS) * share for share in PARTS]
    arguments = [pole_angles, decay_rates, short_taps, residues, skip_gain[None], projected]
    arguments = [pltpu.with_memory_space_constraint(argument, pltpu.HBM) for argument in arguments]
    half = channels // 2
    local_chunk = min(LOCAL_CHUNK, channels)
    square = pltpu.VMEM((rows, rows), bf16)
    dma = pltpu.SemaphoreType.DMA

    def pairs(count, dtype=f32, extent=half):
        return (count, POLES, extent), dtype

    state = pairs(2)
    products, scan, keep, give, powers, taps, gains, skip, query_rows = kernel_call(
        states_kernel, "states",
        [((rows, channels), bf16), ((4, SEGMENTS, channels), f32), pairs(7), pairs(7),
         pairs(2 * (SPAN + levels), f32, channels), (short_taps.shape, f32), (residues.shape, f32),
         ((1, channels), f32), ((rows, channels), bf16)],
        [pltpu.VMEM(*pairs(7, f32, channels)), square]
        + [pltpu.VMEM(pole_angles.shape, f32)] * 2 + [pltpu.VMEM((rows, channels), bf16)] * 2
        + [pltpu.VMEM((2, SUBROWS, channels), bf16), pltpu.VMEM((3, SUBROWS, channels), bf16)]
        + [pltpu.VMEM((rows, chunk), f32)] * 2 + [dma((8,)), dma((2, channels // chunk))],
        arguments, range(6), levels=levels)

    def exchange(array, level):
        return lax.ppermute(array, "seq", [(i, i ^ (1 << level)) for i in range(devices)])

    def message(level):
        return pairs(5 if level == levels - 1 else 7, bf16)

    got = exchange(give, 0)
    ending, sent, lead, enter, base, fix, first = kernel_call(
        merge_kernel, "merge", [state, pairs(7, bf16), state, state, state, state, pairs(2, bf16)], [],
        [keep, got, powers, taps, gains, skip], (), channels=channels)
    head = first
    before = jnp.zeros(*pairs(3, bf16))

    tables = []
    start = 0
    for level in range(1, levels):
        got = exchange(sent, level)
        while len(tables) < len(parts) and (len(tables) < level or level == levels - 1):
            part = parts[len(tables)]
            plane = ((rows, part), f32)
            tables.append(kernel_call(
                local_kernel, "local", [plane, plane, ((4, SEGMENTS, part), f32)],
                [square, pltpu.VMEM((rows, local_chunk), f32)],
                [taps, gains, skip, powers, scan, products, query_rows, ending], (), base=start))
            start += part
        after = tables[-1][2]
        if level + 1 < levels:
            ending, sent, head, lead, enter, before = kernel_call(
                join_kernel, "join", [state, message(level + 1), pairs(2, bf16), state, state, pairs(3, bf16)], [],
                [ending, sent, got, head, powers, taps, lead, enter, before, after], (9,), level=level, channels=channels)

    keep, give = kernel_call(
        last_kernel, "last", [pairs(4)] * 2, [],
        [sent, got, head, powers, taps, gains, skip, lead, enter, before, base, fix, first, after], (13,),
        level=levels - 1, channels=channels)
    got = exchange(give, 0)
    flat = [array for table in tables for array in table]
    half_plane = ((rows, half), bf16)
    scratch = [square, pltpu.VMEM(*half_plane), pltpu.VMEM((rows, chunk), bf16), dma((half // chunk + 1,))]
    (ready,) = kernel_call(
        gate_kernel, "gate", [half_plane], [square, scratch[2]], [powers, keep, *flat], (), parts=parts, ready=False)
    (out,) = kernel_call(
        gate_kernel, "finish", [((rows, channels), bf16)], scratch, [powers, got, *flat, ready], (), (0,),
        parts=parts, ready=True)
    return out


def solution(mesh):
    return jax.shard_map(
        on_device,
        mesh=mesh,
        in_specs=(P(None, ("grp", "seq"), None), P(), P(), P(), P(), P()),
        out_specs=P(("grp", "seq"), None),
        check_vma=False,
    )
```

```python
import jax
import jax.numpy as jnp
from jax import lax
from jax.experimental import pallas as pl
from jax.experimental.pallas import tpu as pltpu
from jax.sharding import PartitionSpec as P

SEGMENTS = 8
WIDTH = 256
CHUNK = 1024
POLES = 2
SUBROWS = 16
LOCAL_CHUNK = 512
STATES_CHUNK = 1024
PARTS = (2, 1, 1)
f32 = jnp.float32
bf16 = jnp.bfloat16

LAM, BACK, SEGMENT, SPAN = 0, 1, 2, 5


def order_matrix(row_count, inverse):
    length = row_count // SEGMENTS
    ordered = lax.broadcasted_iota(jnp.int32, (row_count, row_count), 1 if inverse else 0)
    natural = lax.broadcasted_iota(jnp.int32, (row_count, row_count), 0 if inverse else 1)
    wanted = length * (ordered % SEGMENTS) + ordered // SEGMENTS
    return (wanted == natural).astype(f32).astype(bf16)


def wide(value):
    return jnp.broadcast_to(value, (SEGMENTS, value.shape[1]))


def times(a, b):
    return (a[0] * b[0] - a[1] * b[1], a[0] * b[1] + a[1] * b[0])


def plus(a, b):
    return (a[0] + b[0], a[1] + b[1])


def pair_at(ref, index, cols):
    return (ref[2 * index, :, cols], ref[2 * index + 1, :, cols])


def put_pair(ref, index, cols, value):
    ref[2 * index, :, cols] = value[0]
    ref[2 * index + 1, :, cols] = value[1]


def pole_at(ref, index, pole, cols):
    return (wide(ref[2 * index, pole : pole + 1, cols]), wide(ref[2 * index + 1, pole : pole + 1, cols]))


def half_angle(angle):
    x = 0.5 * angle
    u = x * x
    sine = 1.0 / 6227020800.0
    for term in (-1.0 / 39916800.0, 1.0 / 362880.0, -1.0 / 5040.0, 1.0 / 120.0, -1.0 / 6.0, 1.0):
        sine = sine * u + term
    cosine = -1.0 / 87178291200.0
    for term in (1.0 / 479001600.0, -1.0 / 3628800.0, 1.0 / 40320.0, -1.0 / 720.0, 1.0 / 24.0, -0.5, 1.0):
        cosine = cosine * u + term
    return cosine, sine * x


def fill_powers(power_ref, angle_ref, decay_ref, length, levels):
    cols = slice(None)
    cosine, sine = half_angle(angle_ref[...])
    turn = (1.0 - 2.0 * sine * sine, 2.0 * sine * cosine)
    decay = decay_ref[...]
    damping = jnp.exp(-decay)
    growth = jnp.exp(decay)
    value = (damping * turn[0], damping * turn[1])
    put_pair(power_ref, LAM, cols, value)
    put_pair(power_ref, BACK, cols, (growth * turn[0], -growth * turn[1]))
    for _ in range(length.bit_length() - 1):
        value = times(value, value)
    for level in range(3 + levels):
        put_pair(power_ref, SEGMENT + level, cols, value)
        value = times(value, value)


def steps_of(ref, cols):
    return [ref[SEGMENTS * j : SEGMENTS * (j + 1), cols] for j in range(ref.shape[0] // SEGMENTS)]


def first_mask():
    return lax.broadcasted_iota(jnp.int32, (SEGMENTS, WIDTH), 0) == 0


def delayed(value):
    return jnp.where(first_mask(), 0.0, pltpu.roll(value, 1, 0))


def short_filter(steps, taps_ref, which, cols):
    taps = [wide(taps_ref[tap, which : which + 1, cols]) for tap in range(3)]
    padded = [delayed(steps[-2]), delayed(steps[-1])] + steps
    return [
        taps[0] * padded[j] + taps[1] * padded[j + 1] + taps[2] * padded[j + 2]
        for j in range(len(steps))
    ]


def feedback(lam):
    return 2.0 * lam[0], lam[0] * lam[0] + lam[1] * lam[1]


def span(start, size):
    return pl.ds(pl.multiple_of(start, 128), size)


def loop_columns(chunk_index, chunk, body):
    for part in range(chunk // WIDTH):
        body(part * WIDTH, chunk_index * chunk + part * WIDTH)


def states_kernel(angle_hbm, decay_hbm, taps_hbm, gain_hbm, skip_hbm, proj_ref,
                  prod_ref, scan_ref, keep_ref, give_ref, power_ref, taps_ref, gain_ref, skip_ref,
                  q_ref, total_ref, order_ref, angle_ref, decay_ref, kv_ref, ks_ref, vs_ref,
                  small_sem, in_sem, *, levels):
    _, rows, channels = kv_ref.shape
    chunk = ks_ref.shape[1]
    count = channels // chunk
    smalls = [
        pltpu.make_async_copy(source, target, small_sem.at[i])
        for i, (source, target) in enumerate([
            (angle_hbm, angle_ref), (decay_hbm, decay_ref), (taps_hbm, taps_ref), (gain_hbm, gain_ref),
            (skip_hbm, skip_ref), (proj_ref.at[0], q_ref)])
    ]

    def fetch(i):
        cols = span(i * chunk, chunk)
        return pltpu.make_async_copy(proj_ref.at[pl.ds(1, 2), :, cols], kv_ref.at[:, :, cols], in_sem.at[i])

    for copy in smalls[:3]:
        copy.start()
    for i in range(count):
        fetch(i).start()
    for copy in smalls[3:]:
        copy.start()
    order_ref[...] = order_matrix(rows, False)
    for copy in smalls[:3]:
        copy.wait()
    fill_powers(power_ref, angle_ref, decay_ref, rows // SEGMENTS, levels)

    def body(i, _):
        fetch(i).wait()
        at = span(i * chunk, chunk)
        ks_ref[...] = jnp.dot(order_ref[...], kv_ref[0, :, at], preferred_element_type=f32)
        vs_ref[...] = jnp.dot(order_ref[...], kv_ref[1, :, at], preferred_element_type=f32)

        def column(inner, outer):
            cols = slice(inner, inner + WIDTH)
            here = span(outer, WIDTH)
            keys = short_filter(steps_of(ks_ref, cols), taps_ref, 1, here)
            values = short_filter(steps_of(vs_ref, cols), taps_ref, 2, here)
            products = [a * b for a, b in zip(keys, values)]
            for j in range(2):
                products[j] = jnp.where(first_mask(), 0.0, products[j])
            for j in range(0, len(products), 2):
                both = jnp.concatenate(products[j : j + 2], axis=0)
                prod_ref[SEGMENTS * j : SEGMENTS * (j + 2), here] = both.astype(bf16)
            sublane = lax.broadcasted_iota(jnp.int32, (SEGMENTS, WIDTH), 0)
            for pole in range(POLES):
                lam = pole_at(power_ref, LAM, pole, here)
                a1, a2 = feedback(lam)
                late = products[0]
                now = a1 * late + products[1]
                for value in products[2:]:
                    late, now = now, a1 * now - a2 * late + value
                state = (now - lam[0] * late, lam[1] * late)
                for level in range(3):
                    by = 1 << level
                    factor = pole_at(power_ref, SEGMENT + level, pole, here)
                    moved = tuple(jnp.where(sublane >= by, pltpu.roll(part, by, 0), 0.0) for part in state)
                    state = plus(state, times(factor, moved))
                for part in range(2):
                    scan_ref[2 * part + pole, :, here] = state[part]
                    total_ref[part, pole : pole + 1, here] = state[part][SEGMENTS - 1 :]

        loop_columns(i, chunk, column)
        return 0

    lax.fori_loop(0, count, body, 0)
    for copy in smalls[3:]:
        copy.wait()
    last = slice(rows - SUBROWS, rows)
    for which, tail in enumerate((q_ref[last, :], kv_ref[0, last, :], kv_ref[1, last, :])):
        total_ref[2 + which] = tail[SUBROWS - 2 :].astype(f32)
    for which in range(2):
        total_ref[5 + which] = kv_ref[which, 0:2, :].astype(f32)
    own, other = halves(channels)
    keep_ref[...] = total_ref[:, :, own]
    give_ref[...] = total_ref[:, :, other]


def halves(channels):
    half = channels // 2
    odd = lax.axis_index("seq") % 2
    return span(odd * half, half), span((1 - odd) * half, half)


def first_products(tail, heads, taps):
    def filtered(which):
        before, after = tail[which], heads[which - 1]
        middle = jnp.concatenate([before[1:2], after[0:1]], axis=0)
        planes = (before, middle, after)
        return sum(taps[tap, which : which + 1] * planes[tap] for tap in range(3))

    return filtered(1) * filtered(2)


def extra_state(products, back):
    first, second = products[0:1], products[1:2]
    return times(back, (second * back[0] + first, second * back[1]))


def fixed_rows(products, tail, taps, skip, gain, back):
    jump = sum(gain[0, pole : pole + 1] * back[0][pole : pole + 1] - gain[1, pole : pole + 1] * back[1][pole : pole + 1]
               for pole in range(POLES))
    none = jnp.zeros_like(jump)
    local = skip * products - jnp.concatenate([jump * products[1:2], none], axis=0)
    query = taps[0, 0:1] * tail[0] + jnp.concatenate([taps[1, 0:1] * tail[0][1:2], none], axis=0)
    return local, query


def planes_of(ref, start, stop):
    return [ref[i].astype(f32) for i in range(start, stop)]


def pick(condition, a, b):
    return tuple(jnp.where(condition, x, y) for x, y in zip(a, b))


def mixed(value):
    return jnp.concatenate([value[0:1] + value[1:2], value[0:1] - value[1:2]], axis=0)


def put_wire(wire_ref, value):
    for part in range(2):
        wire_ref[part] = mixed(value[part]).astype(bf16)


def from_wire(wire_ref):
    return tuple(0.5 * mixed(wire_ref[part].astype(f32)) for part in range(2))


ALL = slice(None)


def merge_kernel(own_ref, mate_ref, power_ref, taps_ref, gain_ref, skip_ref,
                 joined_ref, wire_ref, lead_ref, enter_ref, base_ref, fix_ref, head_ref, *, channels):
    device = lax.axis_index("seq")
    odd = device % 2 == 1
    half = halves(channels)[0]
    taps, gain, skip = taps_ref[:, :, half], gain_ref[:, :, half], skip_ref[:, half]
    power, back = pair_at(power_ref, SPAN, half), pair_at(power_ref, BACK, half)
    mine, mates = planes_of(own_ref, 2, 7), planes_of(mate_ref, 2, 7)
    even_edge, odd_edge = pick(odd, mates, mine), pick(odd, mine, mates)
    own, mate = pair_at(own_ref, 0, ALL), pair_at(mate_ref, 0, ALL)
    even_total, odd_total = pick(odd, mate, own), pick(odd, own, mate)
    products = first_products(even_edge[0:3], odd_edge[3:5], taps)
    base = plus(even_total, extra_state(products, back))
    put_pair(base_ref, 0, ALL, base)
    fix_ref[0], fix_ref[1] = fixed_rows(products, even_edge[0:3], taps, skip, gain, back)
    start = extra_state(first_products([jnp.zeros_like(power[0])] * 3, even_edge[3:5], taps), back)
    enter = tuple(jnp.where(device < 2, part, 0.0) for part in start)
    put_pair(enter_ref, 0, ALL, enter)
    joined = plus(odd_total, times(power, plus(base, times(power, enter))))
    put_pair(joined_ref, 0, ALL, joined)
    put_pair(lead_ref, 0, ALL, (jnp.ones_like(power[0]), jnp.zeros_like(power[0])))
    put_wire(wire_ref, joined)
    for i in range(3):
        wire_ref[2 + i] = odd_edge[i].astype(bf16)
    for i in range(2):
        head = even_edge[3 + i].astype(bf16)
        head_ref[i] = head
        wire_ref[5 + i] = head


def step_of(level, sent_ref, got_ref, own_head, power_ref, taps_ref, lead_ref, enter_ref, tail_before, half):
    device = lax.axis_index("seq")
    upper = (device >> level) % 2 == 1
    leads = jnp.logical_and(upper, (device % (1 << level)) < 2)
    back = pair_at(power_ref, BACK, half)
    early_tail = pick(upper, planes_of(got_ref, 2, 5), planes_of(sent_ref, 2, 5))
    late_head = own_head
    if got_ref.shape[0] > 5:
        late_head = pick(upper, own_head, planes_of(got_ref, 5, 7))
    extra = extra_state(first_products(early_tail, late_head, taps_ref[:, :, half]), back)
    other = from_wire(got_ref)
    lead, enter = pair_at(lead_ref, 0, ALL), pair_at(enter_ref, 0, ALL)
    enter = pick(upper, plus(enter, times(lead, plus(other, extra))), enter)
    return upper, other, extra, lead, enter, pick(leads, early_tail, tail_before)


def join_kernel(ending_ref, sent_ref, got_ref, head_ref, power_ref, taps_ref, lead_ref, enter_ref, before_ref, after_ref,
                joined_ref, wire_ref, next_head_ref, next_lead_ref, next_enter_ref, next_before_ref, *, level, channels):
    half = halves(channels)[0]
    own_head = planes_of(head_ref, 0, 2)
    upper, other, extra, lead, enter, before = step_of(
        level, sent_ref, got_ref, own_head, power_ref, taps_ref, lead_ref, enter_ref, planes_of(before_ref, 0, 3), half)
    factor = pair_at(power_ref, SPAN + level, half)
    mine = pair_at(ending_ref, 0, ALL)
    early, late = pick(upper, other, mine), pick(upper, mine, other)
    joined = plus(times(factor, plus(early, extra)), late)
    put_pair(joined_ref, 0, ALL, joined)
    put_wire(wire_ref, joined)
    for i, plane in enumerate(pick(upper, planes_of(sent_ref, 2, 5), planes_of(got_ref, 2, 5))):
        wire_ref[2 + i] = plane.astype(bf16)
    for i, plane in enumerate(pick(upper, planes_of(got_ref, 5, 7), own_head)):
        head = plane.astype(bf16)
        next_head_ref[i] = head
        if wire_ref.shape[0] > 5:
            wire_ref[5 + i] = head
    put_pair(next_lead_ref, 0, ALL, pick(upper, times(lead, factor), lead))
    put_pair(next_enter_ref, 0, ALL, enter)
    for i in range(3):
        next_before_ref[i] = before[i].astype(bf16)


def join_blocks(early, late, factor, back, taps):
    extra = extra_state(first_products(early[2:5], late[5:7], taps), back)
    begin = plus(early[0:2], extra)
    return [*plus(times(factor, begin), late[0:2]), *late[2:5], *early[5:7]], begin


def quad_kernel(ending_ref, sent_ref, near_ref, far_ref, both_ref, power_ref, taps_ref, lead_ref, enter_ref,
                before_ref, after_ref, joined_ref, wire_ref, next_head_ref, next_lead_ref, next_enter_ref,
                next_before_ref, *, level, channels):
    device = lax.axis_index("seq")
    half = halves(channels)[0]
    back, taps = pair_at(power_ref, BACK, half), taps_ref[:, :, half]
    near, far, both = ([*from_wire(ref), *planes_of(ref, 2, 7)] for ref in (near_ref, far_ref, both_ref))
    mine = [*pair_at(ending_ref, 0, ALL), *planes_of(sent_ref, 2, 7)]
    lead, enter, before = pair_at(lead_ref, 0, ALL), pair_at(enter_ref, 0, ALL), planes_of(before_ref, 0, 3)
    upper = (device >> level) % 2 == 1
    factor = pair_at(power_ref, SPAN + level, half)
    other, _ = join_blocks(pick(upper, both, far), pick(upper, far, both), factor, back, taps)
    for step in range(2):
        upper = (device >> (level + step)) % 2 == 1
        leads = jnp.logical_and(upper, (device % (1 << (level + step))) < 2)
        factor = pair_at(power_ref, SPAN + level + step, half)
        across = other if step else near
        early = pick(upper, across, mine)
        mine, begin = join_blocks(early, pick(upper, mine, across), factor, back, taps)
        enter = pick(upper, plus(enter, times(lead, begin)), enter)
        lead = pick(upper, times(lead, factor), lead)
        before = pick(leads, early[2:5], before)
    put_pair(joined_ref, 0, ALL, mine[0:2])
    put_wire(wire_ref, mine[0:2])
    for i in range(3):
        wire_ref[2 + i] = mine[2 + i].astype(bf16)
        next_before_ref[i] = before[i].astype(bf16)
    for i in range(2):
        head = mine[5 + i].astype(bf16)
        next_head_ref[i] = head
        if wire_ref.shape[0] > 5:
            wire_ref[5 + i] = head
    put_pair(next_lead_ref, 0, ALL, lead)
    put_pair(next_enter_ref, 0, ALL, enter)


def last_kernel(sent_ref, got_ref, head_ref, power_ref, taps_ref, gain_ref, skip_ref, lead_ref, enter_ref, before_ref,
                base_ref, fix_ref, first_ref, after_ref, keep_ref, give_ref, *, level, channels):
    half = halves(channels)[0]
    odd = lax.axis_index("seq") % 2 == 1
    _, _, _, _, enter, before = step_of(
        level, sent_ref, got_ref, planes_of(head_ref, 0, 2), power_ref, taps_ref, lead_ref, enter_ref,
        planes_of(before_ref, 0, 3), half)
    taps, gain, skip = taps_ref[:, :, half], gain_ref[:, :, half], skip_ref[:, half]
    power, back = pair_at(power_ref, SPAN, half), pair_at(power_ref, BACK, half)
    products = first_products(before, planes_of(first_ref, 0, 2), taps)
    even = [*enter, *fixed_rows(products, before, taps, skip, gain, back)]
    odds = [*plus(times(power, enter), pair_at(base_ref, 0, ALL)), fix_ref[0], fix_ref[1]]
    for i, (a, b) in enumerate(zip(even, odds)):
        keep_ref[i] = jnp.where(odd, b, a)
        give_ref[i] = jnp.where(odd, a, b)


def local_kernel(taps_ref, gain_ref, skip_ref, power_ref, scan_ref, prod_ref, q_ref, after_ref, part_ref,
                 query_ref, local_ref, enter_ref, order_ref, qs_ref, *, base):
    rows, channels = query_ref.shape
    chunk = qs_ref.shape[1]
    order_ref[...] = order_matrix(rows, False)

    def body(i, _):
        qs_ref[...] = jnp.dot(order_ref[...], q_ref[:, span(base + i * chunk, chunk)], preferred_element_type=f32)

        def column(inner, outer):
            cols = slice(inner, inner + WIDTH)
            put = span(outer, WIDTH)
            here = span(base + outer, WIDTH)
            queries = short_filter(steps_of(qs_ref, cols), taps_ref, 0, here)
            for j, value in enumerate(queries):
                query_ref[SEGMENTS * j : SEGMENTS * (j + 1), put] = value
            products = []
            for j in range(0, len(queries), 2):
                both = prod_ref[SEGMENTS * j : SEGMENTS * (j + 2), here].astype(f32)
                products += [both[:SEGMENTS], both[SEGMENTS:]]
            before = delayed(products[-1])
            skip = wide(skip_ref[0:1, here])
            sublane = lax.broadcasted_iota(jnp.int32, (SEGMENTS, WIDTH), 0)
            coefs = []
            for pole in range(POLES):
                lam = pole_at(power_ref, LAM, pole, here)
                back = pole_at(power_ref, BACK, pole, here)
                gain = tuple(wide(gain_ref[part, pole : pole + 1, here]) for part in range(2))
                a1, a2 = feedback(lam)
                b1 = gain[0] * lam[0] + gain[1] * lam[1]
                carry = tuple(delayed(scan_ref[2 * part + pole, :, here]) for part in range(2))
                gain_back = times(gain, back)
                y1 = gain[0] * carry[0] - gain[1] * carry[1]
                y2 = gain_back[0] * (carry[0] - before) - gain_back[1] * carry[1]
                coefs.append([a1, a2, gain[0], b1, y1, y2])
                reach = gain
                for level in range(3):
                    factor = pole_at(power_ref, SEGMENT + level, pole, here)
                    bit = (sublane // (1 << level)) % 2 == 1
                    reach = times(reach, (jnp.where(bit, factor[0], 1.0), jnp.where(bit, factor[1], 0.0)))
                for part in range(2):
                    enter_ref[2 * part + pole, :, put] = reach[part]
            previous = before
            for j, value in enumerate(products):
                total = skip * value
                for pole in range(POLES):
                    a1, a2, b0, b1, y1, y2 = coefs[pole]
                    y = a1 * y1 - a2 * y2 + (b0 * value - b1 * previous)
                    coefs[pole][4:] = [y, y1]
                    total = total + y
                previous = value
                local_ref[SEGMENTS * j : SEGMENTS * (j + 1), put] = total

        loop_columns(i, chunk, column)
        return 0

    lax.fori_loop(0, channels // chunk, body, 0)


def gate_kernel(power_ref, state_ref, *rest, parts, ready):
    count = 3 * len(parts)
    tables, rest = rest[:count], rest[count:]
    if ready:
        ready_ref, out_hbm, order_ref, out_ref, gated_ref, out_sem = rest
    else:
        out_ref, order_ref, gated_ref = rest
    half = out_ref.shape[1]
    chunk = gated_ref.shape[1]
    own, other = halves(2 * half)
    odd = lax.axis_index("seq") % 2
    side = 1 - odd if ready else odd
    begin = side * half

    def send(i):
        place = span(i * chunk, chunk)
        return pltpu.make_async_copy(
            out_ref.at[:, place], out_hbm.at[:, span(begin + i * chunk, chunk)], out_sem.at[i])

    if ready:
        finished = pltpu.make_async_copy(ready_ref, out_hbm.at[:, own], out_sem.at[half // chunk])
        finished.start()
    order_ref[...] = order_matrix(gated_ref.shape[0], True)

    def gate_part(base, part, query_ref, local_ref, reach_ref):
        def body(i, _):
            def column(inner, outer):
                cols = slice(inner, inner + WIDTH)
                take = span(outer, WIDTH)
                there = span(base % half + outer, WIDTH)
                here = span(base + outer, WIDTH)
                queries = steps_of(query_ref, take)
                local = steps_of(local_ref, take)
                for j in range(2):
                    local[j] = local[j] + jnp.where(first_mask(), wide(state_ref[2, j : j + 1, there]), 0.0)
                    queries[j] = queries[j] + jnp.where(first_mask(), wide(state_ref[3, j : j + 1, there]), 0.0)
                coefs = []
                for pole in range(POLES):
                    lam = pole_at(power_ref, LAM, pole, here)
                    back = pole_at(power_ref, BACK, pole, here)
                    state = times(pole_at(state_ref, 0, pole, there), (reach_ref[pole, :, take], reach_ref[2 + pole, :, take]))
                    y2 = state[0] * back[0] - state[1] * back[1]
                    coefs.append([*feedback(lam), state[0], y2])
                gated = []
                for j in range(len(queries)):
                    total = local[j]
                    for pole in range(POLES):
                        a1, a2, y1, y2 = coefs[pole]
                        y = a1 * y1 - a2 * y2
                        coefs[pole][2:] = [y, y1]
                        total = total + y
                    gated.append(queries[j] * total)
                    if j % 2:
                        both = jnp.concatenate(gated[-2:], axis=0)
                        gated_ref[SEGMENTS * (j - 1) : SEGMENTS * (j + 1), cols] = both.astype(bf16)

            loop_columns(i, chunk, column)
            place = base % half // chunk + i
            out_ref[:, span(place * chunk, chunk)] = jnp.dot(
                order_ref[...], gated_ref[...], preferred_element_type=f32).astype(bf16)
            if ready:
                send(place).start()
            return 0

        lax.fori_loop(0, part // chunk, body, 0)

    base = 0
    for index, part in enumerate(parts):

        @pl.when(side == base // half)
        def _(base=base, part=part, refs=tables[3 * index : 3 * index + 3]):
            gate_part(base, part, *refs)

        base += part
    if ready:
        for i in range(half // chunk):
            send(i).wait()
        finished.wait()


def kernel_call(body, name, outs, scratch, operands, in_hbm, out_hbm=(), **options):
    def spec(far):
        return pl.BlockSpec(memory_space=pltpu.HBM if far else pltpu.VMEM)

    def bound(*refs):
        return body(*refs, **options)

    return pl.pallas_call(
        bound,
        in_specs=[spec(i in in_hbm) for i in range(len(operands))],
        out_specs=[spec(i in out_hbm) for i in range(len(outs))],
        out_shape=[jax.ShapeDtypeStruct(shape, dtype) for shape, dtype in outs],
        scratch_shapes=scratch,
        compiler_params=pltpu.CompilerParams(vmem_limit_bytes=32 << 20),
        name=name,
    )(*operands)


def on_device(projected, short_taps, skip_gain, residues, pole_angles, decay_rates):
    _, rows, channels = projected.shape
    chunk = min(CHUNK, channels)
    devices = lax.axis_size("seq")
    levels = devices.bit_length() - 1
    parts = [channels // sum(PARTS) * share for share in PARTS]
    arguments = [pole_angles, decay_rates, short_taps, residues, skip_gain[None], projected]
    arguments = [pltpu.with_memory_space_constraint(argument, pltpu.HBM) for argument in arguments]
    half = channels // 2
    local_chunk = min(LOCAL_CHUNK, channels)
    wide_chunk = min(STATES_CHUNK, channels)
    square = pltpu.VMEM((rows, rows), bf16)
    dma = pltpu.SemaphoreType.DMA

    def pairs(count, dtype=f32, extent=half):
        return (count, POLES, extent), dtype

    state = pairs(2)
    products, scan, keep, give, powers, taps, gains, skip, query_rows = kernel_call(
        states_kernel, "states",
        [((rows, channels), bf16), ((4, SEGMENTS, channels), f32), pairs(7), pairs(7),
         pairs(2 * (SPAN + levels), f32, channels), (short_taps.shape, f32), (residues.shape, f32),
         ((1, channels), f32), ((rows, channels), bf16)],
        [pltpu.VMEM(*pairs(7, f32, channels)), square]
        + [pltpu.VMEM(pole_angles.shape, f32)] * 2 + [pltpu.VMEM((2, rows, channels), bf16)]
        + [pltpu.VMEM((rows, wide_chunk), f32)] * 2 + [dma((6,)), dma((channels // wide_chunk,))],
        arguments, range(6), levels=levels)

    def exchange(array, mask):
        return lax.ppermute(array, "seq", [(i, i ^ mask) for i in range(devices)])

    def message(level):
        return pairs(5 if level == levels - 1 else 7, bf16)

    got = exchange(give, 1)
    ending, sent, lead, enter, base, fix, first = kernel_call(
        merge_kernel, "merge", [state, pairs(7, bf16), state, state, state, state, pairs(2, bf16)], [],
        [keep, got, powers, taps, gains, skip], (), channels=channels)
    head = first
    before = jnp.zeros(*pairs(3, bf16))

    tables = []

    def run_local(until):
        while len(tables) < min(until, len(parts)):
            part = parts[len(tables)]
            plane = ((rows, part), f32)
            tables.append(kernel_call(
                local_kernel, "local", [plane, plane, ((4, SEGMENTS, part), f32)],
                [square, pltpu.VMEM((rows, local_chunk), f32)],
                [taps, gains, skip, powers, scan, products, query_rows, ending, tables[-1][2] if tables else ending], (7, 8), base=sum(parts[: len(tables)])))
        return tables[-1][2]

    level = 1
    if levels > 3:
        near, far, both = (exchange(sent, mask << level) for mask in (1, 2, 3))
        after = run_local(2)
        level = 3
        ending, sent, head, lead, enter, before = kernel_call(
            quad_kernel, "quad", [state, message(level), pairs(2, bf16), state, state, pairs(3, bf16)], [],
            [ending, sent, near, far, both, powers, taps, lead, enter, before, after], (10,),
            level=1, channels=channels)
    while level < levels:
        got = exchange(sent, 1 << level)
        after = run_local(len(parts) if level == levels - 1 else level)
        level += 1
        if level < levels:
            ending, sent, head, lead, enter, before = kernel_call(
                join_kernel, "join", [state, message(level), pairs(2, bf16), state, state, pairs(3, bf16)], [],
                [ending, sent, got, head, powers, taps, lead, enter, before, after], (9,), level=level - 1,
                channels=channels)

    keep, give = kernel_call(
        last_kernel, "last", [pairs(4)] * 2, [],
        [sent, got, head, powers, taps, gains, skip, lead, enter, before, base, fix, first, after], (13,),
        level=levels - 1, channels=channels)
    got = exchange(give, 1)
    flat = [array for table in tables for array in table]
    half_plane = ((rows, half), bf16)
    scratch = [square, pltpu.VMEM(*half_plane), pltpu.VMEM((rows, chunk), bf16), dma((half // chunk + 1,))]
    (ready,) = kernel_call(
        gate_kernel, "gate", [half_plane], [square, scratch[2]], [powers, keep, *flat], (), parts=parts, ready=False)
    (out,) = kernel_call(
        gate_kernel, "finish", [((rows, channels), bf16)], scratch, [powers, got, *flat, ready], (), (0,),
        parts=parts, ready=True)
    return out


def solution(mesh):
    return jax.shard_map(
        on_device,
        mesh=mesh,
        in_specs=(P(None, ("grp", "seq"), None), P(), P(), P(), P(), P()),
        out_specs=P(("grp", "seq"), None),
        check_vma=False,
    )
```

```python
import jax
import jax.numpy as jnp
from jax import lax
from jax.experimental import pallas as pl
from jax.experimental.pallas import tpu as pltpu
from jax.sharding import PartitionSpec as P

SEGMENTS = 8
WIDTH = 256
CHUNK = 1024
POLES = 2
SUBROWS = 16
LOCAL_CHUNK = 512
STATES_CHUNK = 1024
PARTS = ((False, 0, 2), (True, 0, 1), (True, 1, 1))
f32 = jnp.float32
bf16 = jnp.bfloat16

LAM, BACK, SEGMENT, SPAN = 0, 1, 2, 5


def order_matrix(row_count, inverse):
    length = row_count // SEGMENTS
    ordered = lax.broadcasted_iota(jnp.int32, (row_count, row_count), 1 if inverse else 0)
    natural = lax.broadcasted_iota(jnp.int32, (row_count, row_count), 0 if inverse else 1)
    wanted = length * (ordered % SEGMENTS) + ordered // SEGMENTS
    return (wanted == natural).astype(f32).astype(bf16)


def wide(value):
    return jnp.broadcast_to(value, (SEGMENTS, value.shape[1]))


def times(a, b):
    return (a[0] * b[0] - a[1] * b[1], a[0] * b[1] + a[1] * b[0])


def plus(a, b):
    return (a[0] + b[0], a[1] + b[1])


def pair_at(ref, index, cols):
    return (ref[2 * index, :, cols], ref[2 * index + 1, :, cols])


def put_pair(ref, index, cols, value):
    ref[2 * index, :, cols] = value[0]
    ref[2 * index + 1, :, cols] = value[1]


def pole_at(ref, index, pole, cols):
    return (wide(ref[2 * index, pole : pole + 1, cols]), wide(ref[2 * index + 1, pole : pole + 1, cols]))


def half_angle(angle):
    x = 0.5 * angle
    u = x * x
    sine = 1.0 / 6227020800.0
    for term in (-1.0 / 39916800.0, 1.0 / 362880.0, -1.0 / 5040.0, 1.0 / 120.0, -1.0 / 6.0, 1.0):
        sine = sine * u + term
    cosine = -1.0 / 87178291200.0
    for term in (1.0 / 479001600.0, -1.0 / 3628800.0, 1.0 / 40320.0, -1.0 / 720.0, 1.0 / 24.0, -0.5, 1.0):
        cosine = cosine * u + term
    return cosine, sine * x


def fill_powers(power_ref, angle_ref, decay_ref, length, levels):
    cols = slice(None)
    cosine, sine = half_angle(angle_ref[...])
    turn = (1.0 - 2.0 * sine * sine, 2.0 * sine * cosine)
    decay = decay_ref[...]
    damping = jnp.exp(-decay)
    growth = jnp.exp(decay)
    value = (damping * turn[0], damping * turn[1])
    put_pair(power_ref, LAM, cols, value)
    put_pair(power_ref, BACK, cols, (growth * turn[0], -growth * turn[1]))
    for _ in range(length.bit_length() - 1):
        value = times(value, value)
    for level in range(3 + levels):
        put_pair(power_ref, SEGMENT + level, cols, value)
        value = times(value, value)


def steps_of(ref, cols):
    return [ref[SEGMENTS * j : SEGMENTS * (j + 1), cols] for j in range(ref.shape[0] // SEGMENTS)]


def first_mask():
    return lax.broadcasted_iota(jnp.int32, (SEGMENTS, WIDTH), 0) == 0


def delayed(value):
    return jnp.where(first_mask(), 0.0, pltpu.roll(value, 1, 0))


def short_filter(steps, taps_ref, which, cols):
    taps = [wide(taps_ref[tap, which : which + 1, cols]) for tap in range(3)]
    padded = [delayed(steps[-2]), delayed(steps[-1])] + steps
    return [
        taps[0] * padded[j] + taps[1] * padded[j + 1] + taps[2] * padded[j + 2]
        for j in range(len(steps))
    ]


def feedback(lam):
    return 2.0 * lam[0], lam[0] * lam[0] + lam[1] * lam[1]


def span(start, size):
    return pl.ds(pl.multiple_of(start, 128), size)


def loop_columns(chunk_index, chunk, body):
    for part in range(chunk // WIDTH):
        body(part * WIDTH, chunk_index * chunk + part * WIDTH)


def side_start(theirs, half):
    odd = lax.axis_index("seq") % 2
    return (1 - odd if theirs else odd) * half


def half_states(ready, begin, order_ref, power_ref, taps_ref, kv_ref, q_ref, prod_ref, scan_ref, block_ref, ks_ref, vs_ref):
    _, rows, _ = kv_ref.shape
    half = prod_ref.shape[1]
    chunk = ks_ref.shape[1]

    def body(i, _):
        ready(i)
        at = span(begin + i * chunk, chunk)
        ks_ref[...] = jnp.dot(order_ref[...], kv_ref[0, :, at], preferred_element_type=f32)
        vs_ref[...] = jnp.dot(order_ref[...], kv_ref[1, :, at], preferred_element_type=f32)

        def column(inner, outer):
            cols = slice(inner, inner + WIDTH)
            here = span(begin + outer, WIDTH)
            put = span(outer, WIDTH)
            keys = short_filter(steps_of(ks_ref, cols), taps_ref, 1, here)
            values = short_filter(steps_of(vs_ref, cols), taps_ref, 2, here)
            products = [a * b for a, b in zip(keys, values)]
            for j in range(2):
                products[j] = jnp.where(first_mask(), 0.0, products[j])
            for j in range(0, len(products), 2):
                both = jnp.concatenate(products[j : j + 2], axis=0)
                prod_ref[SEGMENTS * j : SEGMENTS * (j + 2), put] = both.astype(bf16)
            sublane = lax.broadcasted_iota(jnp.int32, (SEGMENTS, WIDTH), 0)
            for pole in range(POLES):
                lam = pole_at(power_ref, LAM, pole, here)
                a1, a2 = feedback(lam)
                late = products[0]
                now = a1 * late + products[1]
                for value in products[2:]:
                    late, now = now, a1 * now - a2 * late + value
                state = (now - lam[0] * late, lam[1] * late)
                for level in range(3):
                    by = 1 << level
                    factor = pole_at(power_ref, SEGMENT + level, pole, here)
                    moved = tuple(jnp.where(sublane >= by, pltpu.roll(part, by, 0), 0.0) for part in state)
                    state = plus(state, times(factor, moved))
                for part in range(2):
                    scan_ref[2 * part + pole, :, put] = state[part]
                    block_ref[part, pole : pole + 1, put] = state[part][SEGMENTS - 1 :]

        loop_columns(i, chunk, column)
        return 0

    lax.fori_loop(0, half // chunk, body, 0)


def put_edges(begin, kv_ref, q_ref, block_ref):
    _, rows, _ = kv_ref.shape
    here = span(begin, block_ref.shape[2])
    last = slice(rows - SUBROWS, rows)
    for which, tail in enumerate((q_ref[last, here], kv_ref[0, last, here], kv_ref[1, last, here])):
        block_ref[2 + which] = tail[SUBROWS - 2 :].astype(f32)
    for which in range(2):
        block_ref[5 + which] = kv_ref[which, 0:SUBROWS, here][0:2].astype(f32)


def first_kernel(angle_hbm, decay_hbm, taps_hbm, gain_hbm, skip_hbm, proj_ref,
                 prod_ref, scan_ref, give_ref, power_ref, taps_ref, gain_ref, skip_ref, kv_ref, q_ref,
                 order_ref, angle_ref, decay_ref, ks_ref, vs_ref, small_sem, in_sem, *, levels):
    _, rows, channels = kv_ref.shape
    half = channels // 2
    chunk = ks_ref.shape[1]
    count = half // chunk
    begin, rest = side_start(True, half), side_start(False, half)
    smalls = [
        pltpu.make_async_copy(source, target, small_sem.at[i])
        for i, (source, target) in enumerate([
            (angle_hbm, angle_ref), (decay_hbm, decay_ref), (taps_hbm, taps_ref), (proj_ref.at[0], q_ref),
            (gain_hbm, gain_ref), (skip_hbm, skip_ref)])
    ]

    def fetch(start, size, which):
        cols = span(start, size)
        return pltpu.make_async_copy(proj_ref.at[pl.ds(1, 2), :, cols], kv_ref.at[:, :, cols], in_sem.at[which])

    for copy in smalls[:3]:
        copy.start()
    for i in range(count):
        fetch(begin + i * chunk, chunk, i).start()
    for copy in smalls[3:]:
        copy.start()
    fetch(rest, half, count).start()
    order_ref[...] = order_matrix(rows, False)
    for copy in smalls[:3]:
        copy.wait()
    fill_powers(power_ref, angle_ref, decay_ref, rows // SEGMENTS, levels)
    half_states(lambda i: fetch(begin + i * chunk, chunk, i).wait(), begin, order_ref, power_ref, taps_ref,
                kv_ref, q_ref, prod_ref, scan_ref, give_ref, ks_ref, vs_ref)
    for copy in smalls[3:]:
        copy.wait()
    fetch(rest, half, count).wait()
    put_edges(begin, kv_ref, q_ref, give_ref)


def second_kernel(power_ref, taps_ref, kv_ref, q_ref, prod_ref, scan_ref, keep_ref, order_ref, ks_ref, vs_ref):
    _, rows, channels = kv_ref.shape
    begin = side_start(False, channels // 2)
    order_ref[...] = order_matrix(rows, False)
    half_states(lambda i: None, begin, order_ref, power_ref, taps_ref, kv_ref, q_ref, prod_ref, scan_ref, keep_ref,
                ks_ref, vs_ref)
    put_edges(begin, kv_ref, q_ref, keep_ref)


def halves(channels):
    half = channels // 2
    odd = lax.axis_index("seq") % 2
    return span(odd * half, half), span((1 - odd) * half, half)


def first_products(tail, heads, taps):
    def filtered(which):
        before, after = tail[which], heads[which - 1]
        middle = jnp.concatenate([before[1:2], after[0:1]], axis=0)
        planes = (before, middle, after)
        return sum(taps[tap, which : which + 1] * planes[tap] for tap in range(3))

    return filtered(1) * filtered(2)


def extra_state(products, back):
    first, second = products[0:1], products[1:2]
    return times(back, (second * back[0] + first, second * back[1]))


def fixed_rows(products, tail, taps, skip, gain, back):
    jump = sum(gain[0, pole : pole + 1] * back[0][pole : pole + 1] - gain[1, pole : pole + 1] * back[1][pole : pole + 1]
               for pole in range(POLES))
    none = jnp.zeros_like(jump)
    local = skip * products - jnp.concatenate([jump * products[1:2], none], axis=0)
    query = taps[0, 0:1] * tail[0] + jnp.concatenate([taps[1, 0:1] * tail[0][1:2], none], axis=0)
    return local, query


def planes_of(ref, start, stop):
    return [ref[i].astype(f32) for i in range(start, stop)]


def pick(condition, a, b):
    return tuple(jnp.where(condition, x, y) for x, y in zip(a, b))


def mixed(value):
    return jnp.concatenate([value[0:1] + value[1:2], value[0:1] - value[1:2]], axis=0)


def put_wire(wire_ref, value):
    for part in range(2):
        wire_ref[part] = mixed(value[part]).astype(bf16)


def from_wire(wire_ref):
    return tuple(0.5 * mixed(wire_ref[part].astype(f32)) for part in range(2))


ALL = slice(None)


def merge_kernel(own_ref, mate_ref, power_ref, taps_ref, gain_ref, skip_ref,
                 joined_ref, wire_ref, lead_ref, enter_ref, base_ref, fix_ref, head_ref, *, channels):
    device = lax.axis_index("seq")
    odd = device % 2 == 1
    half = halves(channels)[0]
    taps, gain, skip = taps_ref[:, :, half], gain_ref[:, :, half], skip_ref[:, half]
    power, back = pair_at(power_ref, SPAN, half), pair_at(power_ref, BACK, half)
    mine, mates = planes_of(own_ref, 2, 7), planes_of(mate_ref, 2, 7)
    even_edge, odd_edge = pick(odd, mates, mine), pick(odd, mine, mates)
    own, mate = pair_at(own_ref, 0, ALL), pair_at(mate_ref, 0, ALL)
    even_total, odd_total = pick(odd, mate, own), pick(odd, own, mate)
    products = first_products(even_edge[0:3], odd_edge[3:5], taps)
    base = plus(even_total, extra_state(products, back))
    put_pair(base_ref, 0, ALL, base)
    fix_ref[0], fix_ref[1] = fixed_rows(products, even_edge[0:3], taps, skip, gain, back)
    start = extra_state(first_products([jnp.zeros_like(power[0])] * 3, even_edge[3:5], taps), back)
    enter = tuple(jnp.where(device < 2, part, 0.0) for part in start)
    put_pair(enter_ref, 0, ALL, enter)
    joined = plus(odd_total, times(power, plus(base, times(power, enter))))
    put_pair(joined_ref, 0, ALL, joined)
    put_pair(lead_ref, 0, ALL, (jnp.ones_like(power[0]), jnp.zeros_like(power[0])))
    put_wire(wire_ref, joined)
    for i in range(3):
        wire_ref[2 + i] = odd_edge[i].astype(bf16)
    for i in range(2):
        head = even_edge[3 + i].astype(bf16)
        head_ref[i] = head
        wire_ref[5 + i] = head


def step_of(level, sent_ref, got_ref, own_head, power_ref, taps_ref, lead_ref, enter_ref, tail_before, half):
    device = lax.axis_index("seq")
    upper = (device >> level) % 2 == 1
    leads = jnp.logical_and(upper, (device % (1 << level)) < 2)
    back = pair_at(power_ref, BACK, half)
    early_tail = pick(upper, planes_of(got_ref, 2, 5), planes_of(sent_ref, 2, 5))
    late_head = own_head
    if got_ref.shape[0] > 5:
        late_head = pick(upper, own_head, planes_of(got_ref, 5, 7))
    extra = extra_state(first_products(early_tail, late_head, taps_ref[:, :, half]), back)
    other = from_wire(got_ref)
    lead, enter = pair_at(lead_ref, 0, ALL), pair_at(enter_ref, 0, ALL)
    enter = pick(upper, plus(enter, times(lead, plus(other, extra))), enter)
    return upper, other, extra, lead, enter, pick(leads, early_tail, tail_before)


def join_kernel(ending_ref, sent_ref, got_ref, head_ref, power_ref, taps_ref, lead_ref, enter_ref, before_ref, after_ref,
                joined_ref, wire_ref, next_head_ref, next_lead_ref, next_enter_ref, next_before_ref, *, level, channels):
    half = halves(channels)[0]
    own_head = planes_of(head_ref, 0, 2)
    upper, other, extra, lead, enter, before = step_of(
        level, sent_ref, got_ref, own_head, power_ref, taps_ref, lead_ref, enter_ref, planes_of(before_ref, 0, 3), half)
    factor = pair_at(power_ref, SPAN + level, half)
    mine = pair_at(ending_ref, 0, ALL)
    early, late = pick(upper, other, mine), pick(upper, mine, other)
    joined = plus(times(factor, plus(early, extra)), late)
    put_pair(joined_ref, 0, ALL, joined)
    put_wire(wire_ref, joined)
    for i, plane in enumerate(pick(upper, planes_of(sent_ref, 2, 5), planes_of(got_ref, 2, 5))):
        wire_ref[2 + i] = plane.astype(bf16)
    for i, plane in enumerate(pick(upper, planes_of(got_ref, 5, 7), own_head)):
        head = plane.astype(bf16)
        next_head_ref[i] = head
        if wire_ref.shape[0] > 5:
            wire_ref[5 + i] = head
    put_pair(next_lead_ref, 0, ALL, pick(upper, times(lead, factor), lead))
    put_pair(next_enter_ref, 0, ALL, enter)
    for i in range(3):
        next_before_ref[i] = before[i].astype(bf16)


def join_blocks(early, late, factor, back, taps):
    extra = extra_state(first_products(early[2:5], late[5:7], taps), back)
    begin = plus(early[0:2], extra)
    return [*plus(times(factor, begin), late[0:2]), *late[2:5], *early[5:7]], begin


def quad_kernel(ending_ref, sent_ref, near_ref, far_ref, both_ref, power_ref, taps_ref, lead_ref, enter_ref,
                before_ref, after_ref, joined_ref, wire_ref, next_head_ref, next_lead_ref, next_enter_ref,
                next_before_ref, *, level, channels):
    device = lax.axis_index("seq")
    half = halves(channels)[0]
    back, taps = pair_at(power_ref, BACK, half), taps_ref[:, :, half]
    near, far, both = ([*from_wire(ref), *planes_of(ref, 2, 7)] for ref in (near_ref, far_ref, both_ref))
    mine = [*pair_at(ending_ref, 0, ALL), *planes_of(sent_ref, 2, 7)]
    lead, enter, before = pair_at(lead_ref, 0, ALL), pair_at(enter_ref, 0, ALL), planes_of(before_ref, 0, 3)
    upper = (device >> level) % 2 == 1
    factor = pair_at(power_ref, SPAN + level, half)
    other, _ = join_blocks(pick(upper, both, far), pick(upper, far, both), factor, back, taps)
    for step in range(2):
        upper = (device >> (level + step)) % 2 == 1
        leads = jnp.logical_and(upper, (device % (1 << (level + step))) < 2)
        factor = pair_at(power_ref, SPAN + level + step, half)
        across = other if step else near
        early = pick(upper, across, mine)
        mine, begin = join_blocks(early, pick(upper, mine, across), factor, back, taps)
        enter = pick(upper, plus(enter, times(lead, begin)), enter)
        lead = pick(upper, times(lead, factor), lead)
        before = pick(leads, early[2:5], before)
    put_pair(joined_ref, 0, ALL, mine[0:2])
    put_wire(wire_ref, mine[0:2])
    for i in range(3):
        wire_ref[2 + i] = mine[2 + i].astype(bf16)
        next_before_ref[i] = before[i].astype(bf16)
    for i in range(2):
        head = mine[5 + i].astype(bf16)
        next_head_ref[i] = head
        if wire_ref.shape[0] > 5:
            wire_ref[5 + i] = head
    put_pair(next_lead_ref, 0, ALL, lead)
    put_pair(next_enter_ref, 0, ALL, enter)


def last_kernel(sent_ref, got_ref, head_ref, power_ref, taps_ref, gain_ref, skip_ref, lead_ref, enter_ref, before_ref,
                base_ref, fix_ref, first_ref, after_ref, keep_ref, give_ref, *, level, channels):
    half = halves(channels)[0]
    odd = lax.axis_index("seq") % 2 == 1
    _, _, _, _, enter, before = step_of(
        level, sent_ref, got_ref, planes_of(head_ref, 0, 2), power_ref, taps_ref, lead_ref, enter_ref,
        planes_of(before_ref, 0, 3), half)
    taps, gain, skip = taps_ref[:, :, half], gain_ref[:, :, half], skip_ref[:, half]
    power, back = pair_at(power_ref, SPAN, half), pair_at(power_ref, BACK, half)
    products = first_products(before, planes_of(first_ref, 0, 2), taps)
    even = [*enter, *fixed_rows(products, before, taps, skip, gain, back)]
    odds = [*plus(times(power, enter), pair_at(base_ref, 0, ALL)), fix_ref[0], fix_ref[1]]
    for i, (a, b) in enumerate(zip(even, odds)):
        keep_ref[i] = jnp.where(odd, b, a)
        give_ref[i] = jnp.where(odd, a, b)


def local_kernel(taps_ref, gain_ref, skip_ref, power_ref, scan_ref, prod_ref, q_ref, after_ref, part_ref,
                 query_ref, local_ref, enter_ref, order_ref, qs_ref, *, theirs, base):
    rows, channels = query_ref.shape
    begin = side_start(theirs, prod_ref.shape[1]) + base
    chunk = qs_ref.shape[1]
    order_ref[...] = order_matrix(rows, False)

    def body(i, _):
        qs_ref[...] = jnp.dot(order_ref[...], q_ref[:, span(begin + i * chunk, chunk)], preferred_element_type=f32)

        def column(inner, outer):
            cols = slice(inner, inner + WIDTH)
            put = span(outer, WIDTH)
            here = span(begin + outer, WIDTH)
            take = span(base + outer, WIDTH)
            queries = short_filter(steps_of(qs_ref, cols), taps_ref, 0, here)
            for j, value in enumerate(queries):
                query_ref[SEGMENTS * j : SEGMENTS * (j + 1), put] = value
            products = []
            for j in range(0, len(queries), 2):
                both = prod_ref[SEGMENTS * j : SEGMENTS * (j + 2), take].astype(f32)
                products += [both[:SEGMENTS], both[SEGMENTS:]]
            before = delayed(products[-1])
            skip = wide(skip_ref[0:1, here])
            sublane = lax.broadcasted_iota(jnp.int32, (SEGMENTS, WIDTH), 0)
            coefs = []
            for pole in range(POLES):
                lam = pole_at(power_ref, LAM, pole, here)
                back = pole_at(power_ref, BACK, pole, here)
                gain = tuple(wide(gain_ref[part, pole : pole + 1, here]) for part in range(2))
                a1, a2 = feedback(lam)
                b1 = gain[0] * lam[0] + gain[1] * lam[1]
                carry = tuple(delayed(scan_ref[2 * part + pole, :, take]) for part in range(2))
                gain_back = times(gain, back)
                y1 = gain[0] * carry[0] - gain[1] * carry[1]
                y2 = gain_back[0] * (carry[0] - before) - gain_back[1] * carry[1]
                coefs.append([a1, a2, gain[0], b1, y1, y2])
                reach = gain
                for level in range(3):
                    factor = pole_at(power_ref, SEGMENT + level, pole, here)
                    bit = (sublane // (1 << level)) % 2 == 1
                    reach = times(reach, (jnp.where(bit, factor[0], 1.0), jnp.where(bit, factor[1], 0.0)))
                for part in range(2):
                    enter_ref[2 * part + pole, :, put] = reach[part]
            previous = before
            for j, value in enumerate(products):
                total = skip * value
                for pole in range(POLES):
                    a1, a2, b0, b1, y1, y2 = coefs[pole]
                    y = a1 * y1 - a2 * y2 + (b0 * value - b1 * previous)
                    coefs[pole][4:] = [y, y1]
                    total = total + y
                previous = value
                local_ref[SEGMENTS * j : SEGMENTS * (j + 1), put] = total

        loop_columns(i, chunk, column)
        return 0

    lax.fori_loop(0, channels // chunk, body, 0)


def gate_kernel(power_ref, state_ref, *rest, parts, ready):
    count = 3 * len(parts)
    tables, rest = rest[:count], rest[count:]
    if ready:
        ready_ref, out_hbm, order_ref, out_ref, gated_ref, out_sem = rest
    else:
        out_ref, order_ref, gated_ref = rest
    half = out_ref.shape[1]
    chunk = gated_ref.shape[1]
    own = halves(2 * half)[0]
    begin = side_start(ready, half)

    def send(i):
        place = span(i * chunk, chunk)
        return pltpu.make_async_copy(
            out_ref.at[:, place], out_hbm.at[:, span(begin + i * chunk, chunk)], out_sem.at[i])

    if ready:
        finished = pltpu.make_async_copy(ready_ref, out_hbm.at[:, own], out_sem.at[half // chunk])
        finished.start()
    order_ref[...] = order_matrix(gated_ref.shape[0], True)

    def gate_part(base, part, query_ref, local_ref, reach_ref):
        def body(i, _):
            def column(inner, outer):
                cols = slice(inner, inner + WIDTH)
                take = span(outer, WIDTH)
                there = span(base + outer, WIDTH)
                here = span(begin + base + outer, WIDTH)
                queries = steps_of(query_ref, take)
                local = steps_of(local_ref, take)
                for j in range(2):
                    local[j] = local[j] + jnp.where(first_mask(), wide(state_ref[2, j : j + 1, there]), 0.0)
                    queries[j] = queries[j] + jnp.where(first_mask(), wide(state_ref[3, j : j + 1, there]), 0.0)
                coefs = []
                for pole in range(POLES):
                    lam = pole_at(power_ref, LAM, pole, here)
                    back = pole_at(power_ref, BACK, pole, here)
                    state = times(pole_at(state_ref, 0, pole, there), (reach_ref[pole, :, take], reach_ref[2 + pole, :, take]))
                    y2 = state[0] * back[0] - state[1] * back[1]
                    coefs.append([*feedback(lam), state[0], y2])
                gated = []
                for j in range(len(queries)):
                    total = local[j]
                    for pole in range(POLES):
                        a1, a2, y1, y2 = coefs[pole]
                        y = a1 * y1 - a2 * y2
                        coefs[pole][2:] = [y, y1]
                        total = total + y
                    gated.append(queries[j] * total)
                    if j % 2:
                        both = jnp.concatenate(gated[-2:], axis=0)
                        gated_ref[SEGMENTS * (j - 1) : SEGMENTS * (j + 1), cols] = both.astype(bf16)

            loop_columns(i, chunk, column)
            place = base // chunk + i
            out_ref[:, span(place * chunk, chunk)] = jnp.dot(
                order_ref[...], gated_ref[...], preferred_element_type=f32).astype(bf16)
            if ready:
                send(place).start()
            return 0

        lax.fori_loop(0, part // chunk, body, 0)

    base = 0
    for index, part in enumerate(parts):
        gate_part(base, part, *tables[3 * index : 3 * index + 3])
        base += part
    if ready:
        for i in range(half // chunk):
            send(i).wait()
        finished.wait()


def kernel_call(body, name, outs, scratch, operands, in_hbm, out_hbm=(), **options):
    def spec(far):
        return pl.BlockSpec(memory_space=pltpu.HBM if far else pltpu.VMEM)

    def bound(*refs):
        return body(*refs, **options)

    return pl.pallas_call(
        bound,
        in_specs=[spec(i in in_hbm) for i in range(len(operands))],
        out_specs=[spec(i in out_hbm) for i in range(len(outs))],
        out_shape=[jax.ShapeDtypeStruct(shape, dtype) for shape, dtype in outs],
        scratch_shapes=scratch,
        compiler_params=pltpu.CompilerParams(vmem_limit_bytes=32 << 20),
        name=name,
    )(*operands)


def on_device(projected, short_taps, skip_gain, residues, pole_angles, decay_rates):
    _, rows, channels = projected.shape
    chunk = min(CHUNK, channels)
    devices = lax.axis_size("seq")
    levels = devices.bit_length() - 1
    arguments = [pole_angles, decay_rates, short_taps, residues, skip_gain[None], projected]
    arguments = [pltpu.with_memory_space_constraint(argument, pltpu.HBM) for argument in arguments]
    half = channels // 2
    local_chunk = min(LOCAL_CHUNK, channels)
    wide_chunk = min(STATES_CHUNK, channels)
    square = pltpu.VMEM((rows, rows), bf16)
    dma = pltpu.SemaphoreType.DMA

    def pairs(count, dtype=f32, extent=half):
        return (count, POLES, extent), dtype

    state = pairs(2)
    side_outs = [((rows, half), bf16), ((4, SEGMENTS, half), f32), pairs(7)]
    working = [pltpu.VMEM((rows, wide_chunk), f32)] * 2
    *theirs, give, powers, taps, gains, skip, kv_rows, query_rows = kernel_call(
        first_kernel, "first",
        [*side_outs, pairs(2 * (SPAN + levels), f32, channels), (short_taps.shape, f32), (residues.shape, f32),
         ((1, channels), f32), ((2, rows, channels), bf16), ((rows, channels), bf16)],
        [square] + [pltpu.VMEM(pole_angles.shape, f32)] * 2 + working + [dma((6,)), dma((half // wide_chunk + 1,))],
        arguments, range(6), levels=levels)

    def exchange(array, mask):
        return lax.ppermute(array, "seq", [(i, i ^ mask) for i in range(devices)])

    def message(level):
        return pairs(5 if level == levels - 1 else 7, bf16)

    got = exchange(give, 1)
    *ours, keep = kernel_call(
        second_kernel, "second", side_outs, [square] + working, [powers, taps, kv_rows, query_rows], ())
    ending, sent, lead, enter, base, fix, first = kernel_call(
        merge_kernel, "merge", [state, pairs(7, bf16), state, state, state, state, pairs(2, bf16)], [],
        [keep, got, powers, taps, gains, skip], (), channels=channels)
    head = first
    before = jnp.zeros(*pairs(3, bf16))

    tables = []

    def run_local(until):
        while len(tables) < min(until, len(PARTS)):
            later, offset, size = PARTS[len(tables)]
            base, part = half * offset // 2, half * size // 2
            plane = ((rows, part), f32)
            prod, scan = theirs if later else ours
            tables.append(kernel_call(
                local_kernel, "local", [plane, plane, ((4, SEGMENTS, part), f32)],
                [square, pltpu.VMEM((rows, local_chunk), f32)],
                [taps, gains, skip, powers, scan, prod, query_rows, ending, tables[-1][2] if tables else ending],
                (7, 8), theirs=later, base=base))
        return tables[-1][2]

    level = 1
    if levels > 3:
        near, far, both = (exchange(sent, mask << level) for mask in (1, 2, 3))
        after = run_local(2)
        level = 3
        ending, sent, head, lead, enter, before = kernel_call(
            quad_kernel, "quad", [state, message(level), pairs(2, bf16), state, state, pairs(3, bf16)], [],
            [ending, sent, near, far, both, powers, taps, lead, enter, before, after], (10,),
            level=1, channels=channels)
    while level < levels:
        got = exchange(sent, 1 << level)
        after = run_local(len(PARTS) if level == levels - 1 else level)
        level += 1
        if level < levels:
            ending, sent, head, lead, enter, before = kernel_call(
                join_kernel, "join", [state, message(level), pairs(2, bf16), state, state, pairs(3, bf16)], [],
                [ending, sent, got, head, powers, taps, lead, enter, before, after], (9,), level=level - 1,
                channels=channels)

    keep, give = kernel_call(
        last_kernel, "last", [pairs(4)] * 2, [],
        [sent, got, head, powers, taps, gains, skip, lead, enter, before, base, fix, first, after], (13,),
        level=levels - 1, channels=channels)
    got = exchange(give, 1)
    half_plane = ((rows, half), bf16)
    scratch = [square, pltpu.VMEM(*half_plane), pltpu.VMEM((rows, chunk), bf16), dma((half // chunk + 1,))]

    def side(later):
        chosen = [(table, half * size // 2) for table, (which, _, size) in zip(tables, PARTS) if which == later]
        return [array for table, _ in chosen for array in table], [size for _, size in chosen]

    arrays, parts = side(False)
    (ready,) = kernel_call(
        gate_kernel, "gate", [half_plane], [square, scratch[2]], [powers, keep, *arrays], (), parts=parts, ready=False)
    arrays, parts = side(True)
    (out,) = kernel_call(
        gate_kernel, "finish", [((rows, channels), bf16)], scratch, [powers, got, *arrays, ready], (), (0,),
        parts=parts, ready=True)
    return out


def solution(mesh):
    return jax.shard_map(
        on_device,
        mesh=mesh,
        in_specs=(P(None, ("grp", "seq"), None), P(), P(), P(), P(), P()),
        out_specs=P(("grp", "seq"), None),
        check_vma=False,
    )
```

```python
import functools
import itertools

import jax
import jax.numpy as jnp
from jax import lax
from jax.experimental import pallas as pl
from jax.experimental.pallas import tpu as pltpu
from jax.sharding import PartitionSpec as P

SEGMENTS = 8
WIDTH = 256
CHUNK = 1024
POLES = 2
SUBROWS = 16
LOCAL_CHUNK = 512
STATES_CHUNK = 1024
PARTS = ((False, 0, 2), (True, 0, 1), (True, 1, 1))
f32 = jnp.float32
bf16 = jnp.bfloat16

LAM, BACK, SEGMENT, SPAN = 0, 1, 2, 5


def order_matrix(row_count, inverse):
    length = row_count // SEGMENTS
    ordered = lax.broadcasted_iota(jnp.int32, (row_count, row_count), 1 if inverse else 0)
    natural = lax.broadcasted_iota(jnp.int32, (row_count, row_count), 0 if inverse else 1)
    wanted = length * (ordered % SEGMENTS) + ordered // SEGMENTS
    return (wanted == natural).astype(f32).astype(bf16)


def wide(value):
    return jnp.broadcast_to(value, (SEGMENTS, value.shape[1]))


def times(a, b):
    return (a[0] * b[0] - a[1] * b[1], a[0] * b[1] + a[1] * b[0])


def plus(a, b):
    return (a[0] + b[0], a[1] + b[1])


def pair_at(ref, index, cols):
    return (ref[2 * index, :, cols], ref[2 * index + 1, :, cols])


def put_pair(ref, index, cols, value):
    ref[2 * index, :, cols] = value[0]
    ref[2 * index + 1, :, cols] = value[1]


def pole_at(ref, index, pole, cols):
    return (wide(ref[2 * index, pole : pole + 1, cols]), wide(ref[2 * index + 1, pole : pole + 1, cols]))


def half_angle(angle):
    x = 0.5 * angle
    u = x * x
    sine = 1.0 / 6227020800.0
    for term in (-1.0 / 39916800.0, 1.0 / 362880.0, -1.0 / 5040.0, 1.0 / 120.0, -1.0 / 6.0, 1.0):
        sine = sine * u + term
    cosine = -1.0 / 87178291200.0
    for term in (1.0 / 479001600.0, -1.0 / 3628800.0, 1.0 / 40320.0, -1.0 / 720.0, 1.0 / 24.0, -0.5, 1.0):
        cosine = cosine * u + term
    return cosine, sine * x


def fill_powers(power_ref, angle_ref, decay_ref, length, levels):
    cols = slice(None)
    cosine, sine = half_angle(angle_ref[...])
    turn = (1.0 - 2.0 * sine * sine, 2.0 * sine * cosine)
    decay = decay_ref[...]
    damping = jnp.exp(-decay)
    growth = jnp.exp(decay)
    value = (damping * turn[0], damping * turn[1])
    put_pair(power_ref, LAM, cols, value)
    put_pair(power_ref, BACK, cols, (growth * turn[0], -growth * turn[1]))
    for _ in range(length.bit_length() - 1):
        value = times(value, value)
    for level in range(3 + levels):
        put_pair(power_ref, SEGMENT + level, cols, value)
        value = times(value, value)


def steps_of(ref, cols):
    return [ref[SEGMENTS * j : SEGMENTS * (j + 1), cols] for j in range(ref.shape[0] // SEGMENTS)]


def first_mask():
    return lax.broadcasted_iota(jnp.int32, (SEGMENTS, WIDTH), 0) == 0


def delayed(value):
    return jnp.where(first_mask(), 0.0, pltpu.roll(value, 1, 0))


def short_filter(steps, taps_ref, which, cols):
    taps = [wide(taps_ref[tap, which : which + 1, cols]) for tap in range(3)]
    padded = [delayed(steps[-2]), delayed(steps[-1])] + steps
    return [
        taps[0] * padded[j] + taps[1] * padded[j + 1] + taps[2] * padded[j + 2]
        for j in range(len(steps))
    ]


def feedback(lam):
    return 2.0 * lam[0], lam[0] * lam[0] + lam[1] * lam[1]


def span(start, size):
    if isinstance(start, int):
        return slice(start, start + size)
    return pl.ds(pl.multiple_of(start, 128), size)


def loop_columns(chunk_index, chunk, body):
    for part in range(chunk // WIDTH):
        body(part * WIDTH, chunk_index * chunk + part * WIDTH)


def side_start(theirs, half):
    odd = lax.axis_index("seq") % 2
    return (1 - odd if theirs else odd) * half


def half_states(ready, begin, order_ref, power_ref, taps_ref, kv_ref, q_ref, prod_ref, scan_ref, block_ref, ks_ref, vs_ref):
    _, rows, _ = kv_ref.shape
    half = prod_ref.shape[1]
    chunk = min(STATES_CHUNK, half)

    def body(i, _):
        ready(i)
        at = span(begin + i * chunk, chunk)
        scratch = slice(i * chunk, (i + 1) * chunk)
        ks_ref[:, scratch] = jnp.dot(order_ref[...], kv_ref[0, :, at], preferred_element_type=f32)
        vs_ref[:, scratch] = jnp.dot(order_ref[...], kv_ref[1, :, at], preferred_element_type=f32)

        def column(inner, outer):
            cols = put = slice(outer, outer + WIDTH)
            here = span(begin + outer, WIDTH)
            keys = short_filter(steps_of(ks_ref, cols), taps_ref, 1, here)
            values = short_filter(steps_of(vs_ref, cols), taps_ref, 2, here)
            products = [a * b for a, b in zip(keys, values)]
            for j in range(2):
                products[j] = jnp.where(first_mask(), 0.0, products[j])
            for j in range(0, len(products), 2):
                both = jnp.concatenate(products[j : j + 2], axis=0)
                prod_ref[SEGMENTS * j : SEGMENTS * (j + 2), put] = both.astype(bf16)
            sublane = lax.broadcasted_iota(jnp.int32, (SEGMENTS, WIDTH), 0)
            for pole in range(POLES):
                lam = pole_at(power_ref, LAM, pole, here)
                a1, a2 = feedback(lam)
                late = products[0]
                now = a1 * late + products[1]
                for value in products[2:]:
                    late, now = now, a1 * now - a2 * late + value
                state = (now - lam[0] * late, lam[1] * late)
                for level in range(3):
                    by = 1 << level
                    factor = pole_at(power_ref, SEGMENT + level, pole, here)
                    moved = tuple(jnp.where(sublane >= by, pltpu.roll(part, by, 0), 0.0) for part in state)
                    state = plus(state, times(factor, moved))
                for part in range(2):
                    scan_ref[2 * part + pole, :, put] = state[part]
                    block_ref[part, pole : pole + 1, put] = state[part][SEGMENTS - 1 :]

        loop_columns(i, chunk, column)
        return 0

    for i in range(half // chunk):
        body(i, 0)


def put_edges(begin, kv_ref, q_ref, block_ref):
    _, rows, _ = kv_ref.shape
    here = span(begin, block_ref.shape[2])
    last = slice(rows - SUBROWS, rows)
    for which, tail in enumerate((q_ref[last, here], kv_ref[0, last, here], kv_ref[1, last, here])):
        block_ref[2 + which] = tail[SUBROWS - 2 :].astype(f32)
    for which in range(2):
        block_ref[5 + which] = kv_ref[which, 0:SUBROWS, here][0:2].astype(f32)


def first_kernel(angle_hbm, decay_hbm, taps_hbm, gain_hbm, skip_hbm, proj_ref,
                 prod_ref, scan_ref, give_ref, power_ref, taps_ref, gain_ref, skip_ref, kv_ref, q_ref,
                 order_ref, angle_ref, decay_ref, ks_ref, vs_ref, small_sem, in_sem, *, levels):
    _, rows, channels = kv_ref.shape
    half = channels // 2
    chunk = min(STATES_CHUNK, half)
    count = half // chunk
    begin, rest = side_start(True, half), side_start(False, half)
    smalls = [
        pltpu.make_async_copy(source, target, small_sem.at[i])
        for i, (source, target) in enumerate([
            (angle_hbm, angle_ref), (decay_hbm, decay_ref), (taps_hbm, taps_ref), (proj_ref.at[0], q_ref),
            (gain_hbm, gain_ref), (skip_hbm, skip_ref)])
    ]

    def fetch(start, size, which):
        cols = span(start, size)
        return pltpu.make_async_copy(proj_ref.at[pl.ds(1, 2), :, cols], kv_ref.at[:, :, cols], in_sem.at[which])

    for copy in smalls[:3]:
        copy.start()
    for i in range(count):
        fetch(begin + i * chunk, chunk, i).start()
    order_ref[...] = order_matrix(rows, False)
    for copy in smalls[:3]:
        copy.wait()
    fill_powers(power_ref, angle_ref, decay_ref, rows // SEGMENTS, levels)

    def ready(i):
        fetch(begin + i * chunk, chunk, i).wait()
        if i == 0:
            for copy in smalls[3:]:
                copy.start()
            fetch(rest, half, count).start()

    half_states(ready, begin, order_ref, power_ref, taps_ref,
                kv_ref, q_ref, prod_ref, scan_ref, give_ref, ks_ref, vs_ref)
    for copy in smalls[3:]:
        copy.wait()
    fetch(rest, half, count).wait()
    put_edges(begin, kv_ref, q_ref, give_ref)


def second_kernel(power_ref, taps_ref, kv_ref, q_ref, prod_ref, scan_ref, keep_ref, order_ref, ks_ref, vs_ref):
    _, rows, channels = kv_ref.shape
    begin = side_start(False, channels // 2)
    order_ref[...] = order_matrix(rows, False)
    half_states(lambda i: None, begin, order_ref, power_ref, taps_ref, kv_ref, q_ref, prod_ref, scan_ref, keep_ref,
                ks_ref, vs_ref)
    put_edges(begin, kv_ref, q_ref, keep_ref)


def halves(channels):
    half = channels // 2
    odd = lax.axis_index("seq") % 2
    return span(odd * half, half), span((1 - odd) * half, half)


def first_products(tail, heads, taps):
    def filtered(which):
        before, after = tail[which], heads[which - 1]
        middle = jnp.concatenate([before[1:2], after[0:1]], axis=0)
        planes = (before, middle, after)
        return sum(taps[tap, which : which + 1] * planes[tap] for tap in range(3))

    return filtered(1) * filtered(2)


def extra_state(products, back):
    first, second = products[0:1], products[1:2]
    return times(back, (second * back[0] + first, second * back[1]))


def fixed_rows(products, tail, taps, skip, gain, back):
    jump = sum(gain[0, pole : pole + 1] * back[0][pole : pole + 1] - gain[1, pole : pole + 1] * back[1][pole : pole + 1]
               for pole in range(POLES))
    none = jnp.zeros_like(jump)
    local = skip * products - jnp.concatenate([jump * products[1:2], none], axis=0)
    query = taps[0, 0:1] * tail[0] + jnp.concatenate([taps[1, 0:1] * tail[0][1:2], none], axis=0)
    return local, query


def planes_of(ref, start, stop):
    return [ref[i].astype(f32) for i in range(start, stop)]


def by_cases(conditions, body):
    for values in itertools.product((False, True), repeat=len(conditions)):
        hits = [c if value else jnp.logical_not(c) for c, value in zip(conditions, values)]
        pl.when(functools.reduce(jnp.logical_and, hits))(functools.partial(body, *values))


def pick(condition, a, b):
    if isinstance(condition, bool):
        return tuple(a) if condition else tuple(b)
    return tuple(jnp.where(condition, x, y) for x, y in zip(a, b))


def mixed(value):
    return jnp.concatenate([value[0:1] + value[1:2], value[0:1] - value[1:2]], axis=0)


def put_wire(wire_ref, value):
    for part in range(2):
        wire_ref[part] = mixed(value[part]).astype(bf16)


def from_wire(wire_ref):
    return tuple(0.5 * mixed(wire_ref[part].astype(f32)) for part in range(2))


ALL = slice(None)


def merge_kernel(own_ref, mate_ref, power_ref, taps_ref, gain_ref, skip_ref,
                 joined_ref, wire_ref, lead_ref, enter_ref, base_ref, fix_ref, head_ref, *, channels):
    device = lax.axis_index("seq")

    def body(odd):
        half = halves(channels)[0]
        taps, gain, skip = taps_ref[:, :, half], gain_ref[:, :, half], skip_ref[:, half]
        power, back = pair_at(power_ref, SPAN, half), pair_at(power_ref, BACK, half)
        mine, mates = planes_of(own_ref, 2, 7), planes_of(mate_ref, 2, 7)
        even_edge, odd_edge = pick(odd, mates, mine), pick(odd, mine, mates)
        own, mate = pair_at(own_ref, 0, ALL), pair_at(mate_ref, 0, ALL)
        even_total, odd_total = pick(odd, mate, own), pick(odd, own, mate)
        products = first_products(even_edge[0:3], odd_edge[3:5], taps)
        base = plus(even_total, extra_state(products, back))
        put_pair(base_ref, 0, ALL, base)
        fix_ref[0], fix_ref[1] = fixed_rows(products, even_edge[0:3], taps, skip, gain, back)
        start = extra_state(first_products([jnp.zeros_like(power[0])] * 3, even_edge[3:5], taps), back)
        enter = tuple(jnp.where(device < 2, part, 0.0) for part in start)
        put_pair(enter_ref, 0, ALL, enter)
        joined = plus(odd_total, times(power, plus(base, times(power, enter))))
        put_pair(joined_ref, 0, ALL, joined)
        put_pair(lead_ref, 0, ALL, (jnp.ones_like(power[0]), jnp.zeros_like(power[0])))
        put_wire(wire_ref, joined)
        for i in range(3):
            wire_ref[2 + i] = odd_edge[i].astype(bf16)
        for i in range(2):
            head = even_edge[3 + i].astype(bf16)
            head_ref[i] = head
            wire_ref[5 + i] = head

    by_cases([device % 2 == 1], body)


def step_of(level, upper, sent_ref, got_ref, own_head, power_ref, taps_ref, lead_ref, enter_ref, tail_before, half):
    leads = jnp.logical_and(upper, (lax.axis_index("seq") % (1 << level)) < 2)
    back = pair_at(power_ref, BACK, half)
    early_tail = pick(upper, planes_of(got_ref, 2, 5), planes_of(sent_ref, 2, 5))
    late_head = own_head
    if got_ref.shape[0] > 5:
        late_head = pick(upper, own_head, planes_of(got_ref, 5, 7))
    extra = extra_state(first_products(early_tail, late_head, taps_ref[:, :, half]), back)
    other = from_wire(got_ref)
    lead, enter = pair_at(lead_ref, 0, ALL), pair_at(enter_ref, 0, ALL)
    enter = pick(upper, plus(enter, times(lead, plus(other, extra))), enter)
    return other, extra, lead, enter, pick(leads, early_tail, tail_before)


def join_kernel(ending_ref, sent_ref, got_ref, head_ref, power_ref, taps_ref, lead_ref, enter_ref, before_ref, after_ref,
                joined_ref, wire_ref, next_head_ref, next_lead_ref, next_enter_ref, next_before_ref, *, level, channels):
    half = halves(channels)[0]
    own_head = planes_of(head_ref, 0, 2)
    upper = (lax.axis_index("seq") >> level) % 2 == 1
    other, extra, lead, enter, before = step_of(
        level, upper, sent_ref, got_ref, own_head, power_ref, taps_ref, lead_ref, enter_ref, planes_of(before_ref, 0, 3), half)
    factor = pair_at(power_ref, SPAN + level, half)
    mine = pair_at(ending_ref, 0, ALL)
    early, late = pick(upper, other, mine), pick(upper, mine, other)
    joined = plus(times(factor, plus(early, extra)), late)
    put_pair(joined_ref, 0, ALL, joined)
    put_wire(wire_ref, joined)
    for i, plane in enumerate(pick(upper, planes_of(sent_ref, 2, 5), planes_of(got_ref, 2, 5))):
        wire_ref[2 + i] = plane.astype(bf16)
    for i, plane in enumerate(pick(upper, planes_of(got_ref, 5, 7), own_head)):
        head = plane.astype(bf16)
        next_head_ref[i] = head
        if wire_ref.shape[0] > 5:
            wire_ref[5 + i] = head
    put_pair(next_lead_ref, 0, ALL, pick(upper, times(lead, factor), lead))
    put_pair(next_enter_ref, 0, ALL, enter)
    for i in range(3):
        next_before_ref[i] = before[i].astype(bf16)


def join_blocks(early, late, factor, back, taps):
    extra = extra_state(first_products(early[2:5], late[5:7], taps), back)
    begin = plus(early[0:2], extra)
    return [*plus(times(factor, begin), late[0:2]), *late[2:5], *early[5:7]], begin


def quad_kernel(ending_ref, sent_ref, near_ref, far_ref, both_ref, power_ref, taps_ref, lead_ref, enter_ref,
                before_ref, after_ref, joined_ref, wire_ref, next_head_ref, next_lead_ref, next_enter_ref,
                next_before_ref, *, level, channels):
    device = lax.axis_index("seq")

    def body(*uppers):
        half = halves(channels)[0]
        back, taps = pair_at(power_ref, BACK, half), taps_ref[:, :, half]
        near, far, both = ([*from_wire(ref), *planes_of(ref, 2, 7)] for ref in (near_ref, far_ref, both_ref))
        mine = [*pair_at(ending_ref, 0, ALL), *planes_of(sent_ref, 2, 7)]
        lead, enter, before = pair_at(lead_ref, 0, ALL), pair_at(enter_ref, 0, ALL), planes_of(before_ref, 0, 3)
        upper = uppers[0]
        factor = pair_at(power_ref, SPAN + level, half)
        other, _ = join_blocks(pick(upper, both, far), pick(upper, far, both), factor, back, taps)
        for step in range(2):
            upper = uppers[step]
            leads = jnp.logical_and(upper, (device % (1 << (level + step))) < 2)
            factor = pair_at(power_ref, SPAN + level + step, half)
            across = other if step else near
            early = pick(upper, across, mine)
            mine, begin = join_blocks(early, pick(upper, mine, across), factor, back, taps)
            enter = pick(upper, plus(enter, times(lead, begin)), enter)
            lead = pick(upper, times(lead, factor), lead)
            before = pick(leads, early[2:5], before)
        put_pair(joined_ref, 0, ALL, mine[0:2])
        put_wire(wire_ref, mine[0:2])
        for i in range(3):
            wire_ref[2 + i] = mine[2 + i].astype(bf16)
            next_before_ref[i] = before[i].astype(bf16)
        for i in range(2):
            head = mine[5 + i].astype(bf16)
            next_head_ref[i] = head
            if wire_ref.shape[0] > 5:
                wire_ref[5 + i] = head
        put_pair(next_lead_ref, 0, ALL, lead)
        put_pair(next_enter_ref, 0, ALL, enter)

    by_cases([(device >> (level + step)) % 2 == 1 for step in range(2)], body)


def last_kernel(sent_ref, got_ref, head_ref, power_ref, taps_ref, gain_ref, skip_ref, lead_ref, enter_ref, before_ref,
                base_ref, fix_ref, first_ref, after_ref, keep_ref, give_ref, *, level, channels):
    device = lax.axis_index("seq")

    def body(odd, upper):
        half = halves(channels)[0]
        _, _, _, enter, before = step_of(
            level, upper, sent_ref, got_ref, planes_of(head_ref, 0, 2), power_ref, taps_ref, lead_ref, enter_ref,
            planes_of(before_ref, 0, 3), half)
        taps, gain, skip = taps_ref[:, :, half], gain_ref[:, :, half], skip_ref[:, half]
        power, back = pair_at(power_ref, SPAN, half), pair_at(power_ref, BACK, half)
        products = first_products(before, planes_of(first_ref, 0, 2), taps)
        even = [*enter, *fixed_rows(products, before, taps, skip, gain, back)]
        odds = [*plus(times(power, enter), pair_at(base_ref, 0, ALL)), fix_ref[0], fix_ref[1]]
        for i, (a, b) in enumerate(zip(even, odds)):
            keep_ref[i], give_ref[i] = (b, a) if odd else (a, b)

    by_cases([device % 2 == 1, (device >> level) % 2 == 1], body)


def local_kernel(taps_ref, gain_ref, skip_ref, power_ref, scan_ref, prod_ref, q_ref, after_ref, part_ref,
                 query_ref, local_ref, enter_ref, order_ref, qs_ref, *, theirs, base):
    rows, channels = query_ref.shape
    begin = side_start(theirs, prod_ref.shape[1]) + base
    chunk = qs_ref.shape[1]
    order_ref[...] = order_matrix(rows, False)

    def body(i, _):
        qs_ref[...] = jnp.dot(order_ref[...], q_ref[:, span(begin + i * chunk, chunk)], preferred_element_type=f32)

        def column(inner, outer):
            cols = slice(inner, inner + WIDTH)
            put = span(outer, WIDTH)
            here = span(begin + outer, WIDTH)
            take = span(base + outer, WIDTH)
            queries = short_filter(steps_of(qs_ref, cols), taps_ref, 0, here)
            for j, value in enumerate(queries):
                query_ref[SEGMENTS * j : SEGMENTS * (j + 1), put] = value
            products = []
            for j in range(0, len(queries), 2):
                both = prod_ref[SEGMENTS * j : SEGMENTS * (j + 2), take].astype(f32)
                products += [both[:SEGMENTS], both[SEGMENTS:]]
            before = delayed(products[-1])
            skip = wide(skip_ref[0:1, here])
            sublane = lax.broadcasted_iota(jnp.int32, (SEGMENTS, WIDTH), 0)
            coefs = []
            for pole in range(POLES):
                lam = pole_at(power_ref, LAM, pole, here)
                back = pole_at(power_ref, BACK, pole, here)
                gain = tuple(wide(gain_ref[part, pole : pole + 1, here]) for part in range(2))
                a1, a2 = feedback(lam)
                b1 = gain[0] * lam[0] + gain[1] * lam[1]
                carry = tuple(delayed(scan_ref[2 * part + pole, :, take]) for part in range(2))
                gain_back = times(gain, back)
                y1 = gain[0] * carry[0] - gain[1] * carry[1]
                y2 = gain_back[0] * (carry[0] - before) - gain_back[1] * carry[1]
                coefs.append([a1, a2, gain[0], b1, y1, y2])
                reach = gain
                for level in range(3):
                    factor = pole_at(power_ref, SEGMENT + level, pole, here)
                    bit = (sublane // (1 << level)) % 2 == 1
                    reach = times(reach, (jnp.where(bit, factor[0], 1.0), jnp.where(bit, factor[1], 0.0)))
                for part in range(2):
                    enter_ref[2 * part + pole, :, put] = reach[part]
            previous = before
            for j, value in enumerate(products):
                total = skip * value
                for pole in range(POLES):
                    a1, a2, b0, b1, y1, y2 = coefs[pole]
                    y = a1 * y1 - a2 * y2 + (b0 * value - b1 * previous)
                    coefs[pole][4:] = [y, y1]
                    total = total + y
                previous = value
                local_ref[SEGMENTS * j : SEGMENTS * (j + 1), put] = total

        loop_columns(i, chunk, column)
        return 0

    lax.fori_loop(0, channels // chunk, body, 0)


def gate_kernel(power_ref, state_ref, *rest, parts, ready):
    count = 3 * len(parts)
    tables, rest = rest[:count], rest[count:]
    if ready:
        ready_ref, out_hbm, order_ref, out_ref, gated_ref, out_sem = rest
    else:
        out_ref, order_ref, gated_ref = rest
    half = out_ref.shape[1]
    chunk = min(CHUNK, half)
    own = halves(2 * half)[0]
    begin = side_start(ready, half)

    def send(i):
        place = span(i * chunk, chunk)
        return pltpu.make_async_copy(
            out_ref.at[:, place], out_hbm.at[:, span(begin + i * chunk, chunk)], out_sem.at[i])

    if ready:
        finished = pltpu.make_async_copy(ready_ref, out_hbm.at[:, own], out_sem.at[half // chunk])
        finished.start()
    order_ref[...] = order_matrix(gated_ref.shape[0], True)

    def gate_part(base, part, query_ref, local_ref, reach_ref):
        def body(i, _):
            def column(inner, outer):
                take = span(outer, WIDTH)
                there = span(base + outer, WIDTH)
                here = span(begin + base + outer, WIDTH)
                queries = steps_of(query_ref, take)
                local = steps_of(local_ref, take)
                for j in range(2):
                    local[j] = local[j] + jnp.where(first_mask(), wide(state_ref[2, j : j + 1, there]), 0.0)
                    queries[j] = queries[j] + jnp.where(first_mask(), wide(state_ref[3, j : j + 1, there]), 0.0)
                coefs = []
                for pole in range(POLES):
                    lam = pole_at(power_ref, LAM, pole, here)
                    back = pole_at(power_ref, BACK, pole, here)
                    state = times(pole_at(state_ref, 0, pole, there), (reach_ref[pole, :, take], reach_ref[2 + pole, :, take]))
                    y2 = state[0] * back[0] - state[1] * back[1]
                    coefs.append([*feedback(lam), state[0], y2])
                gated = []
                for j in range(len(queries)):
                    total = local[j]
                    for pole in range(POLES):
                        a1, a2, y1, y2 = coefs[pole]
                        y = a1 * y1 - a2 * y2
                        coefs[pole][2:] = [y, y1]
                        total = total + y
                    gated.append(queries[j] * total)
                    if j % 2:
                        both = jnp.concatenate(gated[-2:], axis=0)
                        gated_ref[SEGMENTS * (j - 1) : SEGMENTS * (j + 1), base + outer : base + outer + WIDTH] = both.astype(bf16)

            loop_columns(i, chunk, column)
            place = base // chunk + i
            out_ref[:, span(place * chunk, chunk)] = jnp.dot(
                order_ref[...], gated_ref[:, span(place * chunk, chunk)], preferred_element_type=f32).astype(bf16)
            if ready:
                send(place).start()
            return 0

        for i in range(part // chunk):
            body(i, 0)

    base = 0
    for index, part in enumerate(parts):
        gate_part(base, part, *tables[3 * index : 3 * index + 3])
        base += part
    if ready:
        for i in range(half // chunk):
            send(i).wait()
        finished.wait()


def kernel_call(body, name, outs, scratch, operands, in_hbm, out_hbm=(), **options):
    def spec(far):
        return pl.BlockSpec(memory_space=pltpu.HBM if far else pltpu.VMEM)

    def bound(*refs):
        return body(*refs, **options)

    return pl.pallas_call(
        bound,
        in_specs=[spec(i in in_hbm) for i in range(len(operands))],
        out_specs=[spec(i in out_hbm) for i in range(len(outs))],
        out_shape=[jax.ShapeDtypeStruct(shape, dtype) for shape, dtype in outs],
        scratch_shapes=scratch,
        compiler_params=pltpu.CompilerParams(vmem_limit_bytes=32 << 20),
        name=name,
    )(*operands)


def on_device(projected, short_taps, skip_gain, residues, pole_angles, decay_rates):
    _, rows, channels = projected.shape
    chunk = min(CHUNK, channels)
    devices = lax.axis_size("seq")
    levels = devices.bit_length() - 1
    arguments = [pole_angles, decay_rates, short_taps, residues, skip_gain[None], projected]
    arguments = [pltpu.with_memory_space_constraint(argument, pltpu.HBM) for argument in arguments]
    half = channels // 2
    local_chunk = min(LOCAL_CHUNK, channels)
    wide_chunk = min(STATES_CHUNK, channels)
    square = pltpu.VMEM((rows, rows), bf16)
    dma = pltpu.SemaphoreType.DMA

    def pairs(count, dtype=f32, extent=half):
        return (count, POLES, extent), dtype

    state = pairs(2)
    side_outs = [((rows, half), bf16), ((4, SEGMENTS, half), f32), pairs(7)]
    working = [pltpu.VMEM((rows, half), f32)] * 2
    *theirs, give, powers, taps, gains, skip, kv_rows, query_rows = kernel_call(
        first_kernel, "first",
        [*side_outs, pairs(2 * (SPAN + levels), f32, channels), (short_taps.shape, f32), (residues.shape, f32),
         ((1, channels), f32), ((2, rows, channels), bf16), ((rows, channels), bf16)],
        [square] + [pltpu.VMEM(pole_angles.shape, f32)] * 2 + working + [dma((6,)), dma((half // wide_chunk + 1,))],
        arguments, range(6), levels=levels)

    def exchange(array, mask):
        return lax.ppermute(array, "seq", [(i, i ^ mask) for i in range(devices)])

    def message(level):
        return pairs(5 if level == levels - 1 else 7, bf16)

    got = exchange(give, 1)
    *ours, keep = kernel_call(
        second_kernel, "second", side_outs, [square] + working, [powers, taps, kv_rows, query_rows], ())
    ending, sent, lead, enter, base, fix, first = kernel_call(
        merge_kernel, "merge", [state, pairs(7, bf16), state, state, state, state, pairs(2, bf16)], [],
        [keep, got, powers, taps, gains, skip], (), channels=channels)
    head = first
    before = jnp.zeros(*pairs(3, bf16))

    tables = []

    def run_local(until):
        while len(tables) < min(until, len(PARTS)):
            later, offset, size = PARTS[len(tables)]
            base, part = half * offset // 2, half * size // 2
            plane = ((rows, part), f32)
            prod, scan = theirs if later else ours
            tables.append(kernel_call(
                local_kernel, "local", [plane, plane, ((4, SEGMENTS, part), f32)],
                [square, pltpu.VMEM((rows, local_chunk), f32)],
                [taps, gains, skip, powers, scan, prod, query_rows, ending, tables[-1][2] if tables else ending],
                (7, 8), theirs=later, base=base))
        return tables[-1][2]

    level = 1
    if levels > 3:
        near, far, both = (exchange(sent, mask << level) for mask in (1, 2, 3))
        after = run_local(2)
        level = 3
        ending, sent, head, lead, enter, before = kernel_call(
            quad_kernel, "quad", [state, message(level), pairs(2, bf16), state, state, pairs(3, bf16)], [],
            [ending, sent, near, far, both, powers, taps, lead, enter, before, after], (10,),
            level=1, channels=channels)
    while level < levels:
        got = exchange(sent, 1 << level)
        after = run_local(len(PARTS) if level == levels - 1 else level)
        level += 1
        if level < levels:
            ending, sent, head, lead, enter, before = kernel_call(
                join_kernel, "join", [state, message(level), pairs(2, bf16), state, state, pairs(3, bf16)], [],
                [ending, sent, got, head, powers, taps, lead, enter, before, after], (9,), level=level - 1,
                channels=channels)

    keep, give = kernel_call(
        last_kernel, "last", [pairs(4)] * 2, [],
        [sent, got, head, powers, taps, gains, skip, lead, enter, before, base, fix, first, after], (13,),
        level=levels - 1, channels=channels)
    got = exchange(give, 1)
    half_plane = ((rows, half), bf16)
    scratch = [square, pltpu.VMEM(*half_plane), pltpu.VMEM(*half_plane), dma((half // chunk + 1,))]

    def side(later):
        chosen = [(table, half * size // 2) for table, (which, _, size) in zip(tables, PARTS) if which == later]
        return [array for table, _ in chosen for array in table], [size for _, size in chosen]

    arrays, parts = side(False)
    (ready,) = kernel_call(
        gate_kernel, "gate", [half_plane], [square, scratch[2]], [powers, keep, *arrays], (), parts=parts, ready=False)
    arrays, parts = side(True)
    (out,) = kernel_call(
        gate_kernel, "finish", [((rows, channels), bf16)], scratch, [powers, got, *arrays, ready], (), (0,),
        parts=parts, ready=True)
    return out


def solution(mesh):
    return jax.shard_map(
        on_device,
        mesh=mesh,
        in_specs=(P(None, ("grp", "seq"), None), P(), P(), P(), P(), P()),
        out_specs=P(("grp", "seq"), None),
        check_vma=False,
    )
```
